32 devices in a mesh: tile: 16 (over z, y, x), vec: 2 (over core).
Axes of the slice: x: 2, y: 2, z: 4, core: 2. Of those that a mesh axis runs over, the one named last changes fastest.
Arguments:
- trial: bfloat16 [1, 1024, 1024], P(None, ('tile', 'vec')), may hold values from -0.005859375 to 0.005859375
- psi_v: bfloat16 [1024, 8192], P(None, 'tile'), may hold values from -6 to 6
- psi_c: bfloat16 [1024, 2, 4096], P(None, 'vec', 'tile'), may hold values from -6 to 6
- screened: float32 [8192, 8192], P('tile', 'vec'), may hold values from -0.0007324219 to 0.0007324219
Outputs:
- result: float32 [1, 1024, 1024], P(None, ('tile', 'vec'))
The draws below stay inside these ranges and needn't reach their ends.
All inputs are finite; a program needn't handle non-finite values.
Results may differ from the reference program's by a relative error of at most 0.0041.
Values may be sent and summed in bfloat16 or wider, within the bound.
A program may use at most 64 MiB of HBM per device.

```python
import jax
import jax.numpy as jnp
from jax import lax

NV = 1024
NC = 1024
NP = 8192
NVEC = 1
NPH = 4096
N_VEC = 2


def with_spikes(values, stream_key, source, target, blocks, factor):
    owner, partner = [(jnp.arange(values.shape[axis_at]) // (values.shape[axis_at] // blocks)).reshape([-1 if axis == axis_at else 1 for axis in range(values.ndim)]) for axis_at in (source, target)]
    chosen = jax.random.permutation(stream_key, blocks)[partner]
    strong = (owner == chosen) | (owner == (partner + blocks // 2) % blocks)
    return jnp.where(strong, factor * values, values)


def steps_of(rng, dims, cuts, smallest, largest):
    level, own = 1.0, jax.random.fold_in(rng, 6)
    for axis_at, shards_of in cuts:
        draws = jnp.exp(jax.random.uniform(jax.random.fold_in(own, axis_at), (shards_of,), jnp.float32, smallest / len(cuts), largest / len(cuts)))
        level = level * jnp.repeat(draws, dims[axis_at] // shards_of).reshape([-1 if axis == axis_at else 1 for axis in range(len(dims))])
    return level


def noise(stream_key, shape, spread, bound, cuts=(), held_as=jnp.bfloat16):
    factor_of = steps_of(stream_key, shape, cuts, -0.22, 0.18) if cuts else 1.0
    drawn = jax.random.normal(stream_key, shape, jnp.float32) * spread * factor_of
    return jnp.minimum(jnp.maximum(drawn, -bound), bound).astype(held_as)


def bell_draw_with(own_key, shape, scale, reach, pieces, heavy, kind=jnp.bfloat16):
    result = scale * jax.random.normal(own_key, shape, jnp.float32)
    if pieces:
        result = result * steps_of(own_key, shape, pieces, -0.22, 0.18)
    return jnp.clip(with_spikes(result, jax.random.fold_in(own_key, 3), *heavy), -reach, reach).astype(kind)


def setup_inputs(seed: int = 0) -> dict:
    splits = jax.random.split(jax.random.key(seed), 5)
    trial = noise(splits[0], (NVEC, NV, NC), (NV * NC) ** -0.5, 0.005859375, ((1, 32),))
    psi_v = bell_draw_with(splits[1], (NV, NP), 1.0, 6.0, ((1, 16),), (1, 0, 16, 2.0))
    psi_c = noise(splits[2], (NC, N_VEC, NPH), 1.0, 6.0, ((1, 2), (2, 16)))
    screened = noise(splits[3], (NP, NP), (NP * NP) ** -0.5, 0.0007324219, ((0, 16), (1, 2)), jnp.float32)
    return dict(trial=trial, psi_v=psi_v, psi_c=psi_c, screened=screened)


def reference(trial, psi_v, psi_c, screened):
    conduction = psi_c.reshape(NC, NP)
    left = psi_v.astype(jnp.float32)

    def one_vector(single):
        projected = jnp.dot(psi_v.T, single, preferred_element_type=jnp.float32).astype(jnp.bfloat16)
        pair = jnp.dot(projected, conduction, preferred_element_type=jnp.float32)
        weighted = (screened * pair).astype(jnp.bfloat16)
        back = jnp.dot(weighted, conduction.T, preferred_element_type=jnp.float32)
        return jnp.dot(left, back, precision=lax.Precision.HIGHEST)

    return lax.map(one_vector, trial)
```

```python
import functools

import jax
import jax.numpy as jnp
from jax import lax
from jax.experimental import pallas as pl
from jax.experimental.pallas import tpu as pltpu
from jax.sharding import PartitionSpec as P

CUTS = 4
SUBS = 2


def back_product(weighted_flat, panel):
    return lax.dot_general(
        weighted_flat, panel, (((1,), (1,)), ((), ())), preferred_element_type=jnp.float32
    )


def plain(trial, psi_v, psi_c, screened):
    count = trial.shape[0]
    points = psi_v.shape[1]
    conduct = trial.shape[2]
    whole = lax.all_gather(trial, ("tile", "vec"), axis=1, tiled=True)
    projected = jnp.einsum("vp,kvc->kpc", psi_v, whole, preferred_element_type=jnp.float32).astype(
        jnp.bfloat16
    )
    flat = projected.reshape(count * points, conduct)
    panel_local = psi_c[:, 0, :]
    panel = lax.all_gather(panel_local, "tile", axis=1, tiled=True)
    pair = jnp.dot(flat, panel, preferred_element_type=jnp.float32)
    weighted = (screened[None] * pair.reshape(count, points, -1)).astype(jnp.bfloat16)
    weighted_flat = weighted.reshape(count * points, -1)
    back = back_product(weighted_flat, panel)
    back = back.reshape(count, points, conduct)
    left = psi_v.astype(jnp.float32)
    summed = lax.psum(back, "vec")
    tiles = lax.axis_size("tile")
    halves = lax.axis_size("vec")
    owned = left.shape[0] // (tiles * halves)
    grouped = left.reshape(tiles, halves, owned, points)
    mine = lax.dynamic_index_in_dim(grouped, lax.axis_index("vec"), 1, keepdims=False).reshape(
        tiles * owned, points
    )
    pieces = []
    for one in range(count):
        term = jnp.dot(mine, summed[one], precision=lax.Precision.HIGHEST)
        pieces.append(lax.psum_scatter(term, "tile", scatter_dimension=0, tiled=True))
    return jnp.stack(pieces, axis=0)


def sources_of(layers):
    return [
        sorted((o for o in range(layers) if o != z), key=lambda o: (abs(o - z), o))
        for z in range(layers)
    ]


def pick(values, at):
    chosen = jnp.int32(values[0])
    for k, value in enumerate(values[1:], 1):
        chosen = jnp.where(at == k, jnp.int32(value), chosen)
    return chosen


def body(
    layers,
    trial_hbm,
    psi_v_hbm,
    psi_c_hbm,
    screened_hbm,
    out_ref,
    whole,
    psi,
    psi_t,
    stage,
    screened_own,
    screened_out,
    screened_in,
    panel,
    flat,
    back,
    give,
    take,
    first_send,
    first_got,
    keep,
    second_send,
    second_got,
    third,
    parts,
    local_sem,
    sends,
    trial_recv,
    hand_recv,
    psi_recv,
    screened_recv,
    block_recv,
    take_recv,
    first_recv,
    second_recv,
    parts_recv,
):
    bf16, f32 = jnp.bfloat16, jnp.float32
    me = lax.axis_index("tile")
    half = lax.axis_index("vec")
    other = 1 - half
    z, y, x = me // 4, (me // 2) % 2, me % 2
    across = lax.rem(y + 1, 2)
    aside = lax.rem(x + 1, 2)
    table = sources_of(layers)
    events = layers - 1
    source = [pick([row[e] for row in table], z) for e in range(events)]
    distance = [pick([abs(row[e] - k) for k, row in enumerate(table)], z) for e in range(events)]
    at_distance = [[distance[e] == k for k in range(layers)] for e in range(events)]

    def tile_of(zz, yy, xx):
        return zz * 4 + yy * 2 + xx

    mate_x, mate_y = tile_of(z, y, aside), tile_of(z, across, x)
    up, down = jnp.minimum(z + 1, layers - 1), jnp.maximum(z - 1, 0)
    has_up, has_down = z < layers - 1, z > 0
    on_up = [has_up & (source[e] < z) for e in range(events)]
    on_down = [has_down & (source[e] > z) for e in range(events)]

    def slot_of(zz, yy):
        return zz * 2 + yy

    slots = layers * 2
    order = [("own", 0)]
    for e in range(events):
        order += [("z", e), ("y", e - 1)]
    order += [("y", events - 1)]

    def slot_at(kind, e):
        zz = source[e] if e >= 0 and kind != "own" else z
        return slot_of(zz, across if kind == "y" else y)

    turns = [slot_at(*event) for event in order]

    rows, conduct = trial_hbm.shape
    width = psi_c_hbm.shape[1]
    points = psi_v_hbm.shape[-1]
    middle = conduct // 2
    part = middle // 2
    height = psi_c_hbm.shape[0] // CUTS

    def lines(tile, vec):
        start = pl.multiple_of((tile * 2 + vec) * rows, rows)
        return whole.at[pl.ds(start, rows), :]

    def columns(tile):
        return pl.ds(pl.multiple_of(tile * width, 128), width)

    local = []

    def load(src, dst):
        copy = pltpu.make_async_copy(src, dst, local_sem.at[len(local)])
        copy.start()
        local.append(copy)
        return copy

    load_psi = load(psi_v_hbm, psi.at[0])
    load_rows = load(trial_hbm, lines(me, half))
    load_out = [
        load(screened_hbm.at[:, columns(turn * 2 + aside)], stage.at[i])
        for i, turn in enumerate(turns)
    ]
    load_block = load(psi_c_hbm, panel.at[slot_of(z, y)])
    load_own = [
        load(screened_hbm.at[:, columns(turn * 2 + x)], screened_own.at[i])
        for i, turn in enumerate(turns)
    ]

    def remote(src, dst, send, recv, tile, vec):
        return pltpu.make_async_remote_copy(
            src_ref=src,
            dst_ref=dst,
            send_sem=send,
            recv_sem=recv,
            device_id=(tile, vec),
            device_id_type=pl.DeviceIdType.MESH,
        )

    partners = [(mate_x, half), (mate_y, half), (me, other)]
    for d in range(1, layers):
        for v in range(2):
            partners.append((tile_of(lax.rem(z + d, layers), y, x), v))
    with jax.named_scope("pbar"):
        barrier = pltpu.get_barrier_semaphore()
        for partner in partners:
            pl.semaphore_signal(
                barrier, inc=1, device_id=partner, device_id_type=pl.DeviceIdType.MESH
            )
        pl.semaphore_wait(barrier, len(partners))

    pending = []

    def send(src, dst, recv, tile, vec, like, cond=None):
        i = len(pending)
        copy = remote(src, dst, sends.at[i], recv, tile, vec)
        pending.append((like, cond))
        if cond is None:
            copy.start()
        else:
            pl.when(cond)(copy.start)

    def got(ref, recv):
        remote(ref, ref, sends.at[0], recv, me, other).wait_recv()

    some_rows = whole.at[pl.ds(0, rows), :]

    def piece(ref, s):
        return ref.at[pl.ds(s * height, height), :]

    some_piece = piece(panel.at[0], 0)

    def hand(src, tile):
        send(src, lines(tile, half), hand_recv.at[tile], me, other, some_rows)

    def spread(src, tile, to_up, to_down):
        dst = lines(tile, half)
        recv = trial_recv.at[tile]
        send(src, dst, recv, tile_of(up, y, x), half, some_rows, to_up)
        send(src, dst, recv, tile_of(down, y, x), half, some_rows, to_down)
        send(src, dst, recv, mate_y, half, some_rows)
        hand(src, tile)

    def own_piece(s):
        src = piece(psi_c_hbm, s)
        slot = slot_of(z, y)
        dst = piece(panel.at[slot], s)
        recv = block_recv.at[slot, s]
        send(src, dst, recv, tile_of(up, y, x), half, some_piece, has_up)
        send(src, dst, recv, tile_of(down, y, x), half, some_piece, has_down)
        send(src, dst, recv, mate_y, half, some_piece)

    pair_layers = layers // 2

    def psi_half(ref, which):
        return ref.at[pl.ds(which * pair_layers, pair_layers)]

    with jax.named_scope("ptrial"):
        send(trial_hbm, lines(me, half), trial_recv.at[me], mate_x, half, some_rows)
        spread(trial_hbm, me, has_up, has_down)
        own_piece(0)
        send(
            psi_half(psi_v_hbm, half),
            psi_half(psi.at[1], half),
            psi_recv.at[0],
            mate_x,
            half,
            psi_half(psi.at[1], 0),
        )
        got(lines(mate_x, half), trial_recv.at[mate_x])
        spread(lines(mate_x, half), mate_x, has_up, has_down)

        for i in range(slots):
            load_out[i].wait()
            screened_out[i] = stage[i].astype(bf16)
        for i in range(slots):
            send(
                screened_out.at[i],
                screened_in.at[i],
                screened_recv.at[i],
                mate_x,
                half,
                screened_out.at[0],
            )

        for e in range(events):
            for xx in range(2):
                tile = tile_of(source[e], y, xx)
                ref = lines(tile, half)
                got(ref, trial_recv.at[tile])
                spread(ref, tile, on_up[e], on_down[e])
            if e + 1 < CUTS:
                own_piece(e + 1)
        for s in range(events + 1, CUTS):
            own_piece(s)

        back[...] = jnp.zeros_like(back)
        load_psi.wait()
        valence = layers * 4 * 2 * rows
        psi_t[0] = psi[0].reshape(valence, points).T

        for e in range(-1, events):
            for xx in range(2):
                tile = tile_of(source[e] if e >= 0 else z, across, xx)
                ref = lines(tile, half)
                got(ref, trial_recv.at[tile])
                hand(ref, tile)

        ref = psi_half(psi.at[1], half)
        got(ref, psi_recv.at[0])
        send(ref, ref, psi_recv.at[1], me, other, psi_half(psi.at[1], 0))
        load_rows.wait()
        for tile in range(layers * 4):
            got(lines(tile, other), hand_recv.at[tile])

    wide = 256

    def project(p):
        def chunk(j, carry):
            cols = pl.ds(pl.multiple_of(j * wide, wide), wide)
            flat[p, :, cols] = jnp.dot(
                psi_t[p], whole[:, cols], preferred_element_type=f32
            ).astype(bf16)
            return carry

        lax.fori_loop(0, conduct // wide, chunk, 0)

    with jax.named_scope("pproj"):
        project(0)
        got(psi_half(psi.at[1], other), psi_recv.at[1])
        psi_t[1] = psi[1].reshape(valence, points).T
        project(1)

    def arrive(e):
        slot = slot_of(source[e], y)
        for s in range(CUTS):
            ref = piece(panel.at[slot], s)
            recv = block_recv.at[slot, s]
            got(ref, recv)
            send(ref, ref, recv, mate_y, half, some_piece, None)
            send(ref, ref, recv, tile_of(up, y, x), half, some_piece, on_up[e])
            send(ref, ref, recv, tile_of(down, y, x), half, some_piece, on_down[e])

    def arrive_if(e, k):
        start = len(pending)

        @pl.when(at_distance[e][k])
        def _():
            arrive(e)

        for i in range(start, len(pending)):
            pending[i] += (at_distance[e][k],)

    def receive(i):
        kind, e = order[i]
        if kind == "z":
            for late in range(e, events):
                arrive_if(late, e + 1)
        if kind == "y":
            slot = turns[i]
            for s in range(CUTS):
                got(piece(panel.at[slot], s), block_recv.at[slot, s])
        load_own[i].wait()

    def step(p, share, slot):
        block = panel.at[slot]
        pair = jnp.dot(flat[p], block[...], preferred_element_type=f32)
        weighted = (share.astype(f32) * pair).astype(bf16)
        for h in range(2):
            back[p, h] += back_product(weighted, block[pl.ds(h * middle, middle), :])

    load_block.wait()

    def use(k, carry):
        slot = turns[0]
        for i in range(slots):
            slot = jnp.where(k == i, turns[i], slot)

            @pl.when(k == i)
            def _(i=i):
                receive(i)

        step(0, screened_own[k], slot)
        got(screened_in.at[k], screened_recv.at[k])
        step(1, screened_in[k], slot)
        return carry

    with jax.named_scope("puse"):
        lax.fori_loop(0, slots, use, 0)

    def span(kind):
        return pl.ds(kind * part, part)

    with jax.named_scope("pswap"):
        for kind in range(2):
            for p in range(2):
                give[kind, p] = back[p, other, :, span(kind)].astype(bf16)
                send(
                    give.at[kind, p],
                    take.at[kind, p],
                    take_recv.at[kind, p],
                    me,
                    other,
                    give.at[0, 0],
                )

    share = layers // SUBS
    block_rows = 2 * rows

    def product(kind, at, sub):
        total = None
        for p in range(2):
            if kind == 0:
                left = psi[p, pl.ds(sub * share, share), :, pl.ds(at, 1)]
            else:
                left = psi[p, pl.ds(sub * share, share), pl.ds(at, 1)]
            left = left.reshape(share * 2 * block_rows, points)
            for level in range(2):
                cols = pl.ds(level * middle + kind * part, part)
                value = jnp.dot(left, flat[p, :, cols], preferred_element_type=f32)
                total = value if total is None else total + value
        return total.reshape(share, 2, block_rows, part)

    mates = [mate_x, mate_y]
    with jax.named_scope("pfin"):
        for kind in range(2):
            for p in range(2):
                got(take.at[kind, p], take_recv.at[kind, p])
                total = back[p, half, :, span(kind)] + take[kind, p].astype(f32)
                high = total.astype(bf16)
                flat[p, :, span(kind)] = high
                low = (total - high.astype(f32)).astype(bf16)
                flat[p, :, pl.ds(middle + kind * part, part)] = low
            for sub in range(SUBS):
                away = [aside, across][kind]
                first_send[kind, sub] = product(kind, away, sub).astype(bf16)
                send(
                    first_send.at[kind, sub],
                    first_got.at[kind, sub],
                    first_recv.at[kind, sub],
                    mates[kind],
                    half,
                    first_send.at[0, 0],
                )
        for sub in range(SUBS):
            for kind in range(2):
                keep[kind, sub] = product(kind, [x, y][kind], sub)

    with jax.named_scope("psecond"):
        for sub in range(SUBS):
            for kind in range(2):
                got(first_got.at[kind, sub], first_recv.at[kind, sub])
                away, home = [(across, y), (aside, x)][kind]

                def summed(at, kind=kind, sub=sub):
                    mine = keep[kind, sub, :, pl.ds(at, 1)]
                    theirs = first_got[kind, sub, :, pl.ds(at, 1)].astype(f32)
                    return (mine + theirs).reshape(share, block_rows, part)

                second_send[kind, sub] = summed(away).astype(bf16)
                send(
                    second_send.at[kind, sub],
                    second_got.at[kind, sub],
                    second_recv.at[kind, sub],
                    mates[1 - kind],
                    half,
                    second_send.at[0, 0],
                )
                keep[kind, sub, :, pl.ds(home, 1)] = summed(home).reshape(
                    share, 1, block_rows, part
                )

    with jax.named_scope("pthird"):
        for sub in range(SUBS):
            for kind in range(2):
                got(second_got.at[kind, sub], second_recv.at[kind, sub])
                home = [y, x][kind]
                mine = keep[kind, sub, :, pl.ds(home, 1)].reshape(share, block_rows, part)
                value = mine + second_got[kind, sub].astype(f32)
                keep[kind, sub, :, pl.ds(home, 1)] = value.reshape(share, 1, block_rows, part)
                third[kind, sub] = value.astype(bf16)
                for i in range(share):
                    zz = sub * share + i
                    for v in range(2):
                        send(
                            third.at[kind, sub, i, pl.ds(v * rows, rows)],
                            parts.at[z, half, kind],
                            parts_recv.at[z, half, kind],
                            tile_of(zz, y, x),
                            v,
                            parts.at[0, 0, 0],
                            (z != zz) | (half != v),
                        )

    with jax.named_scope("psum"):
        for flip in range(2):
            vec = lax.rem(half + flip, 2)
            for kind in range(2):
                value = None
                if flip == 0:
                    home = [y, x][kind]
                    value = keep[
                        kind, z // share, lax.rem(z, share), home, pl.ds(half * rows, rows)
                    ]
                for d in range(layers):
                    if flip == 0 and d == 0:
                        continue
                    zz = lax.rem(z + d, layers)
                    got(parts.at[zz, vec, kind], parts_recv.at[zz, vec, kind])
                    more = parts[zz, vec, kind].astype(f32)
                    value = more if value is None else value + more
                start = pl.multiple_of(vec * middle + kind * part, 128)
                out_ref[:, pl.ds(start, part)] = value

    assert len(pending) <= sends.shape[0]
    for i, (like, *conds) in enumerate(pending):
        wait = remote(like, like, sends.at[i], parts_recv.at[0, 0, 0], me, other).wait_send
        conds = [cond for cond in conds if cond is not None]
        if conds:
            pl.when(functools.reduce(jnp.logical_and, conds))(wait)
        else:
            wait()


def sends_of(layers):
    events = layers - 1
    slots = layers * 2
    count = 1 + 4 + 4 + 1 + 3 * CUTS + slots
    count += events * 8 + layers * 2 + 1
    count += 3 * CUTS * sum(events - e for e in range(events))
    return count + 4 + 2 * SUBS * 2 + 2 * layers * 2


def fused(tiles, trial, psi_v, psi_c, screened):
    rows, conduct = trial.shape[1:]
    valence, points = psi_v.shape
    width = psi_c.shape[2]
    middle = conduct // 2
    part = middle // 2
    layers = tiles // 4
    slots = layers * 2
    share = layers // SUBS
    bf16, f32 = jnp.bfloat16, jnp.float32
    far = pl.BlockSpec(memory_space=pl.ANY)
    dma = pltpu.SemaphoreType.DMA
    vmem = pltpu.VMEM
    out = pl.pallas_call(
        functools.partial(body, layers),
        out_shape=jax.ShapeDtypeStruct((rows, conduct), f32),
        in_specs=[far] * 4,
        out_specs=pl.BlockSpec(memory_space=vmem),
        scratch_shapes=[
            vmem((valence, conduct), bf16),
            vmem((2, layers, 2, 2, 2 * rows, points), bf16),
            vmem((2, points, valence), bf16),
            vmem((slots, points, width), f32),
            vmem((slots, points, width), f32),
            vmem((slots, points, width), bf16),
            vmem((slots, points, width), bf16),
            vmem((slots, conduct, width), bf16),
            vmem((2, points, conduct), bf16),
            vmem((2, 2, points, middle), f32),
            vmem((2, 2, points, part), bf16),
            vmem((2, 2, points, part), bf16),
            vmem((2, SUBS, share, 2, 2 * rows, part), bf16),
            vmem((2, SUBS, share, 2, 2 * rows, part), bf16),
            vmem((2, SUBS, share, 2, 2 * rows, part), f32),
            vmem((2, SUBS, share, 2 * rows, part), bf16),
            vmem((2, SUBS, share, 2 * rows, part), bf16),
            vmem((2, SUBS, share, 2 * rows, part), bf16),
            vmem((layers, 2, 2, rows, part), bf16),
            dma((3 + 2 * slots,)),
            dma((sends_of(layers),)),
            dma((tiles,)),
            dma((tiles,)),
            dma((2,)),
            dma((slots,)),
            dma((slots, CUTS)),
            dma((2, 2)),
            dma((2, SUBS)),
            dma((2, SUBS)),
            dma((layers, 2, 2)),
        ],
        compiler_params=pltpu.CompilerParams(
            collective_id=0, has_side_effects=True, vmem_limit_bytes=58 * 1024 * 1024
        ),
    )(
        trial[0],
        psi_v.reshape(layers, 2, 2, 2 * rows, points),
        psi_c[:, 0, :],
        screened,
    )
    return out[None]


def solution(mesh):
    tiles = mesh.shape["tile"]

    def shards(trial, psi_v, psi_c, screened):
        fits = (
            trial.shape[0] == 1
            and mesh.shape["vec"] == 2
            and tiles % (4 * SUBS) == 0
            and psi_v.shape[1] % 128 == 0
            and psi_c.shape[2] % 128 == 0
            and trial.shape[1] % 16 == 0
            and trial.shape[2] % 512 == 0
        )
        if fits:
            return fused(tiles, trial, psi_v, psi_c, screened)
        return plain(trial, psi_v, psi_c, screened)

    in_specs = (
        P(None, ("tile", "vec"), None),
        P(None, "tile"),
        P(None, "vec", "tile"),
        P("tile", "vec"),
    )
    out_specs = P(None, ("tile", "vec"), None)
    return jax.shard_map(shards, mesh=mesh, in_specs=in_specs, out_specs=out_specs, check_vma=False)
```

```python
import functools

import jax
import jax.numpy as jnp
from jax import lax
from jax.experimental import pallas as pl
from jax.experimental.pallas import tpu as pltpu
from jax.sharding import PartitionSpec as P

CUTS = 4
SUBS = 2


def back_product(weighted_flat, panel):
    return lax.dot_general(
        weighted_flat, panel, (((1,), (1,)), ((), ())), preferred_element_type=jnp.float32
    )


def plain(trial, psi_v, psi_c, screened):
    count = trial.shape[0]
    points = psi_v.shape[1]
    conduct = trial.shape[2]
    whole = lax.all_gather(trial, ("tile", "vec"), axis=1, tiled=True)
    projected = jnp.einsum("vp,kvc->kpc", psi_v, whole, preferred_element_type=jnp.float32).astype(
        jnp.bfloat16
    )
    flat = projected.reshape(count * points, conduct)
    panel_local = psi_c[:, 0, :]
    panel = lax.all_gather(panel_local, "tile", axis=1, tiled=True)
    pair = jnp.dot(flat, panel, preferred_element_type=jnp.float32)
    weighted = (screened[None] * pair.reshape(count, points, -1)).astype(jnp.bfloat16)
    weighted_flat = weighted.reshape(count * points, -1)
    back = back_product(weighted_flat, panel)
    back = back.reshape(count, points, conduct)
    left = psi_v.astype(jnp.float32)
    summed = lax.psum(back, "vec")
    tiles = lax.axis_size("tile")
    halves = lax.axis_size("vec")
    owned = left.shape[0] // (tiles * halves)
    grouped = left.reshape(tiles, halves, owned, points)
    mine = lax.dynamic_index_in_dim(grouped, lax.axis_index("vec"), 1, keepdims=False).reshape(
        tiles * owned, points
    )
    pieces = []
    for one in range(count):
        term = jnp.dot(mine, summed[one], precision=lax.Precision.HIGHEST)
        pieces.append(lax.psum_scatter(term, "tile", scatter_dimension=0, tiled=True))
    return jnp.stack(pieces, axis=0)


def sources_of(layers):
    return [
        sorted((o for o in range(layers) if o != z), key=lambda o: (abs(o - z), o))
        for z in range(layers)
    ]


def pick(values, at):
    chosen = jnp.int32(values[0])
    for k, value in enumerate(values[1:], 1):
        chosen = jnp.where(at == k, jnp.int32(value), chosen)
    return chosen


def body(
    layers,
    trial_hbm,
    psi_v_hbm,
    psi_c_hbm,
    screened_hbm,
    out_ref,
    whole,
    psi,
    psi_t,
    stage,
    screened_own,
    screened_out,
    screened_in,
    panel,
    flat,
    back,
    give,
    take,
    first_send,
    first_got,
    keep,
    leave,
    second_send,
    second_got,
    third,
    parts,
    local_sem,
    sends,
    trial_recv,
    hand_recv,
    psi_recv,
    screened_recv,
    block_recv,
    take_recv,
    first_recv,
    second_recv,
    parts_recv,
):
    bf16, f32 = jnp.bfloat16, jnp.float32
    me = lax.axis_index("tile")
    half = lax.axis_index("vec")
    other = 1 - half
    z, y, x = me // 4, (me // 2) % 2, me % 2
    across = lax.rem(y + 1, 2)
    aside = lax.rem(x + 1, 2)
    table = sources_of(layers)
    events = layers - 1
    source = [pick([row[e] for row in table], z) for e in range(events)]
    distance = [pick([abs(row[e] - k) for k, row in enumerate(table)], z) for e in range(events)]
    at_distance = [[distance[e] == k for k in range(layers)] for e in range(events)]

    def tile_of(zz, yy, xx):
        return zz * 4 + yy * 2 + xx

    mate_x, mate_y = tile_of(z, y, aside), tile_of(z, across, x)
    up, down = jnp.minimum(z + 1, layers - 1), jnp.maximum(z - 1, 0)
    has_up, has_down = z < layers - 1, z > 0
    on_up = [has_up & (source[e] < z) for e in range(events)]
    on_down = [has_down & (source[e] > z) for e in range(events)]

    def slot_of(zz, yy):
        return zz * 2 + yy

    slots = layers * 2
    order = [("own", 0)]
    for e in range(events):
        order += [("z", e), ("y", e - 1)]
    order += [("y", events - 1)]

    def slot_at(kind, e):
        zz = source[e] if e >= 0 and kind != "own" else z
        return slot_of(zz, across if kind == "y" else y)

    turns = [slot_at(*event) for event in order]

    rows, conduct = trial_hbm.shape
    width = psi_c_hbm.shape[1]
    points = psi_v_hbm.shape[-1]
    middle = conduct // 2
    part = middle // 2
    height = psi_c_hbm.shape[0] // CUTS

    def lines(tile, vec):
        start = pl.multiple_of((tile * 2 + vec) * rows, rows)
        return whole.at[pl.ds(start, rows), :]

    def columns(tile):
        return pl.ds(pl.multiple_of(tile * width, 128), width)

    local = []

    def load(src, dst):
        copy = pltpu.make_async_copy(src, dst, local_sem.at[len(local)])
        copy.start()
        local.append(copy)
        return copy

    load_psi = load(psi_v_hbm, psi.at[0])
    load_rows = load(trial_hbm, lines(me, half))
    load_out = [
        load(screened_hbm.at[:, columns(turn * 2 + aside)], stage.at[i])
        for i, turn in enumerate(turns)
    ]
    load_block = load(psi_c_hbm, panel.at[slot_of(z, y)])
    load_own = [
        load(screened_hbm.at[:, columns(turn * 2 + x)], screened_own.at[i])
        for i, turn in enumerate(turns)
    ]

    def remote(src, dst, send, recv, tile, vec):
        return pltpu.make_async_remote_copy(
            src_ref=src,
            dst_ref=dst,
            send_sem=send,
            recv_sem=recv,
            device_id=(tile, vec),
            device_id_type=pl.DeviceIdType.MESH,
        )

    partners = [(mate_x, half), (mate_y, half), (me, other)]
    for d in range(1, layers):
        for v in range(2):
            partners.append((tile_of(lax.rem(z + d, layers), y, x), v))
    with jax.named_scope("pbar"):
        barrier = pltpu.get_barrier_semaphore()
        for partner in partners:
            pl.semaphore_signal(
                barrier, inc=1, device_id=partner, device_id_type=pl.DeviceIdType.MESH
            )
        pl.semaphore_wait(barrier, len(partners))

    pending = []

    def send(src, dst, recv, tile, vec, like, cond=None):
        i = len(pending)
        copy = remote(src, dst, sends.at[i], recv, tile, vec)
        pending.append((like, cond))
        if cond is None:
            copy.start()
        else:
            pl.when(cond)(copy.start)

    def got(ref, recv):
        remote(ref, ref, sends.at[0], recv, me, other).wait_recv()

    some_rows = whole.at[pl.ds(0, rows), :]

    def piece(ref, s):
        return ref.at[pl.ds(s * height, height), :]

    some_piece = piece(panel.at[0], 0)

    def hand(src, tile):
        send(src, lines(tile, half), hand_recv.at[tile], me, other, some_rows)

    def spread(src, tile, to_up, to_down):
        dst = lines(tile, half)
        recv = trial_recv.at[tile]
        send(src, dst, recv, tile_of(up, y, x), half, some_rows, to_up)
        send(src, dst, recv, tile_of(down, y, x), half, some_rows, to_down)
        send(src, dst, recv, mate_y, half, some_rows)
        hand(src, tile)

    last = CUTS - 1
    home_slot, mate_slot = slot_of(z, y), slot_of(z, across)

    def along(src, slot, s, to_up, to_down):
        dst = piece(panel.at[slot], s)
        recv = block_recv.at[slot, s]
        send(src, dst, recv, tile_of(up, y, x), half, some_piece, to_up)
        send(src, dst, recv, tile_of(down, y, x), half, some_piece, to_down)

    def cross(src, slot, s):
        dst = piece(panel.at[slot], s)
        send(src, dst, block_recv.at[slot, s], mate_y, half, some_piece)

    def own_piece_z(s):
        along(piece(psi_c_hbm, s), home_slot, s, has_up, has_down)

    def own_piece_y(s):
        cross(piece(psi_c_hbm, s), home_slot, s)

    def came(slot, s):
        ref = piece(panel.at[slot], s)
        got(ref, block_recv.at[slot, s])
        return ref

    pair_layers = layers // 2

    def psi_half(ref, which):
        return ref.at[pl.ds(which * pair_layers, pair_layers)]

    with jax.named_scope("ptrial"):
        send(trial_hbm, lines(me, half), trial_recv.at[me], mate_x, half, some_rows)
        spread(trial_hbm, me, has_up, has_down)
        send(
            psi_half(psi_v_hbm, half),
            psi_half(psi.at[1], half),
            psi_recv.at[0],
            mate_x,
            half,
            psi_half(psi.at[1], 0),
        )
        got(lines(mate_x, half), trial_recv.at[mate_x])
        spread(lines(mate_x, half), mate_x, has_up, has_down)

        for i in range(slots):
            load_out[i].wait()
            screened_out[i] = stage[i].astype(bf16)
        for i in range(slots):
            send(
                screened_out.at[i],
                screened_in.at[i],
                screened_recv.at[i],
                mate_x,
                half,
                screened_out.at[0],
            )

        for e in range(events):
            for xx in range(2):
                tile = tile_of(source[e], y, xx)
                ref = lines(tile, half)
                got(ref, trial_recv.at[tile])
                spread(ref, tile, on_up[e], on_down[e])
            if e == events - 2:
                own_piece_y(last)
                own_piece_z(0)
        for s in range(CUTS):
            if s < last:
                own_piece_y(s)
            if s > 0:
                own_piece_z(s)

        back[...] = jnp.zeros_like(back)
        load_psi.wait()
        valence = layers * 4 * 2 * rows
        psi_t[0] = psi[0].reshape(valence, points).T

        for e in range(-1, events):
            for xx in range(2):
                tile = tile_of(source[e] if e >= 0 else z, across, xx)
                ref = lines(tile, half)
                got(ref, trial_recv.at[tile])
                hand(ref, tile)

        ref = psi_half(psi.at[1], half)
        got(ref, psi_recv.at[0])
        send(ref, ref, psi_recv.at[1], me, other, psi_half(psi.at[1], 0))
        load_rows.wait()
        along(came(mate_slot, last), mate_slot, last, has_up, has_down)
        for tile in range(layers * 4):
            got(lines(tile, other), hand_recv.at[tile])

    wide = 256

    def project(p):
        def chunk(j, carry):
            cols = pl.ds(pl.multiple_of(j * wide, wide), wide)
            flat[p, :, cols] = jnp.dot(
                psi_t[p], whole[:, cols], preferred_element_type=f32
            ).astype(bf16)
            return carry

        lax.fori_loop(0, conduct // wide, chunk, 0)

    with jax.named_scope("pproj"):
        project(0)
        got(psi_half(psi.at[1], other), psi_recv.at[1])
        psi_t[1] = psi[1].reshape(valence, points).T
        project(1)

    def arrive(e):
        slot = slot_of(source[e], y)
        for s in range(CUTS):
            ref = came(slot, s)
            along(ref, slot, s, on_up[e], on_down[e])
            if s < last:
                cross(ref, slot, s)
        slot = slot_of(source[e], across)
        along(came(slot, last), slot, last, on_up[e], on_down[e])

    def arrive_if(e, k):
        start = len(pending)

        @pl.when(at_distance[e][k])
        def _():
            arrive(e)

        for i in range(start, len(pending)):
            pending[i] += (at_distance[e][k],)

    def receive(i):
        kind, e = order[i]
        if kind == "z":
            for late in range(e, events):
                arrive_if(late, e + 1)
        if kind == "y":
            for s in range(last):
                came(turns[i], s)
        load_own[i].wait()

    def step(p, share, slot):
        block = panel.at[slot]
        pair = jnp.dot(flat[p], block[...], preferred_element_type=f32)
        weighted = (share.astype(f32) * pair).astype(bf16)
        for h in range(2):
            back[p, h] += back_product(weighted, block[pl.ds(h * middle, middle), :])

    load_block.wait()

    def use(k, carry):
        slot = turns[0]
        for i in range(final):
            slot = jnp.where(k == i, turns[i], slot)

            @pl.when(k == i)
            def _(i=i):
                receive(i)

        step(0, screened_own[k], slot)
        got(screened_in.at[k], screened_recv.at[k])
        step(1, screened_in[k], slot)
        return carry

    final = slots - 1
    with jax.named_scope("puse"):
        lax.fori_loop(0, final, use, 0)
        receive(final)
        step(0, screened_own[final], turns[final])

    def span(kind):
        return pl.ds(kind * part, part)

    def swap(p):
        for kind in range(2):
            give[kind, p] = back[p, other, :, span(kind)].astype(bf16)
            send(
                give.at[kind, p],
                take.at[kind, p],
                take_recv.at[kind, p],
                me,
                other,
                give.at[0, 0],
            )

    def split(kind, p):
        got(take.at[kind, p], take_recv.at[kind, p])
        total = back[p, half, :, span(kind)] + take[kind, p].astype(f32)
        high = total.astype(bf16)
        flat[p, :, span(kind)] = high
        low = (total - high.astype(f32)).astype(bf16)
        flat[p, :, pl.ds(middle + kind * part, part)] = low

    share = layers // SUBS
    block_rows = 2 * rows

    def product(p, kind, at, sub):
        if kind == 0:
            left = psi[p, pl.ds(sub * share, share), :, pl.ds(at, 1)]
        else:
            left = psi[p, pl.ds(sub * share, share), pl.ds(at, 1)]
        left = left.reshape(share * 2 * block_rows, points)
        total = None
        for level in range(2):
            cols = pl.ds(level * middle + kind * part, part)
            value = jnp.dot(left, flat[p, :, cols], preferred_element_type=f32)
            total = value if total is None else total + value
        return total.reshape(share, 2, block_rows, part)

    settled = [0]

    def settle():
        for i in range(settled[0], len(pending)):
            like, *conds = pending[i]
            wait = remote(like, like, sends.at[i], parts_recv.at[0, 0, 0], me, other).wait_send
            conds = [cond for cond in conds if cond is not None]
            if conds:
                pl.when(functools.reduce(jnp.logical_and, conds))(wait)
            else:
                wait()
        settled[0] = len(pending)

    mates = [mate_x, mate_y]
    homes, aways = [x, y], [aside, across]
    with jax.named_scope("pearly"):
        swap(0)
        for kind in range(2):
            split(kind, 0)
        for sub in range(SUBS):
            for kind in range(2):
                keep[kind, sub] = product(0, kind, homes[kind], sub)
                leave[kind, sub] = product(0, kind, aways[kind], sub)

    with jax.named_scope("plast"):
        got(screened_in.at[final], screened_recv.at[final])
        step(1, screened_in[final], turns[final])

    with jax.named_scope("pfin"):
        swap(1)
        for sub in range(SUBS):
            for kind in range(2):
                if sub == 0:
                    split(kind, 1)
                value = leave[kind, sub] + product(1, kind, aways[kind], sub)
                first_send[kind, sub] = value.astype(bf16)
                send(
                    first_send.at[kind, sub],
                    first_got.at[kind, sub],
                    first_recv.at[kind, sub],
                    mates[kind],
                    half,
                    first_send.at[0, 0],
                )
        for sub in range(SUBS):
            for kind in range(2):
                keep[kind, sub] += product(1, kind, homes[kind], sub)

    with jax.named_scope("psettle"):
        settle()

    with jax.named_scope("psecond"):
        for sub in range(SUBS):
            for kind in range(2):
                got(first_got.at[kind, sub], first_recv.at[kind, sub])
                away, home = [(across, y), (aside, x)][kind]

                def summed(at, kind=kind, sub=sub):
                    mine = keep[kind, sub, :, pl.ds(at, 1)]
                    theirs = first_got[kind, sub, :, pl.ds(at, 1)].astype(f32)
                    return (mine + theirs).reshape(share, block_rows, part)

                second_send[kind, sub] = summed(away).astype(bf16)
                send(
                    second_send.at[kind, sub],
                    second_got.at[kind, sub],
                    second_recv.at[kind, sub],
                    mates[1 - kind],
                    half,
                    second_send.at[0, 0],
                )
                keep[kind, sub, :, pl.ds(home, 1)] = summed(home).reshape(
                    share, 1, block_rows, part
                )

    with jax.named_scope("pthird"):
        for sub in range(SUBS):
            for kind in range(2):
                got(second_got.at[kind, sub], second_recv.at[kind, sub])
                home = [y, x][kind]
                mine = keep[kind, sub, :, pl.ds(home, 1)].reshape(share, block_rows, part)
                value = mine + second_got[kind, sub].astype(f32)
                keep[kind, sub, :, pl.ds(home, 1)] = value.reshape(share, 1, block_rows, part)
                third[kind, sub] = value.astype(bf16)
                for i in range(share):
                    zz = sub * share + i
                    for v in range(2):
                        send(
                            third.at[kind, sub, i, pl.ds(v * rows, rows)],
                            parts.at[z, half, kind],
                            parts_recv.at[z, half, kind],
                            tile_of(zz, y, x),
                            v,
                            parts.at[0, 0, 0],
                            (z != zz) | (half != v),
                        )

    with jax.named_scope("psum"):
        for flip in range(2):
            vec = lax.rem(half + flip, 2)
            for kind in range(2):
                value = None
                if flip == 0:
                    home = [y, x][kind]
                    value = keep[
                        kind, z // share, lax.rem(z, share), home, pl.ds(half * rows, rows)
                    ]
                for d in range(layers):
                    if flip == 0 and d == 0:
                        continue
                    zz = lax.rem(z + d, layers)
                    got(parts.at[zz, vec, kind], parts_recv.at[zz, vec, kind])
                    more = parts[zz, vec, kind].astype(f32)
                    value = more if value is None else value + more
                start = pl.multiple_of(vec * middle + kind * part, 128)
                out_ref[:, pl.ds(start, part)] = value

    assert len(pending) <= sends.shape[0]
    settle()


def sends_of(layers):
    events = layers - 1
    slots = layers * 2
    count = 1 + 4 + 4 + 1 + 3 * CUTS + slots
    count += events * 8 + layers * 2 + 1
    count += 2 + (3 * CUTS + 2) * sum(events - e for e in range(events))
    return count + 4 + 2 * SUBS * 2 + 2 * layers * 2


def fused(tiles, trial, psi_v, psi_c, screened):
    rows, conduct = trial.shape[1:]
    valence, points = psi_v.shape
    width = psi_c.shape[2]
    middle = conduct // 2
    part = middle // 2
    layers = tiles // 4
    slots = layers * 2
    share = layers // SUBS
    bf16, f32 = jnp.bfloat16, jnp.float32
    far = pl.BlockSpec(memory_space=pl.ANY)
    dma = pltpu.SemaphoreType.DMA
    vmem = pltpu.VMEM
    out = pl.pallas_call(
        functools.partial(body, layers),
        out_shape=jax.ShapeDtypeStruct((rows, conduct), f32),
        in_specs=[far] * 4,
        out_specs=pl.BlockSpec(memory_space=vmem),
        scratch_shapes=[
            vmem((valence, conduct), bf16),
            vmem((2, layers, 2, 2, 2 * rows, points), bf16),
            vmem((2, points, valence), bf16),
            vmem((slots, points, width), f32),
            vmem((slots, points, width), f32),
            vmem((slots, points, width), bf16),
            vmem((slots, points, width), bf16),
            vmem((slots, conduct, width), bf16),
            vmem((2, points, conduct), bf16),
            vmem((2, 2, points, middle), f32),
            vmem((2, 2, points, part), bf16),
            vmem((2, 2, points, part), bf16),
            vmem((2, SUBS, share, 2, 2 * rows, part), bf16),
            vmem((2, SUBS, share, 2, 2 * rows, part), bf16),
            vmem((2, SUBS, share, 2, 2 * rows, part), f32),
            vmem((2, SUBS, share, 2, 2 * rows, part), f32),
            vmem((2, SUBS, share, 2 * rows, part), bf16),
            vmem((2, SUBS, share, 2 * rows, part), bf16),
            vmem((2, SUBS, share, 2 * rows, part), bf16),
            vmem((layers, 2, 2, rows, part), bf16),
            dma((3 + 2 * slots,)),
            dma((sends_of(layers),)),
            dma((tiles,)),
            dma((tiles,)),
            dma((2,)),
            dma((slots,)),
            dma((slots, CUTS)),
            dma((2, 2)),
            dma((2, SUBS)),
            dma((2, SUBS)),
            dma((layers, 2, 2)),
        ],
        compiler_params=pltpu.CompilerParams(
            collective_id=0, has_side_effects=True, vmem_limit_bytes=58 * 1024 * 1024
        ),
    )(
        trial[0],
        psi_v.reshape(layers, 2, 2, 2 * rows, points),
        psi_c[:, 0, :],
        screened,
    )
    return out[None]


def solution(mesh):
    tiles = mesh.shape["tile"]

    def shards(trial, psi_v, psi_c, screened):
        fits = (
            trial.shape[0] == 1
            and mesh.shape["vec"] == 2
            and tiles % (4 * SUBS) == 0
            and psi_v.shape[1] % 128 == 0
            and psi_c.shape[2] % 128 == 0
            and trial.shape[1] % 16 == 0
            and trial.shape[2] % 512 == 0
        )
        if fits:
            return fused(tiles, trial, psi_v, psi_c, screened)
        return plain(trial, psi_v, psi_c, screened)

    in_specs = (
        P(None, ("tile", "vec"), None),
        P(None, "tile"),
        P(None, "vec", "tile"),
        P("tile", "vec"),
    )
    out_specs = P(None, ("tile", "vec"), None)
    return jax.shard_map(shards, mesh=mesh, in_specs=in_specs, out_specs=out_specs, check_vma=False)
```

```python
import functools

import jax
import jax.numpy as jnp
from jax import lax
from jax.experimental import pallas as pl
from jax.experimental.pallas import tpu as pltpu
from jax.sharding import PartitionSpec as P

CUTS = 4
SUBS = 2


def back_product(weighted_flat, panel):
    return lax.dot_general(
        weighted_flat, panel, (((1,), (1,)), ((), ())), preferred_element_type=jnp.float32
    )


def plain(trial, psi_v, psi_c, screened):
    count = trial.shape[0]
    points = psi_v.shape[1]
    conduct = trial.shape[2]
    whole = lax.all_gather(trial, ("tile", "vec"), axis=1, tiled=True)
    projected = jnp.einsum("vp,kvc->kpc", psi_v, whole, preferred_element_type=jnp.float32).astype(
        jnp.bfloat16
    )
    flat = projected.reshape(count * points, conduct)
    panel_local = psi_c[:, 0, :]
    panel = lax.all_gather(panel_local, "tile", axis=1, tiled=True)
    pair = jnp.dot(flat, panel, preferred_element_type=jnp.float32)
    weighted = (screened[None] * pair.reshape(count, points, -1)).astype(jnp.bfloat16)
    weighted_flat = weighted.reshape(count * points, -1)
    back = back_product(weighted_flat, panel)
    back = back.reshape(count, points, conduct)
    left = psi_v.astype(jnp.float32)
    summed = lax.psum(back, "vec")
    tiles = lax.axis_size("tile")
    halves = lax.axis_size("vec")
    owned = left.shape[0] // (tiles * halves)
    grouped = left.reshape(tiles, halves, owned, points)
    mine = lax.dynamic_index_in_dim(grouped, lax.axis_index("vec"), 1, keepdims=False).reshape(
        tiles * owned, points
    )
    pieces = []
    for one in range(count):
        term = jnp.dot(mine, summed[one], precision=lax.Precision.HIGHEST)
        pieces.append(lax.psum_scatter(term, "tile", scatter_dimension=0, tiled=True))
    return jnp.stack(pieces, axis=0)


def sources_of(layers):
    return [
        sorted((o for o in range(layers) if o != z), key=lambda o: (abs(o - z), o))
        for z in range(layers)
    ]


def pick(values, at):
    chosen = jnp.int32(values[0])
    for k, value in enumerate(values[1:], 1):
        chosen = jnp.where(at == k, jnp.int32(value), chosen)
    return chosen


def body(
    layers,
    trial_hbm,
    psi_v_hbm,
    psi_c_hbm,
    screened_hbm,
    out_ref,
    whole,
    psi,
    psi_t,
    stage,
    screened_own,
    screened_out,
    screened_in,
    panel,
    flat,
    back,
    give,
    take,
    first_send,
    first_got,
    keep,
    leave,
    second_send,
    second_got,
    third,
    parts,
    local_sem,
    sends,
    trial_recv,
    hand_recv,
    psi_recv,
    screened_recv,
    block_recv,
    take_recv,
    first_recv,
    second_recv,
    parts_recv,
):
    bf16, f32 = jnp.bfloat16, jnp.float32
    me = lax.axis_index("tile")
    half = lax.axis_index("vec")
    other = 1 - half
    z, y, x = me // 4, (me // 2) % 2, me % 2
    across = lax.rem(y + 1, 2)
    aside = lax.rem(x + 1, 2)
    table = sources_of(layers)
    events = layers - 1
    source = [pick([row[e] for row in table], z) for e in range(events)]
    distance = [pick([abs(row[e] - k) for k, row in enumerate(table)], z) for e in range(events)]
    at_distance = [[distance[e] == k for k in range(layers)] for e in range(events)]

    def tile_of(zz, yy, xx):
        return zz * 4 + yy * 2 + xx

    mate_x, mate_y = tile_of(z, y, aside), tile_of(z, across, x)
    up, down = jnp.minimum(z + 1, layers - 1), jnp.maximum(z - 1, 0)
    has_up, has_down = z < layers - 1, z > 0
    on_up = [has_up & (source[e] < z) for e in range(events)]
    on_down = [has_down & (source[e] > z) for e in range(events)]

    def slot_of(zz, yy):
        return zz * 2 + yy

    slots = layers * 2
    order = [("own", 0)]
    for e in range(events):
        order += [("z", e), ("y", e - 1)]
    order += [("y", events - 1)]

    def slot_at(kind, e):
        zz = source[e] if e >= 0 and kind != "own" else z
        return slot_of(zz, across if kind == "y" else y)

    turns = [slot_at(*event) for event in order]

    rows, conduct = trial_hbm.shape
    width = psi_c_hbm.shape[1]
    points = psi_v_hbm.shape[-1]
    middle = conduct // 2
    part = middle // 2
    height = psi_c_hbm.shape[0] // CUTS

    def lines(tile, vec):
        start = pl.multiple_of((tile * 2 + vec) * rows, rows)
        return whole.at[pl.ds(start, rows), :]

    def columns(tile):
        return pl.ds(pl.multiple_of(tile * width, 128), width)

    local = []

    def load(src, dst):
        copy = pltpu.make_async_copy(src, dst, local_sem.at[len(local)])
        copy.start()
        local.append(copy)
        return copy

    load_rows = load(trial_hbm, lines(me, half))
    load_psi = load(psi_v_hbm, psi.at[0])
    load_block = load(psi_c_hbm, panel.at[slot_of(z, y)])

    def remote(src, dst, send, recv, tile, vec):
        return pltpu.make_async_remote_copy(
            src_ref=src,
            dst_ref=dst,
            send_sem=send,
            recv_sem=recv,
            device_id=(tile, vec),
            device_id_type=pl.DeviceIdType.MESH,
        )

    partners = [(mate_x, half), (mate_y, half), (me, other)]
    for d in range(1, layers):
        for v in range(2):
            partners.append((tile_of(lax.rem(z + d, layers), y, x), v))
    with jax.named_scope("pbar"):
        barrier = pltpu.get_barrier_semaphore()
        for partner in partners:
            pl.semaphore_signal(
                barrier, inc=1, device_id=partner, device_id_type=pl.DeviceIdType.MESH
            )
        pl.semaphore_wait(barrier, len(partners))

    pending = []

    def send(src, dst, recv, tile, vec, like, cond=None):
        i = len(pending)
        copy = remote(src, dst, sends.at[i], recv, tile, vec)
        pending.append((like, cond))
        if cond is None:
            copy.start()
        else:
            pl.when(cond)(copy.start)

    def got(ref, recv):
        remote(ref, ref, sends.at[0], recv, me, other).wait_recv()

    some_rows = whole.at[pl.ds(0, rows), :]

    def piece(ref, s):
        return ref.at[pl.ds(s * height, height), :]

    some_piece = piece(panel.at[0], 0)

    def hand(src, tile):
        send(src, lines(tile, half), hand_recv.at[tile], me, other, some_rows)

    def spread(tile, column):
        ref = lines(tile, half)
        recv = trial_recv.at[tile]
        if column:
            for e in range(events):
                send(ref, ref, recv, tile_of(source[e], y, x), half, some_rows)
        send(ref, ref, recv, mate_y, half, some_rows)
        hand(ref, tile)

    last = CUTS - 1
    home_slot, mate_slot = slot_of(z, y), slot_of(z, across)

    def along(src, slot, s, to_up, to_down):
        dst = piece(panel.at[slot], s)
        recv = block_recv.at[slot, s]
        send(src, dst, recv, tile_of(up, y, x), half, some_piece, to_up)
        send(src, dst, recv, tile_of(down, y, x), half, some_piece, to_down)

    def cross(src, slot, s):
        dst = piece(panel.at[slot], s)
        send(src, dst, block_recv.at[slot, s], mate_y, half, some_piece)

    def own_piece_z(s):
        along(piece(panel.at[home_slot], s), home_slot, s, has_up, has_down)

    def own_piece_y(s):
        cross(piece(panel.at[home_slot], s), home_slot, s)

    def came(slot, s):
        ref = piece(panel.at[slot], s)
        got(ref, block_recv.at[slot, s])
        return ref

    pair_layers = layers // 2

    def psi_half(ref, which):
        return ref.at[pl.ds(which * pair_layers, pair_layers)]

    with jax.named_scope("ptrial"):
        ref = lines(me, half)
        load_rows.wait()
        send(ref, ref, trial_recv.at[me], mate_x, half, some_rows)
        spread(me, True)
        load_out = [
            load(screened_hbm.at[:, columns(turn * 2 + aside)], stage.at[i])
            for i, turn in enumerate(turns)
        ]
        load_own = [
            load(screened_hbm.at[:, columns(turn * 2 + x)], screened_own.at[i])
            for i, turn in enumerate(turns)
        ]
        load_psi.wait()
        send(
            psi_half(psi.at[0], half),
            psi_half(psi.at[1], half),
            psi_recv.at[0],
            mate_x,
            half,
            psi_half(psi.at[1], 0),
        )
        got(lines(mate_x, half), trial_recv.at[mate_x])
        spread(mate_x, True)
        load_block.wait()
        own_piece_y(last)
        for s in range(CUTS):
            own_piece_z(s)

        for i in range(slots):
            load_out[i].wait()
            screened_out[i] = stage[i].astype(bf16)
        for i in range(slots):
            send(
                screened_out.at[i],
                screened_in.at[i],
                screened_recv.at[i],
                mate_x,
                half,
                screened_out.at[0],
            )

        for e in range(events):
            for xx in range(2):
                tile = tile_of(source[e], y, xx)
                got(lines(tile, half), trial_recv.at[tile])
                spread(tile, False)
        for s in range(last):
            own_piece_y(s)

        back[...] = jnp.zeros_like(back)
        valence = layers * 4 * 2 * rows
        psi_t[0] = psi[0].reshape(valence, points).T

        for e in range(-1, events):
            for xx in range(2):
                tile = tile_of(source[e] if e >= 0 else z, across, xx)
                ref = lines(tile, half)
                got(ref, trial_recv.at[tile])
                hand(ref, tile)

        ref = psi_half(psi.at[1], half)
        got(ref, psi_recv.at[0])
        send(ref, ref, psi_recv.at[1], me, other, psi_half(psi.at[1], 0))
        along(came(mate_slot, last), mate_slot, last, has_up, has_down)
        for tile in range(layers * 4):
            got(lines(tile, other), hand_recv.at[tile])

    wide = 256

    def project(p):
        def chunk(j, carry):
            cols = pl.ds(pl.multiple_of(j * wide, wide), wide)
            flat[p, :, cols] = jnp.dot(
                psi_t[p], whole[:, cols], preferred_element_type=f32
            ).astype(bf16)
            return carry

        lax.fori_loop(0, conduct // wide, chunk, 0)

    with jax.named_scope("pproj"):
        project(0)
        got(psi_half(psi.at[1], other), psi_recv.at[1])
        psi_t[1] = psi[1].reshape(valence, points).T
        project(1)

    def arrive(e):
        slot = slot_of(source[e], y)
        for s in range(CUTS):
            ref = came(slot, s)
            along(ref, slot, s, on_up[e], on_down[e])
            if s < last:
                cross(ref, slot, s)
        slot = slot_of(source[e], across)
        along(came(slot, last), slot, last, on_up[e], on_down[e])

    def arrive_if(e, k):
        start = len(pending)

        @pl.when(at_distance[e][k])
        def _():
            arrive(e)

        for i in range(start, len(pending)):
            pending[i] += (at_distance[e][k],)

    def receive(i):
        kind, e = order[i]
        if kind == "z":
            for late in range(e, events):
                arrive_if(late, e + 1)
        if kind == "y":
            for s in range(last):
                came(turns[i], s)
        load_own[i].wait()

    def step(p, share, slot):
        block = panel.at[slot]
        pair = jnp.dot(flat[p], block[...], preferred_element_type=f32)
        weighted = (share.astype(f32) * pair).astype(bf16)
        for h in range(2):
            back[p, h] += back_product(weighted, block[pl.ds(h * middle, middle), :])

    def use(k, carry):
        slot = turns[0]
        for i in range(final):
            slot = jnp.where(k == i, turns[i], slot)

            @pl.when(k == i)
            def _(i=i):
                receive(i)

        step(0, screened_own[k], slot)
        got(screened_in.at[k], screened_recv.at[k])
        step(1, screened_in[k], slot)
        return carry

    final = slots - 1
    with jax.named_scope("puse"):
        lax.fori_loop(0, final, use, 0)
        receive(final)
        step(0, screened_own[final], turns[final])

    def span(kind):
        return pl.ds(kind * part, part)

    def swap(p):
        for kind in range(2):
            give[kind, p] = back[p, other, :, span(kind)].astype(bf16)
            send(
                give.at[kind, p],
                take.at[kind, p],
                take_recv.at[kind, p],
                me,
                other,
                give.at[0, 0],
            )

    def split(kind, p):
        got(take.at[kind, p], take_recv.at[kind, p])
        total = back[p, half, :, span(kind)] + take[kind, p].astype(f32)
        high = total.astype(bf16)
        flat[p, :, span(kind)] = high
        low = (total - high.astype(f32)).astype(bf16)
        flat[p, :, pl.ds(middle + kind * part, part)] = low

    share = layers // SUBS
    block_rows = 2 * rows

    def product(p, kind, at, sub):
        if kind == 0:
            left = psi[p, pl.ds(sub * share, share), :, pl.ds(at, 1)]
        else:
            left = psi[p, pl.ds(sub * share, share), pl.ds(at, 1)]
        left = left.reshape(share * 2 * block_rows, points)
        total = None
        for level in range(2):
            cols = pl.ds(level * middle + kind * part, part)
            value = jnp.dot(left, flat[p, :, cols], preferred_element_type=f32)
            total = value if total is None else total + value
        return total.reshape(share, 2, block_rows, part)

    settled = [0]

    def settle():
        for i in range(settled[0], len(pending)):
            like, *conds = pending[i]
            wait = remote(like, like, sends.at[i], parts_recv.at[0, 0, 0], me, other).wait_send
            conds = [cond for cond in conds if cond is not None]
            if conds:
                pl.when(functools.reduce(jnp.logical_and, conds))(wait)
            else:
                wait()
        settled[0] = len(pending)

    mates = [mate_x, mate_y]
    homes, aways = [x, y], [aside, across]
    with jax.named_scope("pearly"):
        swap(0)
        for kind in range(2):
            split(kind, 0)
        for sub in range(SUBS):
            for kind in range(2):
                keep[kind, sub] = product(0, kind, homes[kind], sub)
                leave[kind, sub] = product(0, kind, aways[kind], sub)

    with jax.named_scope("plast"):
        got(screened_in.at[final], screened_recv.at[final])
        step(1, screened_in[final], turns[final])

    with jax.named_scope("pfin"):
        swap(1)
        for sub in range(SUBS):
            for kind in range(2):
                if sub == 0:
                    split(kind, 1)
                value = leave[kind, sub] + product(1, kind, aways[kind], sub)
                first_send[kind, sub] = value.astype(bf16)
                send(
                    first_send.at[kind, sub],
                    first_got.at[kind, sub],
                    first_recv.at[kind, sub],
                    mates[kind],
                    half,
                    first_send.at[0, 0],
                )
        for sub in range(SUBS):
            for kind in range(2):
                keep[kind, sub] += product(1, kind, homes[kind], sub)

    with jax.named_scope("psettle"):
        settle()

    with jax.named_scope("psecond"):
        for sub in range(SUBS):
            for kind in range(2):
                got(first_got.at[kind, sub], first_recv.at[kind, sub])
                away, home = [(across, y), (aside, x)][kind]

                def summed(at, kind=kind, sub=sub):
                    mine = keep[kind, sub, :, pl.ds(at, 1)]
                    theirs = first_got[kind, sub, :, pl.ds(at, 1)].astype(f32)
                    return (mine + theirs).reshape(share, block_rows, part)

                second_send[kind, sub] = summed(away).astype(bf16)
                send(
                    second_send.at[kind, sub],
                    second_got.at[kind, sub],
                    second_recv.at[kind, sub],
                    mates[1 - kind],
                    half,
                    second_send.at[0, 0],
                )
                keep[kind, sub, :, pl.ds(home, 1)] = summed(home).reshape(
                    share, 1, block_rows, part
                )

    with jax.named_scope("pthird"):
        for sub in range(SUBS):
            for kind in range(2):
                got(second_got.at[kind, sub], second_recv.at[kind, sub])
                home = [y, x][kind]
                mine = keep[kind, sub, :, pl.ds(home, 1)].reshape(share, block_rows, part)
                value = mine + second_got[kind, sub].astype(f32)
                keep[kind, sub, :, pl.ds(home, 1)] = value.reshape(share, 1, block_rows, part)
                third[kind, sub] = value.astype(bf16)
                for i in range(share):
                    zz = sub * share + i
                    for v in range(2):
                        send(
                            third.at[kind, sub, i, pl.ds(v * rows, rows)],
                            parts.at[z, half, kind],
                            parts_recv.at[z, half, kind],
                            tile_of(zz, y, x),
                            v,
                            parts.at[0, 0, 0],
                            (z != zz) | (half != v),
                        )

    with jax.named_scope("psum"):
        for flip in range(2):
            vec = lax.rem(half + flip, 2)
            for kind in range(2):
                value = None
                if flip == 0:
                    home = [y, x][kind]
                    value = keep[
                        kind, z // share, lax.rem(z, share), home, pl.ds(half * rows, rows)
                    ]
                for d in range(layers):
                    if flip == 0 and d == 0:
                        continue
                    zz = lax.rem(z + d, layers)
                    got(parts.at[zz, vec, kind], parts_recv.at[zz, vec, kind])
                    more = parts[zz, vec, kind].astype(f32)
                    value = more if value is None else value + more
                start = pl.multiple_of(vec * middle + kind * part, 128)
                out_ref[:, pl.ds(start, part)] = value

    assert len(pending) <= sends.shape[0]
    settle()


def sends_of(layers):
    events = layers - 1
    slots = layers * 2
    count = 1 + 2 * (events + 2) + 1 + 3 * CUTS + slots
    count += events * 4 + layers * 2 + 1
    count += 2 + (3 * CUTS + 2) * sum(events - e for e in range(events))
    return count + 4 + 2 * SUBS * 2 + 2 * layers * 2


def fused(tiles, trial, psi_v, psi_c, screened):
    rows, conduct = trial.shape[1:]
    valence, points = psi_v.shape
    width = psi_c.shape[2]
    middle = conduct // 2
    part = middle // 2
    layers = tiles // 4
    slots = layers * 2
    share = layers // SUBS
    bf16, f32 = jnp.bfloat16, jnp.float32
    far = pl.BlockSpec(memory_space=pl.ANY)
    dma = pltpu.SemaphoreType.DMA
    vmem = pltpu.VMEM
    out = pl.pallas_call(
        functools.partial(body, layers),
        out_shape=jax.ShapeDtypeStruct((rows, conduct), f32),
        in_specs=[far] * 4,
        out_specs=pl.BlockSpec(memory_space=vmem),
        scratch_shapes=[
            vmem((valence, conduct), bf16),
            vmem((2, layers, 2, 2, 2 * rows, points), bf16),
            vmem((2, points, valence), bf16),
            vmem((slots, points, width), f32),
            vmem((slots, points, width), f32),
            vmem((slots, points, width), bf16),
            vmem((slots, points, width), bf16),
            vmem((slots, conduct, width), bf16),
            vmem((2, points, conduct), bf16),
            vmem((2, 2, points, middle), f32),
            vmem((2, 2, points, part), bf16),
            vmem((2, 2, points, part), bf16),
            vmem((2, SUBS, share, 2, 2 * rows, part), bf16),
            vmem((2, SUBS, share, 2, 2 * rows, part), bf16),
            vmem((2, SUBS, share, 2, 2 * rows, part), f32),
            vmem((2, SUBS, share, 2, 2 * rows, part), f32),
            vmem((2, SUBS, share, 2 * rows, part), bf16),
            vmem((2, SUBS, share, 2 * rows, part), bf16),
            vmem((2, SUBS, share, 2 * rows, part), bf16),
            vmem((layers, 2, 2, rows, part), bf16),
            dma((3 + 2 * slots,)),
            dma((sends_of(layers),)),
            dma((tiles,)),
            dma((tiles,)),
            dma((2,)),
            dma((slots,)),
            dma((slots, CUTS)),
            dma((2, 2)),
            dma((2, SUBS)),
            dma((2, SUBS)),
            dma((layers, 2, 2)),
        ],
        compiler_params=pltpu.CompilerParams(
            collective_id=0, has_side_effects=True, vmem_limit_bytes=58 * 1024 * 1024
        ),
    )(
        trial[0],
        psi_v.reshape(layers, 2, 2, 2 * rows, points),
        psi_c[:, 0, :],
        screened,
    )
    return out[None]


def solution(mesh):
    tiles = mesh.shape["tile"]

    def shards(trial, psi_v, psi_c, screened):
        fits = (
            trial.shape[0] == 1
            and mesh.shape["vec"] == 2
            and tiles % (4 * SUBS) == 0
            and psi_v.shape[1] % 128 == 0
            and psi_c.shape[2] % 128 == 0
            and trial.shape[1] % 16 == 0
            and trial.shape[2] % 512 == 0
        )
        if fits:
            return fused(tiles, trial, psi_v, psi_c, screened)
        return plain(trial, psi_v, psi_c, screened)

    in_specs = (
        P(None, ("tile", "vec"), None),
        P(None, "tile"),
        P(None, "vec", "tile"),
        P("tile", "vec"),
    )
    out_specs = P(None, ("tile", "vec"), None)
    return jax.shard_map(shards, mesh=mesh, in_specs=in_specs, out_specs=out_specs, check_vma=False)
```

```python
import functools

import jax
import jax.numpy as jnp
from jax import lax
from jax.experimental import pallas as pl
from jax.experimental.pallas import tpu as pltpu
from jax.sharding import PartitionSpec as P

CUTS = 4
SUBS = 2


def back_product(weighted_flat, panel):
    return lax.dot_general(
        weighted_flat, panel, (((1,), (1,)), ((), ())), preferred_element_type=jnp.float32
    )


def plain(trial, psi_v, psi_c, screened):
    count = trial.shape[0]
    points = psi_v.shape[1]
    conduct = trial.shape[2]
    whole = lax.all_gather(trial, ("tile", "vec"), axis=1, tiled=True)
    projected = jnp.einsum("vp,kvc->kpc", psi_v, whole, preferred_element_type=jnp.float32).astype(
        jnp.bfloat16
    )
    flat = projected.reshape(count * points, conduct)
    panel_local = psi_c[:, 0, :]
    panel = lax.all_gather(panel_local, "tile", axis=1, tiled=True)
    pair = jnp.dot(flat, panel, preferred_element_type=jnp.float32)
    weighted = (screened[None] * pair.reshape(count, points, -1)).astype(jnp.bfloat16)
    weighted_flat = weighted.reshape(count * points, -1)
    back = back_product(weighted_flat, panel)
    back = back.reshape(count, points, conduct)
    left = psi_v.astype(jnp.float32)
    summed = lax.psum(back, "vec")
    tiles = lax.axis_size("tile")
    halves = lax.axis_size("vec")
    owned = left.shape[0] // (tiles * halves)
    grouped = left.reshape(tiles, halves, owned, points)
    mine = lax.dynamic_index_in_dim(grouped, lax.axis_index("vec"), 1, keepdims=False).reshape(
        tiles * owned, points
    )
    pieces = []
    for one in range(count):
        term = jnp.dot(mine, summed[one], precision=lax.Precision.HIGHEST)
        pieces.append(lax.psum_scatter(term, "tile", scatter_dimension=0, tiled=True))
    return jnp.stack(pieces, axis=0)


def sources_of(layers):
    return [
        sorted((o for o in range(layers) if o != z), key=lambda o: (abs(o - z), o))
        for z in range(layers)
    ]


def pick(values, at):
    chosen = jnp.int32(values[0])
    for k, value in enumerate(values[1:], 1):
        chosen = jnp.where(at == k, jnp.int32(value), chosen)
    return chosen


def body(
    layers,
    trial_hbm,
    psi_v_hbm,
    psi_c_hbm,
    screened_hbm,
    out_hbm,
    result,
    whole,
    psi,
    psi_t,
    stage,
    screened_own,
    screened_out,
    screened_in,
    panel,
    flat,
    back,
    give,
    take,
    first_send,
    first_got,
    keep,
    leave,
    second_send,
    second_got,
    third,
    parts,
    local_sem,
    sends,
    trial_recv,
    hand_recv,
    psi_recv,
    screened_recv,
    block_recv,
    take_recv,
    first_recv,
    second_recv,
    parts_recv,
):
    bf16, f32 = jnp.bfloat16, jnp.float32
    me = lax.axis_index("tile")
    half = lax.axis_index("vec")
    other = 1 - half
    z, y, x = me // 4, (me // 2) % 2, me % 2
    across = lax.rem(y + 1, 2)
    aside = lax.rem(x + 1, 2)
    table = sources_of(layers)
    events = layers - 1
    source = [pick([row[e] for row in table], z) for e in range(events)]
    distance = [pick([abs(row[e] - k) for k, row in enumerate(table)], z) for e in range(events)]
    at_distance = [[distance[e] == k for k in range(layers)] for e in range(events)]

    def tile_of(zz, yy, xx):
        return zz * 4 + yy * 2 + xx

    mate_x, mate_y = tile_of(z, y, aside), tile_of(z, across, x)
    up, down = jnp.minimum(z + 1, layers - 1), jnp.maximum(z - 1, 0)
    has_up, has_down = z < layers - 1, z > 0
    on_up = [has_up & (source[e] < z) for e in range(events)]
    on_down = [has_down & (source[e] > z) for e in range(events)]

    def slot_of(zz, yy):
        return zz * 2 + yy

    slots = layers * 2
    order = [("own", 0)]
    for e in range(events):
        order += [("z", e), ("y", e - 1)]
    order += [("y", events - 1)]

    def slot_at(kind, e):
        zz = source[e] if e >= 0 and kind != "own" else z
        return slot_of(zz, across if kind == "y" else y)

    turns = [slot_at(*event) for event in order]

    rows, conduct = trial_hbm.shape
    width = psi_c_hbm.shape[1]
    points = psi_v_hbm.shape[-1]
    middle = conduct // 2
    part = middle // 2
    height = psi_c_hbm.shape[0] // CUTS

    def lines(tile, vec):
        start = pl.multiple_of((tile * 2 + vec) * rows, rows)
        return whole.at[pl.ds(start, rows), :]

    def columns(tile):
        return pl.ds(pl.multiple_of(tile * width, 128), width)

    local = []

    def load(src, dst):
        copy = pltpu.make_async_copy(src, dst, local_sem.at[len(local)])
        copy.start()
        local.append(copy)
        return copy

    load_rows = load(trial_hbm, lines(me, half))
    load_psi = load(psi_v_hbm, psi.at[0])
    load_block = load(psi_c_hbm, panel.at[slot_of(z, y)])

    def remote(src, dst, send, recv, tile, vec):
        return pltpu.make_async_remote_copy(
            src_ref=src,
            dst_ref=dst,
            send_sem=send,
            recv_sem=recv,
            device_id=(tile, vec),
            device_id_type=pl.DeviceIdType.MESH,
        )

    partners = [(mate_x, half), (mate_y, half), (me, other)]
    for d in range(1, layers):
        for v in range(2):
            partners.append((tile_of(lax.rem(z + d, layers), y, x), v))
    with jax.named_scope("pbar"):
        barrier = pltpu.get_barrier_semaphore()
        for partner in partners:
            pl.semaphore_signal(
                barrier, inc=1, device_id=partner, device_id_type=pl.DeviceIdType.MESH
            )
        pl.semaphore_wait(barrier, len(partners))

    pending = []

    def send(src, dst, recv, tile, vec, like, cond=None):
        i = len(pending)
        copy = remote(src, dst, sends.at[i], recv, tile, vec)
        pending.append((like, cond))
        if cond is None:
            copy.start()
        else:
            pl.when(cond)(copy.start)

    def got(ref, recv):
        remote(ref, ref, sends.at[0], recv, me, other).wait_recv()

    some_rows = whole.at[pl.ds(0, rows), :]

    def piece(ref, s):
        return ref.at[pl.ds(s * height, height), :]

    some_piece = piece(panel.at[0], 0)

    def hand(src, tile):
        send(src, lines(tile, half), hand_recv.at[tile], me, other, some_rows)

    def spread(tile, column):
        ref = lines(tile, half)
        recv = trial_recv.at[tile]
        if column:
            for e in range(events):
                send(ref, ref, recv, tile_of(source[e], y, x), half, some_rows)
        send(ref, ref, recv, mate_y, half, some_rows)
        hand(ref, tile)

    last = CUTS - 1
    home_slot, mate_slot = slot_of(z, y), slot_of(z, across)

    def along(src, slot, s, to_up, to_down):
        dst = piece(panel.at[slot], s)
        recv = block_recv.at[slot, s]
        send(src, dst, recv, tile_of(up, y, x), half, some_piece, to_up)
        send(src, dst, recv, tile_of(down, y, x), half, some_piece, to_down)

    def cross(src, slot, s):
        dst = piece(panel.at[slot], s)
        send(src, dst, block_recv.at[slot, s], mate_y, half, some_piece)

    def own_piece_z(s):
        along(piece(panel.at[home_slot], s), home_slot, s, has_up, has_down)

    def own_piece_y(s):
        cross(piece(panel.at[home_slot], s), home_slot, s)

    def came(slot, s):
        ref = piece(panel.at[slot], s)
        got(ref, block_recv.at[slot, s])
        return ref

    pair_layers = layers // 2

    def psi_half(ref, which):
        return ref.at[pl.ds(which * pair_layers, pair_layers)]

    def arrive(e):
        slot = slot_of(source[e], y)
        for s in range(CUTS):
            ref = came(slot, s)
            along(ref, slot, s, on_up[e], on_down[e])
            if s < last:
                cross(ref, slot, s)
        slot = slot_of(source[e], across)
        along(came(slot, last), slot, last, on_up[e], on_down[e])

    def arrive_if(e, k):
        start = len(pending)

        @pl.when(at_distance[e][k])
        def _():
            arrive(e)

        for i in range(start, len(pending)):
            pending[i] += (at_distance[e][k],)

    with jax.named_scope("ptrial"):
        ref = lines(me, half)
        load_rows.wait()
        send(ref, ref, trial_recv.at[me], mate_x, half, some_rows)
        spread(me, True)
        load_out = [
            load(screened_hbm.at[:, columns(turn * 2 + aside)], stage.at[i])
            for i, turn in enumerate(turns)
        ]
        load_own = [
            load(screened_hbm.at[:, columns(turn * 2 + x)], screened_own.at[i])
            for i, turn in enumerate(turns)
        ]
        load_psi.wait()
        send(
            psi_half(psi.at[0], half),
            psi_half(psi.at[1], half),
            psi_recv.at[0],
            mate_x,
            half,
            psi_half(psi.at[1], 0),
        )
        got(lines(mate_x, half), trial_recv.at[mate_x])
        spread(mate_x, True)
        load_block.wait()
        own_piece_y(last)

        for i in range(slots):
            load_out[i].wait()
            screened_out[i] = stage[i].astype(bf16)
        for i in range(slots):
            send(
                screened_out.at[i],
                screened_in.at[i],
                screened_recv.at[i],
                mate_x,
                half,
                screened_out.at[0],
            )

        for e in range(events):
            for xx in range(2):
                tile = tile_of(source[e], y, xx)
                got(lines(tile, half), trial_recv.at[tile])
                spread(tile, False)
            if e == max(events - 2, 0):
                for s in range(CUTS):
                    own_piece_z(s)
        for s in range(last):
            own_piece_y(s)

        back[...] = jnp.zeros_like(back)
        valence = layers * 4 * 2 * rows
        psi_t[0] = psi[0].reshape(valence, points).T

        for e in range(-1, events):
            for xx in range(2):
                tile = tile_of(source[e] if e >= 0 else z, across, xx)
                ref = lines(tile, half)
                got(ref, trial_recv.at[tile])
                hand(ref, tile)

        ref = psi_half(psi.at[1], half)
        got(ref, psi_recv.at[0])
        send(ref, ref, psi_recv.at[1], me, other, psi_half(psi.at[1], 0))
        along(came(mate_slot, last), mate_slot, last, has_up, has_down)
        for e in range(events):
            arrive_if(e, 1)
        for tile in range(layers * 4):
            got(lines(tile, other), hand_recv.at[tile])

    wide = 256

    def project(p):
        def chunk(j, carry):
            cols = pl.ds(pl.multiple_of(j * wide, wide), wide)
            flat[p, :, cols] = jnp.dot(
                psi_t[p], whole[:, cols], preferred_element_type=f32
            ).astype(bf16)
            return carry

        lax.fori_loop(0, conduct // wide, chunk, 0)

    with jax.named_scope("pproj"):
        project(0)
        got(psi_half(psi.at[1], other), psi_recv.at[1])
        psi_t[1] = psi[1].reshape(valence, points).T
        project(1)

    def receive(i):
        kind, e = order[i]
        if kind == "z" and e > 0:
            for late in range(e, events):
                arrive_if(late, e + 1)
        if kind == "y":
            for s in range(last):
                came(turns[i], s)
        load_own[i].wait()

    def step(p, share, slot):
        block = panel.at[slot]
        pair = jnp.dot(flat[p], block[...], preferred_element_type=f32)
        weighted = (share.astype(f32) * pair).astype(bf16)
        for h in range(2):
            back[p, h] += back_product(weighted, block[pl.ds(h * middle, middle), :])

    def use(k, carry):
        slot = turns[0]
        for i in range(final):
            slot = jnp.where(k == i, turns[i], slot)

            @pl.when(k == i)
            def _(i=i):
                receive(i)

        step(0, screened_own[k], slot)
        got(screened_in.at[k], screened_recv.at[k])
        step(1, screened_in[k], slot)
        return carry

    final = slots - 1
    with jax.named_scope("puse"):
        lax.fori_loop(0, final, use, 0)
        receive(final)
        step(0, screened_own[final], turns[final])

    def span(kind):
        return pl.ds(kind * part, part)

    def swap(p):
        for kind in range(2):
            give[kind, p] = back[p, other, :, span(kind)].astype(bf16)
            send(
                give.at[kind, p],
                take.at[kind, p],
                take_recv.at[kind, p],
                me,
                other,
                give.at[0, 0],
            )

    def split(kind, p):
        got(take.at[kind, p], take_recv.at[kind, p])
        total = back[p, half, :, span(kind)] + take[kind, p].astype(f32)
        high = total.astype(bf16)
        flat[p, :, span(kind)] = high
        low = (total - high.astype(f32)).astype(bf16)
        flat[p, :, pl.ds(middle + kind * part, part)] = low

    share = layers // SUBS
    block_rows = 2 * rows

    def product(p, kind, at, sub):
        if kind == 0:
            left = psi[p, pl.ds(sub * share, share), :, pl.ds(at, 1)]
        else:
            left = psi[p, pl.ds(sub * share, share), pl.ds(at, 1)]
        left = left.reshape(share * 2 * block_rows, points)
        total = None
        for level in range(2):
            cols = pl.ds(level * middle + kind * part, part)
            value = jnp.dot(left, flat[p, :, cols], preferred_element_type=f32)
            total = value if total is None else total + value
        return total.reshape(share, 2, block_rows, part)

    settled = [0]

    def settle(upto):
        for i in range(settled[0], upto):
            like, *conds = pending[i]
            wait = remote(like, like, sends.at[i], parts_recv.at[0, 0, 0], me, other).wait_send
            conds = [cond for cond in conds if cond is not None]
            if conds:
                pl.when(functools.reduce(jnp.logical_and, conds))(wait)
            else:
                wait()
        settled[0] = upto

    mates = [mate_x, mate_y]
    homes, aways = [x, y], [aside, across]
    with jax.named_scope("pearly"):
        swap(0)
        for kind in range(2):
            split(kind, 0)
        for sub in range(SUBS):
            for kind in range(2):
                keep[kind, sub] = product(0, kind, homes[kind], sub)
                leave[kind, sub] = product(0, kind, aways[kind], sub)

    with jax.named_scope("plast"):
        got(screened_in.at[final], screened_recv.at[final])
        step(1, screened_in[final], turns[final])

    earlier = len(pending)
    with jax.named_scope("pfin"):
        swap(1)
        for sub in range(SUBS):
            for kind in range(2):
                if sub == 0:
                    split(kind, 1)
                value = leave[kind, sub] + product(1, kind, aways[kind], sub)
                first_send[kind, sub] = value.astype(bf16)
                send(
                    first_send.at[kind, sub],
                    first_got.at[kind, sub],
                    first_recv.at[kind, sub],
                    mates[kind],
                    half,
                    first_send.at[0, 0],
                )
        for sub in range(SUBS):
            for kind in range(2):
                keep[kind, sub] += product(1, kind, homes[kind], sub)

    with jax.named_scope("psettle"):
        settle(earlier)

    with jax.named_scope("psecond"):
        for sub in range(SUBS):
            for kind in range(2):
                got(first_got.at[kind, sub], first_recv.at[kind, sub])
                away, home = [(across, y), (aside, x)][kind]

                def summed(at, kind=kind, sub=sub):
                    mine = keep[kind, sub, :, pl.ds(at, 1)]
                    theirs = first_got[kind, sub, :, pl.ds(at, 1)].astype(f32)
                    return (mine + theirs).reshape(share, block_rows, part)

                second_send[kind, sub] = summed(away).astype(bf16)
                send(
                    second_send.at[kind, sub],
                    second_got.at[kind, sub],
                    second_recv.at[kind, sub],
                    mates[1 - kind],
                    half,
                    second_send.at[0, 0],
                )
                keep[kind, sub, :, pl.ds(home, 1)] = summed(home).reshape(
                    share, 1, block_rows, part
                )

    with jax.named_scope("pthird"):
        for sub in range(SUBS):
            for kind in range(2):
                got(second_got.at[kind, sub], second_recv.at[kind, sub])
                home = [y, x][kind]
                mine = keep[kind, sub, :, pl.ds(home, 1)].reshape(share, block_rows, part)
                value = mine + second_got[kind, sub].astype(f32)
                keep[kind, sub, :, pl.ds(home, 1)] = value.reshape(share, 1, block_rows, part)
                third[kind, sub] = value.astype(bf16)
                for i in range(share):
                    zz = sub * share + i
                    for v in range(2):
                        send(
                            third.at[kind, sub, i, pl.ds(v * rows, rows)],
                            parts.at[z, half, kind],
                            parts_recv.at[z, half, kind],
                            tile_of(zz, y, x),
                            v,
                            parts.at[0, 0, 0],
                            (z != zz) | (half != v),
                        )

    with jax.named_scope("psum"):
        for flip in range(2):
            vec = lax.rem(half + flip, 2)
            for kind in range(2):
                value = None
                if flip == 0:
                    home = [y, x][kind]
                    value = keep[
                        kind, z // share, lax.rem(z, share), home, pl.ds(half * rows, rows)
                    ]
                for d in range(layers):
                    if flip == 0 and d == 0:
                        continue
                    zz = lax.rem(z + d, layers)
                    got(parts.at[zz, vec, kind], parts_recv.at[zz, vec, kind])
                    more = parts[zz, vec, kind].astype(f32)
                    value = more if value is None else value + more
                block = pl.ds(pl.multiple_of(vec * middle + kind * part, 128), part)
                result[:, block] = value
                load(result.at[:, block], out_hbm.at[:, block])

    assert len(pending) <= sends.shape[0]
    settle(len(pending))
    for copy in local[-4:]:
        copy.wait()


def sends_of(layers):
    events = layers - 1
    slots = layers * 2
    count = 1 + 2 * (events + 2) + 1 + 3 * CUTS + slots
    count += events * 4 + layers * 2 + 1
    count += 2 + (3 * CUTS + 2) * sum(events - e for e in range(events))
    return count + 4 + 2 * SUBS * 2 + 2 * layers * 2


def fused(tiles, trial, psi_v, psi_c, screened):
    rows, conduct = trial.shape[1:]
    valence, points = psi_v.shape
    width = psi_c.shape[2]
    middle = conduct // 2
    part = middle // 2
    layers = tiles // 4
    slots = layers * 2
    share = layers // SUBS
    bf16, f32 = jnp.bfloat16, jnp.float32
    far = pl.BlockSpec(memory_space=pl.ANY)
    dma = pltpu.SemaphoreType.DMA
    vmem = pltpu.VMEM
    out = pl.pallas_call(
        functools.partial(body, layers),
        out_shape=jax.ShapeDtypeStruct((rows, conduct), f32),
        in_specs=[far] * 4,
        out_specs=far,
        scratch_shapes=[
            vmem((rows, conduct), f32),
            vmem((valence, conduct), bf16),
            vmem((2, layers, 2, 2, 2 * rows, points), bf16),
            vmem((2, points, valence), bf16),
            vmem((slots, points, width), f32),
            vmem((slots, points, width), f32),
            vmem((slots, points, width), bf16),
            vmem((slots, points, width), bf16),
            vmem((slots, conduct, width), bf16),
            vmem((2, points, conduct), bf16),
            vmem((2, 2, points, middle), f32),
            vmem((2, 2, points, part), bf16),
            vmem((2, 2, points, part), bf16),
            vmem((2, SUBS, share, 2, 2 * rows, part), bf16),
            vmem((2, SUBS, share, 2, 2 * rows, part), bf16),
            vmem((2, SUBS, share, 2, 2 * rows, part), f32),
            vmem((2, SUBS, share, 2, 2 * rows, part), f32),
            vmem((2, SUBS, share, 2 * rows, part), bf16),
            vmem((2, SUBS, share, 2 * rows, part), bf16),
            vmem((2, SUBS, share, 2 * rows, part), bf16),
            vmem((layers, 2, 2, rows, part), bf16),
            dma((3 + 2 * slots + 4,)),
            dma((sends_of(layers),)),
            dma((tiles,)),
            dma((tiles,)),
            dma((2,)),
            dma((slots,)),
            dma((slots, CUTS)),
            dma((2, 2)),
            dma((2, SUBS)),
            dma((2, SUBS)),
            dma((layers, 2, 2)),
        ],
        compiler_params=pltpu.CompilerParams(
            collective_id=0, has_side_effects=True, vmem_limit_bytes=58 * 1024 * 1024
        ),
    )(
        trial[0],
        psi_v.reshape(layers, 2, 2, 2 * rows, points),
        psi_c[:, 0, :],
        screened,
    )
    return out[None]


def solution(mesh):
    tiles = mesh.shape["tile"]

    def shards(trial, psi_v, psi_c, screened):
        fits = (
            trial.shape[0] == 1
            and mesh.shape["vec"] == 2
            and tiles % (4 * SUBS) == 0
            and psi_v.shape[1] % 128 == 0
            and psi_c.shape[2] % 128 == 0
            and trial.shape[1] % 16 == 0
            and trial.shape[2] % 512 == 0
        )
        if fits:
            return fused(tiles, trial, psi_v, psi_c, screened)
        return plain(trial, psi_v, psi_c, screened)

    in_specs = (
        P(None, ("tile", "vec"), None),
        P(None, "tile"),
        P(None, "vec", "tile"),
        P("tile", "vec"),
    )
    out_specs = P(None, ("tile", "vec"), None)
    return jax.shard_map(shards, mesh=mesh, in_specs=in_specs, out_specs=out_specs, check_vma=False)
```

```python
import functools

import jax
import jax.numpy as jnp
from jax import lax
from jax.experimental import pallas as pl
from jax.experimental.pallas import tpu as pltpu
from jax.sharding import PartitionSpec as P

CUTS = 4
SUBS = 2
ROWS, ACROSS, LAYERS, SHARE, POINTS, GIVE, FIRST, SECOND, THIRD = range(9)


def back_product(weighted_flat, panel):
    return lax.dot_general(
        weighted_flat, panel, (((1,), (1,)), ((), ())), preferred_element_type=jnp.float32
    )


def plain(trial, psi_v, psi_c, screened):
    count = trial.shape[0]
    points = psi_v.shape[1]
    conduct = trial.shape[2]
    whole = lax.all_gather(trial, ("tile", "vec"), axis=1, tiled=True)
    projected = jnp.einsum("vp,kvc->kpc", psi_v, whole, preferred_element_type=jnp.float32).astype(
        jnp.bfloat16
    )
    flat = projected.reshape(count * points, conduct)
    panel_local = psi_c[:, 0, :]
    panel = lax.all_gather(panel_local, "tile", axis=1, tiled=True)
    pair = jnp.dot(flat, panel, preferred_element_type=jnp.float32)
    weighted = (screened[None] * pair.reshape(count, points, -1)).astype(jnp.bfloat16)
    weighted_flat = weighted.reshape(count * points, -1)
    back = back_product(weighted_flat, panel)
    back = back.reshape(count, points, conduct)
    left = psi_v.astype(jnp.float32)
    summed = lax.psum(back, "vec")
    tiles = lax.axis_size("tile")
    halves = lax.axis_size("vec")
    owned = left.shape[0] // (tiles * halves)
    grouped = left.reshape(tiles, halves, owned, points)
    mine = lax.dynamic_index_in_dim(grouped, lax.axis_index("vec"), 1, keepdims=False).reshape(
        tiles * owned, points
    )
    pieces = []
    for one in range(count):
        term = jnp.dot(mine, summed[one], precision=lax.Precision.HIGHEST)
        pieces.append(lax.psum_scatter(term, "tile", scatter_dimension=0, tiled=True))
    return jnp.stack(pieces, axis=0)


def sources_of(layers):
    return [
        sorted((o for o in range(layers) if o != z), key=lambda o: (abs(o - z), o))
        for z in range(layers)
    ]


def pick(values, at):
    chosen = jnp.int32(values[0])
    for k, value in enumerate(values[1:], 1):
        chosen = jnp.where(at == k, jnp.int32(value), chosen)
    return chosen


def body(
    layers,
    trial_hbm,
    psi_v_hbm,
    psi_c_hbm,
    screened_hbm,
    result,
    whole,
    psi,
    psi_t,
    stage,
    screened_own,
    screened_out,
    screened_in,
    panel,
    flat,
    back,
    give,
    take,
    first_send,
    first_got,
    keep,
    leave,
    second_send,
    second_got,
    third,
    parts,
    local_sem,
    sends,
    trial_recv,
    hand_recv,
    psi_recv,
    screened_recv,
    block_recv,
    take_recv,
    first_recv,
    second_recv,
    parts_recv,
):
    bf16, f32 = jnp.bfloat16, jnp.float32
    me = lax.axis_index("tile")
    half = lax.axis_index("vec")
    other = 1 - half
    z, y, x = me // 4, (me // 2) % 2, me % 2
    across = lax.rem(y + 1, 2)
    aside = lax.rem(x + 1, 2)
    table = sources_of(layers)
    events = layers - 1
    source = [pick([row[e] for row in table], z) for e in range(events)]
    distance = [pick([abs(row[e] - k) for k, row in enumerate(table)], z) for e in range(events)]
    at_distance = [[distance[e] == k for k in range(layers)] for e in range(events)]

    def tile_of(zz, yy, xx):
        return zz * 4 + yy * 2 + xx

    mate_x, mate_y = tile_of(z, y, aside), tile_of(z, across, x)
    up, down = jnp.minimum(z + 1, layers - 1), jnp.maximum(z - 1, 0)
    has_up, has_down = z < layers - 1, z > 0
    on_up = [has_up & (source[e] < z) for e in range(events)]
    on_down = [has_down & (source[e] > z) for e in range(events)]

    def slot_of(zz, yy):
        return zz * 2 + yy

    slots = layers * 2
    order = [("own", 0)]
    for e in range(events - 1):
        order += [("z", e), ("y", e - 1)]
    order += [("y", events - 2), ("z", events - 1), ("y", events - 1)]

    def slot_at(kind, e):
        zz = source[e] if e >= 0 and kind != "own" else z
        return slot_of(zz, across if kind == "y" else y)

    turns = [slot_at(*event) for event in order]

    rows, conduct = trial_hbm.shape
    width = psi_c_hbm.shape[1]
    points = psi_v_hbm.shape[-1]
    middle = conduct // 2
    part = middle // 2
    height = psi_c_hbm.shape[0] // CUTS

    def lines(tile, vec):
        start = pl.multiple_of((tile * 2 + vec) * rows, rows)
        return whole.at[pl.ds(start, rows), :]

    def columns(tile):
        return pl.ds(pl.multiple_of(tile * width, 128), width)

    def load(src, dst, sem):
        copy = pltpu.make_async_copy(src, dst, local_sem.at[sem])
        copy.start()
        return copy

    home_slot, mate_slot = slot_of(z, y), slot_of(z, across)

    def block_of(slot):
        return panel.at[pl.ds(pl.multiple_of(slot * conduct, conduct), conduct), :]

    load_rows = load(trial_hbm, lines(me, half), 0)
    load_psi = load(psi_v_hbm, psi.at[0], 1)
    load_block = load(psi_c_hbm, block_of(home_slot), 2)

    def remote(src, dst, send, recv, tile, vec):
        return pltpu.make_async_remote_copy(
            src_ref=src,
            dst_ref=dst,
            send_sem=send,
            recv_sem=recv,
            device_id=(tile, vec),
            device_id_type=pl.DeviceIdType.MESH,
        )

    partners = [(mate_x, half), (mate_y, half), (me, other)]
    for d in range(1, layers):
        for v in range(2):
            partners.append((tile_of(lax.rem(z + d, layers), y, x), v))
    with jax.named_scope("pbar"):
        barrier = pltpu.get_barrier_semaphore()
        for partner in partners:
            pl.semaphore_signal(
                barrier, inc=1, device_id=partner, device_id_type=pl.DeviceIdType.MESH
            )
        pl.semaphore_wait(barrier, len(partners))

    def send(src, dst, group, recv, tile, vec, cond=None):
        copy = remote(src, dst, sends.at[group], recv, tile, vec)
        if cond is None:
            copy.start()
        else:
            pl.when(cond)(copy.start)

    def sent(ref, group):
        remote(ref, ref, sends.at[group], psi_recv.at[0], me, other).wait_send()

    def got(ref, recv):
        remote(ref, ref, sends.at[0], recv, me, other).wait_recv()

    def piece(slot, s):
        start = pl.multiple_of(slot * conduct + s * height, height)
        return panel.at[pl.ds(start, height), :]

    def hand(tile):
        ref = lines(tile, half)
        send(ref, ref, ROWS, hand_recv.at[0], me, other)

    def spread(tile, column):
        ref = lines(tile, half)
        recv = trial_recv.at[tile]
        if column:
            for e in range(events):
                send(ref, ref, ROWS, recv, tile_of(source[e], y, x), half)
        send(ref, ref, ROWS, recv, mate_y, half)
        hand(tile)

    last = CUTS - 1

    def along(slot, s, to_up, to_down):
        ref = piece(slot, s)
        recv = block_recv.at[slot, s]
        send(ref, ref, LAYERS, recv, tile_of(up, y, x), half, to_up)
        send(ref, ref, LAYERS, recv, tile_of(down, y, x), half, to_down)

    def cross(slot, s):
        ref = piece(slot, s)
        send(ref, ref, ACROSS, block_recv.at[slot, s], mate_y, half)

    def came(slot, s):
        got(piece(slot, s), block_recv.at[slot, s])

    pair_layers = layers // 2

    def psi_half(ref, which):
        return ref.at[pl.ds(which * pair_layers, pair_layers)]

    def take_piece(e, s):
        slot = slot_of(source[e], y)
        came(slot, s)
        along(slot, s, on_up[e], on_down[e])
        if s < last:
            cross(slot, s)

    def take_mate(e):
        slot = slot_of(source[e], across)
        came(slot, last)
        along(slot, last, on_up[e], on_down[e])

    def at_k(k):
        return [e for e in range(events) if any(abs(row[e] - r) == k for r, row in enumerate(table))]

    def arrive(k, first, final):
        for s in range(first, final):
            for e in at_k(k):
                pl.when(at_distance[e][k])(functools.partial(take_piece, e, s))
        if final == CUTS:
            for e in at_k(k):
                pl.when(at_distance[e][k])(functools.partial(take_mate, e))

    with jax.named_scope("ptrial"):
        ref = lines(me, half)
        load_rows.wait()
        send(ref, ref, ROWS, trial_recv.at[me], mate_x, half)
        spread(me, True)
        for i, turn in enumerate(turns):
            load(screened_hbm.at[:, columns(turn * 2 + aside)], stage.at[i], 3)
        for i, turn in enumerate(turns):
            load(screened_hbm.at[:, columns(turn * 2 + x)], screened_own.at[i], 4)
        load_psi.wait()
        ref = psi_half(psi.at[0], half)
        send(ref, psi_half(psi.at[1], half), POINTS, psi_recv.at[0], mate_x, half)
        got(lines(mate_x, half), trial_recv.at[mate_x])
        spread(mate_x, True)
        load_block.wait()
        cross(home_slot, last)

        pltpu.make_async_copy(stage, stage, local_sem.at[3]).wait()
        for i in range(slots):
            screened_out[i] = stage[i].astype(bf16)
        for i in range(slots):
            send(screened_out.at[i], screened_in.at[i], SHARE, screened_recv.at[i], mate_x, half)

        for e in range(events):
            for xx in range(2):
                tile = tile_of(source[e], y, xx)
                got(lines(tile, half), trial_recv.at[tile])
                spread(tile, False)
            if e == max(events - 2, 0):
                for s in range(CUTS):
                    along(home_slot, s, has_up, has_down)
        for s in range(last):
            cross(home_slot, s)

        back[...] = jnp.zeros_like(back)
        valence = layers * 4 * 2 * rows
        psi_t[0] = psi[0].reshape(valence, points).T

        for e in range(-1, events):
            for xx in range(2):
                tile = tile_of(source[e] if e >= 0 else z, across, xx)
                got(lines(tile, half), trial_recv.at[tile])
                hand(tile)

        ref = psi_half(psi.at[1], half)
        got(ref, psi_recv.at[0])
        send(ref, ref, POINTS, psi_recv.at[1], me, other)
        came(mate_slot, last)
        along(mate_slot, last, has_up, has_down)
        arrive(1, 0, CUTS)
        got(whole.at[pl.ds(0, layers * 4 * rows), :], hand_recv.at[0])

    wide = 256

    def project(p):
        def chunk(j, carry):
            cols = pl.ds(pl.multiple_of(j * wide, wide), wide)
            flat[p, :, cols] = jnp.dot(
                psi_t[p], whole[:, cols], preferred_element_type=f32
            ).astype(bf16)
            return carry

        lax.fori_loop(0, conduct // wide, chunk, 0)

    with jax.named_scope("pproj"):
        project(0)
        got(psi_half(psi.at[1], other), psi_recv.at[1])
        psi_t[1] = psi[1].reshape(valence, points).T
        project(1)

    farthest = layers - 1

    def receive(i):
        kind, e = order[i]
        if kind == "z" and e > 0:
            arrive(e + 1, last if e + 1 == farthest else 0, CUTS)
        if kind == "y":
            for s in range(last):
                came(turns[i], s)

    def between(i):
        if i + 1 < slots and order[i + 1] == ("z", farthest - 1) and farthest > 1:
            arrive(farthest, 0, last)

    def step(p, share, slot):
        block = block_of(slot)
        pair = jnp.dot(flat[p], block[...], preferred_element_type=f32)
        weighted = (share.astype(f32) * pair).astype(bf16)
        for h in range(2):
            back[p, h] += back_product(weighted, block[pl.ds(h * middle, middle), :])

    pltpu.make_async_copy(screened_own, screened_own, local_sem.at[4]).wait()

    def use(k, carry):
        slot = turns[0]
        for i in range(final):
            slot = jnp.where(k == i, turns[i], slot)
            pl.when(k == i)(functools.partial(receive, i))
        step(0, screened_own[k], slot)
        for i in range(final):
            pl.when(k == i)(functools.partial(between, i))
        got(screened_in.at[k], screened_recv.at[k])
        step(1, screened_in[k], slot)
        return carry

    final = slots - 1
    with jax.named_scope("puse"):
        lax.fori_loop(0, final, use, 0)
        receive(final)
        step(0, screened_own[final], turns[final])

    def span(kind):
        return pl.ds(kind * part, part)

    def swap(p):
        for kind in range(2):
            give[kind, p] = back[p, other, :, span(kind)].astype(bf16)
            send(give.at[kind, p], take.at[kind, p], GIVE, take_recv.at[kind, p], me, other)

    def split(kind, p):
        got(take.at[kind, p], take_recv.at[kind, p])
        total = back[p, half, :, span(kind)] + take[kind, p].astype(f32)
        high = total.astype(bf16)
        flat[p, :, span(kind)] = high
        low = (total - high.astype(f32)).astype(bf16)
        flat[p, :, pl.ds(middle + kind * part, part)] = low

    share = layers // SUBS
    block_rows = 2 * rows

    def product(p, kind, at, sub):
        if kind == 0:
            left = psi[p, pl.ds(sub * share, share), :, pl.ds(at, 1)]
        else:
            left = psi[p, pl.ds(sub * share, share), pl.ds(at, 1)]
        left = left.reshape(share * 2 * block_rows, points)
        total = None
        for level in range(2):
            cols = pl.ds(level * middle + kind * part, part)
            value = jnp.dot(left, flat[p, :, cols], preferred_element_type=f32)
            total = value if total is None else total + value
        return total.reshape(share, 2, block_rows, part)

    mates = [mate_x, mate_y]
    homes, aways = [x, y], [aside, across]
    with jax.named_scope("plast"):
        swap(0)
        got(screened_in.at[final], screened_recv.at[final])
        step(1, screened_in[final], turns[final])
        swap(1)

    with jax.named_scope("pearly"):
        for kind in range(2):
            split(kind, 0)
        for sub in range(SUBS):
            for kind in range(2):
                leave[kind, sub] = product(0, kind, aways[kind], sub)

    with jax.named_scope("pfin"):
        for sub in range(SUBS):
            for kind in range(2):
                if sub == 0:
                    split(kind, 1)
                value = leave[kind, sub] + product(1, kind, aways[kind], sub)
                first_send[kind, sub] = value.astype(bf16)
                send(
                    first_send.at[kind, sub],
                    first_got.at[kind, sub],
                    FIRST,
                    first_recv.at[kind, sub],
                    mates[kind],
                    half,
                )
        for sub in range(SUBS):
            for kind in range(2):
                home = homes[kind]
                value = product(0, kind, home, sub) + product(1, kind, home, sub)
                keep[kind, sub] = value

    with jax.named_scope("psecond"):
        for sub in range(SUBS):
            for kind in range(2):
                got(first_got.at[kind, sub], first_recv.at[kind, sub])
                away, home = [(across, y), (aside, x)][kind]

                def summed(at, kind=kind, sub=sub):
                    mine = keep[kind, sub, :, pl.ds(at, 1)]
                    theirs = first_got[kind, sub, :, pl.ds(at, 1)].astype(f32)
                    return (mine + theirs).reshape(share, block_rows, part)

                second_send[kind, sub] = summed(away).astype(bf16)
                send(
                    second_send.at[kind, sub],
                    second_got.at[kind, sub],
                    SECOND,
                    second_recv.at[kind, sub],
                    mates[1 - kind],
                    half,
                )
                keep[kind, sub, :, pl.ds(home, 1)] = summed(home).reshape(
                    share, 1, block_rows, part
                )

    with jax.named_scope("pthird"):
        for sub in range(SUBS):
            for kind in range(2):
                got(second_got.at[kind, sub], second_recv.at[kind, sub])
                home = [y, x][kind]
                mine = keep[kind, sub, :, pl.ds(home, 1)].reshape(share, block_rows, part)
                value = mine + second_got[kind, sub].astype(f32)
                keep[kind, sub, :, pl.ds(home, 1)] = value.reshape(share, 1, block_rows, part)
                third[kind, sub] = value.astype(bf16)
                for i in range(share):
                    zz = sub * share + i
                    for v in range(2):
                        send(
                            third.at[kind, sub, i, pl.ds(v * rows, rows)],
                            parts.at[half, kind, z],
                            THIRD,
                            parts_recv.at[half, kind],
                            tile_of(zz, y, x),
                            v,
                            (z != zz) | (half != v),
                        )

    with jax.named_scope("psum"):
        for flip in range(2):
            vec = lax.rem(half + flip, 2)
            for kind in range(2):
                value = None
                if flip == 0:
                    home = [y, x][kind]
                    value = keep[
                        kind, z // share, lax.rem(z, share), home, pl.ds(half * rows, rows)
                    ]
                count = layers - 1 + flip
                got(parts.at[vec, kind, pl.ds(0, count)], parts_recv.at[vec, kind])
                for d in range(1 - flip, layers):
                    more = parts[vec, kind, lax.rem(z + d, layers)].astype(f32)
                    value = more if value is None else value + more
                block = pl.ds(pl.multiple_of(vec * middle + kind * part, 128), part)
                result[:, block] = value

    def rows_as(count):
        return whole.at[pl.ds(0, count), :]

    def pieces_as(count):
        return panel.at[pl.ds(0, count * height), :]

    with jax.named_scope("pend"):
        sent(rows_as((8 * layers - 1) * rows), ROWS)
        sent(pieces_as(CUTS + events * last), ACROSS)
        for k in range(layers):
            ends = (k == 0) + (k == layers - 1)
            onward = sum((o < k < layers - 1) or (0 < k < o) for o in table[k])
            count = (2 - ends + onward) * (CUTS + 1)
            pl.when(z == k)(functools.partial(sent, pieces_as(count), LAYERS))
        sent(screened_out, SHARE)
        sent(psi.at[1], POINTS)
        sent(give, GIVE)
        sent(first_send, FIRST)
        sent(second_send, SECOND)
        sent(rows_as(2 * (2 * layers - 1) * rows * part // conduct), THIRD)


def write_out(result, out_hbm, sem):
    copy = pltpu.make_async_copy(result, out_hbm, sem)
    copy.start()
    copy.wait()


def fused(tiles, trial, psi_v, psi_c, screened):
    rows, conduct = trial.shape[1:]
    valence, points = psi_v.shape
    width = psi_c.shape[2]
    middle = conduct // 2
    part = middle // 2
    layers = tiles // 4
    slots = layers * 2
    share = layers // SUBS
    bf16, f32 = jnp.bfloat16, jnp.float32
    far = pl.BlockSpec(memory_space=pl.ANY)
    dma = pltpu.SemaphoreType.DMA
    vmem = pltpu.VMEM
    out = pl.pallas_call(
        functools.partial(body, layers),
        out_shape=vmem((rows, conduct), f32),
        in_specs=[far] * 4,
        out_specs=pl.BlockSpec(memory_space=vmem),
        scratch_shapes=[
            vmem((valence, conduct), bf16),
            vmem((2, layers, 2, 2, 2 * rows, points), bf16),
            vmem((2, points, valence), bf16),
            vmem((slots, points, width), f32),
            vmem((slots, points, width), f32),
            vmem((slots, points, width), bf16),
            vmem((slots, points, width), bf16),
            vmem((slots * conduct, width), bf16),
            vmem((2, points, conduct), bf16),
            vmem((2, 2, points, middle), f32),
            vmem((2, 2, points, part), bf16),
            vmem((2, 2, points, part), bf16),
            vmem((2, SUBS, share, 2, 2 * rows, part), bf16),
            vmem((2, SUBS, share, 2, 2 * rows, part), bf16),
            vmem((2, SUBS, share, 2, 2 * rows, part), f32),
            vmem((2, SUBS, share, 2, 2 * rows, part), f32),
            vmem((2, SUBS, share, 2 * rows, part), bf16),
            vmem((2, SUBS, share, 2 * rows, part), bf16),
            vmem((2, SUBS, share, 2 * rows, part), bf16),
            vmem((2, 2, layers, rows, part), bf16),
            dma((5,)),
            dma((9,)),
            dma((tiles,)),
            dma((1,)),
            dma((2,)),
            dma((slots,)),
            dma((slots, CUTS)),
            dma((2, 2)),
            dma((2, SUBS)),
            dma((2, SUBS)),
            dma((2, 2)),
        ],
        compiler_params=pltpu.CompilerParams(
            collective_id=0, has_side_effects=True, vmem_limit_bytes=58 * 1024 * 1024
        ),
    )(
        trial[0],
        psi_v.reshape(layers, 2, 2, 2 * rows, points),
        psi_c[:, 0, :],
        screened,
    )
    out = pl.pallas_call(
        write_out,
        out_shape=jax.ShapeDtypeStruct((rows, conduct), f32),
        in_specs=[pl.BlockSpec(memory_space=vmem)],
        out_specs=far,
        scratch_shapes=[dma(())],
        compiler_params=pltpu.CompilerParams(vmem_limit_bytes=1024 * 1024),
    )(out)
    return out[None]


def solution(mesh):
    tiles = mesh.shape["tile"]

    def shards(trial, psi_v, psi_c, screened):
        fits = (
            trial.shape[0] == 1
            and mesh.shape["vec"] == 2
            and tiles % (4 * SUBS) == 0
            and psi_v.shape[1] % 128 == 0
            and psi_c.shape[2] % 128 == 0
            and trial.shape[1] % 16 == 0
            and trial.shape[2] % 512 == 0
        )
        if fits:
            return fused(tiles, trial, psi_v, psi_c, screened)
        return plain(trial, psi_v, psi_c, screened)

    in_specs = (
        P(None, ("tile", "vec"), None),
        P(None, "tile"),
        P(None, "vec", "tile"),
        P("tile", "vec"),
    )
    out_specs = P(None, ("tile", "vec"), None)
    return jax.shard_map(shards, mesh=mesh, in_specs=in_specs, out_specs=out_specs, check_vma=False)
```

```python
import functools

import jax
import jax.numpy as jnp
from jax import lax
from jax.experimental import pallas as pl
from jax.experimental.pallas import tpu as pltpu
from jax.sharding import PartitionSpec as P

CUTS = 4
AHEAD = 2
ROWS, ACROSS, LAYERS, SHARE, POINTS, GIVE, FIRST, SECOND, THIRD = range(9)


def back_product(weighted_flat, panel):
    return lax.dot_general(
        weighted_flat, panel, (((1,), (1,)), ((), ())), preferred_element_type=jnp.float32
    )


def plain(trial, psi_v, psi_c, screened):
    count = trial.shape[0]
    points = psi_v.shape[1]
    conduct = trial.shape[2]
    whole = lax.all_gather(trial, ("tile", "vec"), axis=1, tiled=True)
    projected = jnp.einsum("vp,kvc->kpc", psi_v, whole, preferred_element_type=jnp.float32).astype(
        jnp.bfloat16
    )
    flat = projected.reshape(count * points, conduct)
    panel_local = psi_c[:, 0, :]
    panel = lax.all_gather(panel_local, "tile", axis=1, tiled=True)
    pair = jnp.dot(flat, panel, preferred_element_type=jnp.float32)
    weighted = (screened[None] * pair.reshape(count, points, -1)).astype(jnp.bfloat16)
    weighted_flat = weighted.reshape(count * points, -1)
    back = back_product(weighted_flat, panel)
    back = back.reshape(count, points, conduct)
    left = psi_v.astype(jnp.float32)
    summed = lax.psum(back, "vec")
    tiles = lax.axis_size("tile")
    halves = lax.axis_size("vec")
    owned = left.shape[0] // (tiles * halves)
    grouped = left.reshape(tiles, halves, owned, points)
    mine = lax.dynamic_index_in_dim(grouped, lax.axis_index("vec"), 1, keepdims=False).reshape(
        tiles * owned, points
    )
    pieces = []
    for one in range(count):
        term = jnp.dot(mine, summed[one], precision=lax.Precision.HIGHEST)
        pieces.append(lax.psum_scatter(term, "tile", scatter_dimension=0, tiled=True))
    return jnp.stack(pieces, axis=0)


def sources_of(layers):
    return [
        sorted((o for o in range(layers) if o != z), key=lambda o: (abs(o - z), o))
        for z in range(layers)
    ]


def outer_first(layers):
    return sorted(range(layers), key=lambda k: (-abs(2 * k - layers + 1), k))


def pick(values, at):
    chosen = jnp.int32(values[0])
    for k, value in enumerate(values[1:], 1):
        chosen = jnp.where(at == k, jnp.int32(value), chosen)
    return chosen


def body(
    layers,
    trial_hbm,
    psi_v_hbm,
    psi_c_hbm,
    screened_hbm,
    result,
    whole,
    psi,
    psi_t,
    stage,
    screened_own,
    screened_out,
    screened_in,
    panel,
    flat,
    back,
    give,
    take,
    first_send,
    first_got,
    keep,
    second_send,
    second_got,
    third,
    parts,
    local_sem,
    sends,
    trial_recv,
    hand_recv,
    psi_recv,
    screened_recv,
    block_recv,
    take_recv,
    first_recv,
    second_recv,
    parts_recv,
):
    bf16, f32 = jnp.bfloat16, jnp.float32
    me = lax.axis_index("tile")
    half = lax.axis_index("vec")
    other = 1 - half
    z, y, x = me // 4, (me // 2) % 2, me % 2
    across = lax.rem(y + 1, 2)
    aside = lax.rem(x + 1, 2)
    table = sources_of(layers)
    events = layers - 1
    source = [pick([row[e] for row in table], z) for e in range(events)]
    distance = [pick([abs(row[e] - k) for k, row in enumerate(table)], z) for e in range(events)]
    at_distance = [[distance[e] == k for k in range(layers)] for e in range(events)]

    ranks = outer_first(layers)

    def place_of(zz):
        return pick([ranks.index(k) for k in range(layers)], zz)

    def tile_of(zz, yy, xx):
        return zz * 4 + yy * 2 + xx

    mate_x, mate_y = tile_of(z, y, aside), tile_of(z, across, x)
    up, down = jnp.minimum(z + 1, layers - 1), jnp.maximum(z - 1, 0)
    has_up, has_down = z < layers - 1, z > 0
    on_up = [has_up & (source[e] < z) for e in range(events)]
    on_down = [has_down & (source[e] > z) for e in range(events)]

    def slot_of(zz, yy):
        return zz * 2 + yy

    slots = layers * 2
    order = [("own", 0)]
    for e in range(events - 1):
        order += [("z", e), ("y", e - 1)]
    order += [("y", events - 2), ("z", events - 1), ("y", events - 1)]

    def slot_at(kind, e):
        zz = source[e] if e >= 0 and kind != "own" else z
        return slot_of(zz, across if kind == "y" else y)

    turns = [slot_at(*event) for event in order]

    rows, conduct = trial_hbm.shape
    width = psi_c_hbm.shape[1]
    points = psi_v_hbm.shape[-1]
    middle = conduct // 2
    part = middle // 2
    height = psi_c_hbm.shape[0] // CUTS

    def lines(tile, vec):
        tile = place_of(tile // 4) * 4 + tile % 4
        start = pl.multiple_of((tile * 2 + vec) * rows, rows)
        return whole.at[pl.ds(start, rows), :]

    def columns(tile):
        return pl.ds(pl.multiple_of(tile * width, 128), width)

    def load(src, dst, sem):
        copy = pltpu.make_async_copy(src, dst, local_sem.at[sem])
        copy.start()
        return copy

    home_slot, mate_slot = slot_of(z, y), slot_of(z, across)

    def block_of(slot):
        return panel.at[pl.ds(pl.multiple_of(slot * conduct, conduct), conduct), :]

    load_rows = load(trial_hbm, lines(me, half), 0)
    for i, layer in enumerate(ranks):
        load(psi_v_hbm.at[layer], psi.at[0, i], 1)
    load_block = load(psi_c_hbm, block_of(home_slot), 2)

    def remote(src, dst, send, recv, tile, vec):
        return pltpu.make_async_remote_copy(
            src_ref=src,
            dst_ref=dst,
            send_sem=send,
            recv_sem=recv,
            device_id=(tile, vec),
            device_id_type=pl.DeviceIdType.MESH,
        )

    partners = [(mate_x, half), (mate_y, half), (me, other)]
    for d in range(1, layers):
        for v in range(2):
            partners.append((tile_of(lax.rem(z + d, layers), y, x), v))
    with jax.named_scope("pbar"):
        barrier = pltpu.get_barrier_semaphore()
        for partner in partners:
            pl.semaphore_signal(
                barrier, inc=1, device_id=partner, device_id_type=pl.DeviceIdType.MESH
            )
        pl.semaphore_wait(barrier, len(partners))

    def send(src, dst, group, recv, tile, vec, cond=None):
        copy = remote(src, dst, sends.at[group], recv, tile, vec)
        if cond is None:
            copy.start()
        else:
            pl.when(cond)(copy.start)

    def sent(ref, group):
        remote(ref, ref, sends.at[group], psi_recv.at[0], me, other).wait_send()

    def got(ref, recv):
        remote(ref, ref, sends.at[0], recv, me, other).wait_recv()

    def piece(slot, s):
        start = pl.multiple_of(slot * conduct + s * height, height)
        return panel.at[pl.ds(start, height), :]

    def hand(tile):
        ref = lines(tile, half)
        send(ref, ref, ROWS, hand_recv.at[0], me, other)

    def spread(tile, column):
        ref = lines(tile, half)
        recv = trial_recv.at[tile]
        if column:
            for e in range(events):
                send(ref, ref, ROWS, recv, tile_of(source[e], y, x), half)
        send(ref, ref, ROWS, recv, mate_y, half)
        hand(tile)

    last = CUTS - 1

    def along(slot, s, to_up, to_down):
        ref = piece(slot, s)
        recv = block_recv.at[slot, s]
        send(ref, ref, LAYERS, recv, tile_of(up, y, x), half, to_up)
        send(ref, ref, LAYERS, recv, tile_of(down, y, x), half, to_down)

    def cross(slot, s):
        ref = piece(slot, s)
        send(ref, ref, ACROSS, block_recv.at[slot, s], mate_y, half)

    def came(slot, s):
        got(piece(slot, s), block_recv.at[slot, s])

    pair_layers = layers // 2

    def psi_half(ref, which):
        return ref.at[pl.ds(which * pair_layers, pair_layers)]

    def take_piece(e, s):
        slot = slot_of(source[e], y)
        came(slot, s)
        along(slot, s, on_up[e], on_down[e])
        if s < last:
            cross(slot, s)

    def take_mate(e):
        slot = slot_of(source[e], across)
        came(slot, last)
        along(slot, last, on_up[e], on_down[e])

    def at_k(k):
        return [e for e in range(events) if any(abs(row[e] - r) == k for r, row in enumerate(table))]

    def arrive(k, first, final):
        for s in range(first, final):
            for e in at_k(k):
                pl.when(at_distance[e][k])(functools.partial(take_piece, e, s))
        if final == CUTS:
            for e in at_k(k):
                pl.when(at_distance[e][k])(functools.partial(take_mate, e))

    with jax.named_scope("ptrial"):
        ref = lines(me, half)
        load_rows.wait()
        send(ref, ref, ROWS, trial_recv.at[me], mate_x, half)
        spread(me, True)
        for i, turn in enumerate(turns):
            load(screened_hbm.at[:, columns(turn * 2 + aside)], stage.at[i], 3)
        for i, turn in enumerate(turns):
            load(screened_hbm.at[:, columns(turn * 2 + x)], screened_own.at[i], 4)
        pltpu.make_async_copy(psi_v_hbm, psi.at[0], local_sem.at[1]).wait()
        ref = psi_half(psi.at[0], half)
        send(ref, psi_half(psi.at[1], half), POINTS, psi_recv.at[0], mate_x, half)
        got(lines(mate_x, half), trial_recv.at[mate_x])
        spread(mate_x, True)
        load_block.wait()
        cross(home_slot, last)

        pltpu.make_async_copy(stage, stage, local_sem.at[3]).wait()
        for i in range(slots):
            screened_out[i] = stage[i].astype(bf16)
        for i in range(slots):
            send(screened_out.at[i], screened_in.at[i], SHARE, screened_recv.at[i], mate_x, half)

        for e in range(events):
            for xx in range(2):
                tile = tile_of(source[e], y, xx)
                got(lines(tile, half), trial_recv.at[tile])
                spread(tile, False)
            if e == max(events - 2, 0):
                for s in range(CUTS):
                    along(home_slot, s, has_up, has_down)
        for s in range(last):
            cross(home_slot, s)

        back[...] = jnp.zeros_like(back)
        valence = layers * 4 * 2 * rows
        psi_t[0] = psi[0].reshape(valence, points).T

        for e in range(-1, events):
            for xx in range(2):
                tile = tile_of(source[e] if e >= 0 else z, across, xx)
                got(lines(tile, half), trial_recv.at[tile])
                hand(tile)

        ref = psi_half(psi.at[1], half)
        got(ref, psi_recv.at[0])
        send(ref, ref, POINTS, psi_recv.at[1], me, other)
        came(mate_slot, last)
        along(mate_slot, last, has_up, has_down)
        arrive(1, 0, CUTS)
        got(whole.at[pl.ds(0, layers * 4 * rows), :], hand_recv.at[0])

    wide = 256

    def project(p):
        def chunk(j, carry):
            cols = pl.ds(pl.multiple_of(j * wide, wide), wide)
            flat[p, :, cols] = jnp.dot(
                psi_t[p], whole[:, cols], preferred_element_type=f32
            ).astype(bf16)
            return carry

        lax.fori_loop(0, conduct // wide, chunk, 0)

    with jax.named_scope("pproj"):
        project(0)
        got(psi_half(psi.at[1], other), psi_recv.at[1])
        psi_t[1] = psi[1].reshape(valence, points).T
        project(1)

    farthest = layers - 1

    def receive(i):
        kind, e = order[i]
        if kind == "z" and e > 0:
            arrive(e + 1, last if e + 1 == farthest else 0, CUTS)
        if kind == "y":
            for s in range(last):
                came(turns[i], s)

    def between(i):
        if i + 1 < slots and order[i + 1] == ("z", farthest - 1) and farthest > 1:
            arrive(farthest, 0, last)

    def step(p, share, slot, ready=None, between=None):
        block = block_of(slot)
        pair = jnp.dot(flat[p], block[...], preferred_element_type=f32)
        if ready is not None:
            ready()
        weighted = (share().astype(f32) * pair).astype(bf16)
        for h in (other, half):
            rows_of = pl.ds(pl.multiple_of(h * middle, middle), middle)
            back[p, h] += back_product(weighted, block[rows_of, :])
            if between is not None and h is other:
                between()

    pltpu.make_async_copy(screened_own, screened_own, local_sem.at[4]).wait()

    def use(k, carry):
        slot = turns[0]
        for i in range(final):
            slot = jnp.where(k == i, turns[i], slot)
            pl.when(k == i)(functools.partial(receive, i))
        step(0, lambda: screened_own[k], slot)
        for i in range(final):
            pl.when(k == i)(functools.partial(between, i))
        got(screened_in.at[k], screened_recv.at[k])
        step(1, lambda: screened_in[k], slot)
        return carry

    final = slots - 1
    with jax.named_scope("puse"):
        lax.fori_loop(0, final, use, 0)
        receive(final)
        step(0, lambda: screened_own[final], turns[final])

    def span(kind):
        return pl.ds(kind * part, part)

    def swap(p):
        for kind in range(2):
            give[kind, p] = back[p, other, :, span(kind)].astype(bf16)
            send(give.at[kind, p], take.at[kind, p], GIVE, take_recv.at[kind, p], me, other)

    def split(kind, p):
        got(take.at[kind, p], take_recv.at[kind, p])
        total = back[p, half, :, span(kind)] + take[kind, p].astype(f32)
        high = total.astype(bf16)
        flat[p, :, span(kind)] = high
        low = (total - high.astype(f32)).astype(bf16)
        flat[p, :, pl.ds(middle + kind * part, part)] = low

    block_rows = 2 * rows

    def product(p, kind, i):
        left = psi[p, i].reshape(4 * block_rows, points)
        total = None
        for level in range(2):
            cols = pl.ds(level * middle + kind * part, part)
            value = jnp.dot(left, flat[p, :, cols], preferred_element_type=f32)
            total = value if total is None else total + value
        return total.reshape(2, 2, block_rows, part)

    def leave(i, kind):
        if i < AHEAD:
            keep[kind, i] += product(1, kind, i)
        else:
            keep[kind, i] = product(0, kind, i) + product(1, kind, i)
        if kind == 0:
            away = keep[kind, i, :, pl.ds(aside, 1)]
        else:
            away = keep[kind, i, pl.ds(across, 1)]
        first_send[kind, i] = away.reshape(2, block_rows, part).astype(bf16)
        ref = first_send.at[kind, i]
        recv = first_recv.at[kind, i]
        send(ref, first_got.at[kind, i], FIRST, recv, [mate_x, mate_y][kind], half)

    def again(i, kind):
        got(first_got.at[kind, i], first_recv.at[kind, i])
        yy, xx = [(across, x), (y, aside)][kind]
        away = [across, aside][kind]
        value = keep[kind, i, yy, xx] + first_got[kind, i, away].astype(f32)
        second_send[kind, i] = value.astype(bf16)
        ref = second_send.at[kind, i]
        recv = second_recv.at[kind, i]
        send(ref, second_got.at[kind, i], SECOND, recv, [mate_y, mate_x][kind], half)
        keep[kind, i, y, x] += first_got[kind, i, [y, x][kind]].astype(f32)

    def deliver(i, kind):
        got(second_got.at[kind, i], second_recv.at[kind, i])
        value = keep[kind, i, y, x] + second_got[kind, i].astype(f32)
        keep[kind, i, y, x] = value
        third[kind, i] = value.astype(bf16)
        layer = ranks[i]
        for v in range(2):
            send(
                third.at[kind, i, pl.ds(v * rows, rows)],
                parts.at[half, kind, z],
                THIRD,
                parts_recv.at[half, kind],
                tile_of(layer, y, x),
                v,
                (z != layer) | (half != v),
            )

    with jax.named_scope("plast"):
        swap(0)
        step(
            1,
            lambda: screened_in[final],
            turns[final],
            lambda: got(screened_in.at[final], screened_recv.at[final]),
            lambda: swap(1),
        )

    with jax.named_scope("pearly"):
        for kind in range(2):
            split(kind, 0)
        for i in range(AHEAD):
            for kind in range(2):
                keep[kind, i] = product(0, kind, i)

    with jax.named_scope("preduce"):
        for i in range(layers + 2):
            for kind in range(2):
                if i == 0:
                    split(kind, 1)
                if i < layers:
                    leave(i, kind)
            for kind in range(2):
                if 0 <= i - 1 < layers:
                    again(i - 1, kind)
            for kind in range(2):
                if 0 <= i - 2 < layers:
                    deliver(i - 2, kind)

    with jax.named_scope("psum"):
        for flip in range(2):
            vec = lax.rem(half + flip, 2)
            for kind in range(2):
                value = None
                if flip == 0:
                    mine = pl.ds(pl.multiple_of(half * rows, rows), rows)
                    value = keep[kind, place_of(z), y, x, mine]
                count = layers - 1 + flip
                got(parts.at[vec, kind, pl.ds(0, count)], parts_recv.at[vec, kind])
                for d in range(1 - flip, layers):
                    more = parts[vec, kind, lax.rem(z + d, layers)].astype(f32)
                    value = more if value is None else value + more
                block = pl.ds(pl.multiple_of(vec * middle + kind * part, 128), part)
                result[:, block] = value

    def rows_as(count):
        return whole.at[pl.ds(0, count), :]

    def pieces_as(count):
        return panel.at[pl.ds(0, count * height), :]

    with jax.named_scope("pend"):
        sent(rows_as((8 * layers - 1) * rows), ROWS)
        sent(pieces_as(CUTS + events * last), ACROSS)
        for k in range(layers):
            ends = (k == 0) + (k == layers - 1)
            onward = sum((o < k < layers - 1) or (0 < k < o) for o in table[k])
            count = (2 - ends + onward) * (CUTS + 1)
            pl.when(z == k)(functools.partial(sent, pieces_as(count), LAYERS))
        sent(screened_out, SHARE)
        sent(psi.at[1], POINTS)
        sent(give, GIVE)
        sent(first_send, FIRST)
        sent(second_send, SECOND)
        sent(rows_as(2 * (2 * layers - 1) * rows * part // conduct), THIRD)


def write_out(result, out_hbm, sem):
    copy = pltpu.make_async_copy(result, out_hbm, sem)
    copy.start()
    copy.wait()


def fused(tiles, trial, psi_v, psi_c, screened):
    rows, conduct = trial.shape[1:]
    valence, points = psi_v.shape
    width = psi_c.shape[2]
    middle = conduct // 2
    part = middle // 2
    layers = tiles // 4
    slots = layers * 2
    bf16, f32 = jnp.bfloat16, jnp.float32
    far = pl.BlockSpec(memory_space=pl.ANY)
    dma = pltpu.SemaphoreType.DMA
    vmem = pltpu.VMEM
    out = pl.pallas_call(
        functools.partial(body, layers),
        out_shape=vmem((rows, conduct), f32),
        in_specs=[far] * 4,
        out_specs=pl.BlockSpec(memory_space=vmem),
        scratch_shapes=[
            vmem((valence, conduct), bf16),
            vmem((2, layers, 2, 2, 2 * rows, points), bf16),
            vmem((2, points, valence), bf16),
            vmem((slots, points, width), f32),
            vmem((slots, points, width), f32),
            vmem((slots, points, width), bf16),
            vmem((slots, points, width), bf16),
            vmem((slots * conduct, width), bf16),
            vmem((2, points, conduct), bf16),
            vmem((2, 2, points, middle), f32),
            vmem((2, 2, points, part), bf16),
            vmem((2, 2, points, part), bf16),
            vmem((2, layers, 2, 2 * rows, part), bf16),
            vmem((2, layers, 2, 2 * rows, part), bf16),
            vmem((2, layers, 2, 2, 2 * rows, part), f32),
            vmem((2, layers, 2 * rows, part), bf16),
            vmem((2, layers, 2 * rows, part), bf16),
            vmem((2, layers, 2 * rows, part), bf16),
            vmem((2, 2, layers, rows, part), bf16),
            dma((5,)),
            dma((9,)),
            dma((tiles,)),
            dma((1,)),
            dma((2,)),
            dma((slots,)),
            dma((slots, CUTS)),
            dma((2, 2)),
            dma((2, layers)),
            dma((2, layers)),
            dma((2, 2)),
        ],
        compiler_params=pltpu.CompilerParams(
            collective_id=0, has_side_effects=True, vmem_limit_bytes=58 * 1024 * 1024
        ),
    )(
        trial[0],
        psi_v.reshape(layers, 2, 2, 2 * rows, points),
        psi_c[:, 0, :],
        screened,
    )
    out = pl.pallas_call(
        write_out,
        out_shape=jax.ShapeDtypeStruct((rows, conduct), f32),
        in_specs=[pl.BlockSpec(memory_space=vmem)],
        out_specs=far,
        scratch_shapes=[dma(())],
        compiler_params=pltpu.CompilerParams(vmem_limit_bytes=1024 * 1024),
    )(out)
    return out[None]


def solution(mesh):
    tiles = mesh.shape["tile"]

    def shards(trial, psi_v, psi_c, screened):
        fits = (
            trial.shape[0] == 1
            and mesh.shape["vec"] == 2
            and tiles % 8 == 0
            and psi_v.shape[1] % 128 == 0
            and psi_c.shape[2] % 128 == 0
            and trial.shape[1] % 16 == 0
            and trial.shape[2] % 512 == 0
        )
        if fits:
            return fused(tiles, trial, psi_v, psi_c, screened)
        return plain(trial, psi_v, psi_c, screened)

    in_specs = (
        P(None, ("tile", "vec"), None),
        P(None, "tile"),
        P(None, "vec", "tile"),
        P("tile", "vec"),
    )
    out_specs = P(None, ("tile", "vec"), None)
    return jax.shard_map(shards, mesh=mesh, in_specs=in_specs, out_specs=out_specs, check_vma=False)
```

```python
import functools

import jax
import jax.numpy as jnp
from jax import lax
from jax.experimental import pallas as pl
from jax.experimental.pallas import tpu as pltpu
from jax.sharding import PartitionSpec as P

CUTS = 4
AHEAD = 2
ROWS, ACROSS, LAYERS, SHARE, POINTS, GIVE, FIRST, SECOND, THIRD = range(9)


def back_product(weighted_flat, panel):
    return lax.dot_general(
        weighted_flat, panel, (((1,), (1,)), ((), ())), preferred_element_type=jnp.float32
    )


def plain(trial, psi_v, psi_c, screened):
    count = trial.shape[0]
    points = psi_v.shape[1]
    conduct = trial.shape[2]
    whole = lax.all_gather(trial, ("tile", "vec"), axis=1, tiled=True)
    projected = jnp.einsum("vp,kvc->kpc", psi_v, whole, preferred_element_type=jnp.float32).astype(
        jnp.bfloat16
    )
    flat = projected.reshape(count * points, conduct)
    panel_local = psi_c[:, 0, :]
    panel = lax.all_gather(panel_local, "tile", axis=1, tiled=True)
    pair = jnp.dot(flat, panel, preferred_element_type=jnp.float32)
    weighted = (screened[None] * pair.reshape(count, points, -1)).astype(jnp.bfloat16)
    weighted_flat = weighted.reshape(count * points, -1)
    back = back_product(weighted_flat, panel)
    back = back.reshape(count, points, conduct)
    left = psi_v.astype(jnp.float32)
    summed = lax.psum(back, "vec")
    tiles = lax.axis_size("tile")
    halves = lax.axis_size("vec")
    owned = left.shape[0] // (tiles * halves)
    grouped = left.reshape(tiles, halves, owned, points)
    mine = lax.dynamic_index_in_dim(grouped, lax.axis_index("vec"), 1, keepdims=False).reshape(
        tiles * owned, points
    )
    pieces = []
    for one in range(count):
        term = jnp.dot(mine, summed[one], precision=lax.Precision.HIGHEST)
        pieces.append(lax.psum_scatter(term, "tile", scatter_dimension=0, tiled=True))
    return jnp.stack(pieces, axis=0)


def sources_of(layers):
    return [
        sorted((o for o in range(layers) if o != z), key=lambda o: (abs(o - z), o))
        for z in range(layers)
    ]


def outer_first(layers):
    return sorted(range(layers), key=lambda k: (-abs(2 * k - layers + 1), k))


def pick(values, at):
    chosen = jnp.int32(values[0])
    for k, value in enumerate(values[1:], 1):
        chosen = jnp.where(at == k, jnp.int32(value), chosen)
    return chosen


def body(
    layers,
    trial_hbm,
    psi_v_hbm,
    psi_c_hbm,
    screened_hbm,
    result,
    whole,
    psi,
    psi_t,
    stage,
    screened_own,
    screened_out,
    screened_in,
    panel,
    flat,
    back,
    give,
    take,
    first_send,
    first_got,
    keep,
    second_send,
    second_got,
    third,
    parts,
    local_sem,
    sends,
    trial_recv,
    hand_recv,
    psi_recv,
    screened_recv,
    block_recv,
    take_recv,
    first_recv,
    second_recv,
    parts_recv,
):
    bf16, f32 = jnp.bfloat16, jnp.float32
    me = lax.axis_index("tile")
    half = lax.axis_index("vec")
    other = 1 - half
    z, y, x = me // 4, (me // 2) % 2, me % 2
    across = lax.rem(y + 1, 2)
    aside = lax.rem(x + 1, 2)
    table = sources_of(layers)
    events = layers - 1
    source = [pick([row[e] for row in table], z) for e in range(events)]
    distance = [pick([abs(row[e] - k) for k, row in enumerate(table)], z) for e in range(events)]
    at_distance = [[distance[e] == k for k in range(layers)] for e in range(events)]

    ranks = outer_first(layers)

    def place_of(zz):
        return pick([ranks.index(k) for k in range(layers)], zz)

    def tile_of(zz, yy, xx):
        return zz * 4 + yy * 2 + xx

    mate_x, mate_y = tile_of(z, y, aside), tile_of(z, across, x)
    up, down = jnp.minimum(z + 1, layers - 1), jnp.maximum(z - 1, 0)
    has_up, has_down = z < layers - 1, z > 0
    at_end = (z == 0) | (z == layers - 1)
    on_up = [has_up & (source[e] < z) for e in range(events)]
    on_down = [has_down & (source[e] > z) for e in range(events)]

    def slot_of(zz, yy):
        return zz * 2 + yy

    slots = layers * 2
    order = [("own", 0)]
    for e in range(events - 1):
        order += [("z", e), ("y", e - 1)]
    order += [("y", events - 2), ("z", events - 1), ("y", events - 1)]

    def slot_at(kind, e):
        zz = source[e] if e >= 0 and kind != "own" else z
        return slot_of(zz, across if kind == "y" else y)

    turns = [slot_at(*event) for event in order]

    rows, conduct = trial_hbm.shape
    width = psi_c_hbm.shape[1]
    points = psi_v_hbm.shape[-1]
    middle = conduct // 2
    part = middle // 2
    height = psi_c_hbm.shape[0] // CUTS

    def lines(tile, vec):
        tile = place_of(tile // 4) * 4 + tile % 4
        start = pl.multiple_of((tile * 2 + vec) * rows, rows)
        return whole.at[pl.ds(start, rows), :]

    def columns(tile):
        return pl.ds(pl.multiple_of(tile * width, 128), width)

    def load(src, dst, sem):
        copy = pltpu.make_async_copy(src, dst, local_sem.at[sem])
        copy.start()
        return copy

    home_slot, mate_slot = slot_of(z, y), slot_of(z, across)

    def block_of(slot):
        return panel.at[pl.ds(pl.multiple_of(slot * conduct, conduct), conduct), :]

    load_rows = load(trial_hbm, lines(me, half), 0)
    for i, layer in enumerate(ranks):
        load(psi_v_hbm.at[layer], psi.at[0, i], 1)
    load_block = load(psi_c_hbm, block_of(home_slot), 2)

    def remote(src, dst, send, recv, tile, vec):
        return pltpu.make_async_remote_copy(
            src_ref=src,
            dst_ref=dst,
            send_sem=send,
            recv_sem=recv,
            device_id=(tile, vec),
            device_id_type=pl.DeviceIdType.MESH,
        )

    partners = [(mate_x, half, None), (mate_y, half, None), (me, other, None)]
    partners += [(tile_of(up, y, x), half, has_up), (tile_of(down, y, x), half, has_down)]
    with jax.named_scope("pbar"):
        barrier = pltpu.get_barrier_semaphore()

        def greet(tile, vec):
            pl.semaphore_signal(
                barrier, inc=1, device_id=(tile, vec), device_id_type=pl.DeviceIdType.MESH
            )

        for tile, vec, cond in partners:
            if cond is None:
                greet(tile, vec)
            else:
                pl.when(cond)(functools.partial(greet, tile, vec))
        for k in range(layers):
            count = 3 + (k > 0) + (k < layers - 1)
            pl.when(z == k)(functools.partial(pl.semaphore_wait, barrier, count))

    def send(src, dst, group, recv, tile, vec, cond=None):
        copy = remote(src, dst, sends.at[group], recv, tile, vec)
        if cond is None:
            copy.start()
        else:
            pl.when(cond)(copy.start)

    def sent(ref, group):
        remote(ref, ref, sends.at[group], psi_recv.at[0], me, other).wait_send()

    def got(ref, recv):
        remote(ref, ref, sends.at[0], recv, me, other).wait_recv()

    def piece(slot, s):
        start = pl.multiple_of(slot * conduct + s * height, height)
        return panel.at[pl.ds(start, height), :]

    def hand(tile):
        ref = lines(tile, half)
        send(ref, ref, ROWS, hand_recv.at[0], me, other)

    def spread(tile, to_up, to_down):
        ref = lines(tile, half)
        recv = trial_recv.at[tile]
        send(ref, ref, ROWS, recv, tile_of(up, y, x), half, to_up)
        send(ref, ref, ROWS, recv, tile_of(down, y, x), half, to_down)
        send(ref, ref, ROWS, recv, mate_y, half)
        hand(tile)

    last = CUTS - 1

    def along(slot, s, to_up, to_down):
        ref = piece(slot, s)
        recv = block_recv.at[slot, s]
        send(ref, ref, LAYERS, recv, tile_of(up, y, x), half, to_up)
        send(ref, ref, LAYERS, recv, tile_of(down, y, x), half, to_down)

    def cross(slot, s):
        ref = piece(slot, s)
        send(ref, ref, ACROSS, block_recv.at[slot, s], mate_y, half)

    def came(slot, s):
        got(piece(slot, s), block_recv.at[slot, s])

    pair_layers = layers // 2

    def psi_half(ref, which):
        return ref.at[pl.ds(which * pair_layers, pair_layers)]

    def take_piece(e, s):
        slot = slot_of(source[e], y)
        came(slot, s)
        along(slot, s, on_up[e], on_down[e])
        if s < last:
            cross(slot, s)

    def take_mate(e):
        slot = slot_of(source[e], across)
        came(slot, last)
        along(slot, last, on_up[e], on_down[e])

    def at_k(k):
        return [e for e in range(events) if any(abs(row[e] - r) == k for r, row in enumerate(table))]

    def arrive(k, first, final):
        for s in range(first, final):
            for e in at_k(k):
                pl.when(at_distance[e][k])(functools.partial(take_piece, e, s))
        if final == CUTS:
            for e in at_k(k):
                pl.when(at_distance[e][k])(functools.partial(take_mate, e))

    with jax.named_scope("ptrial"):
        ref = lines(me, half)
        load_rows.wait()
        send(ref, ref, ROWS, trial_recv.at[me], mate_x, half)
        spread(me, has_up, has_down)
        for i, turn in enumerate(turns):
            load(screened_hbm.at[:, columns(turn * 2 + aside)], stage.at[i], 3)
        for i, turn in enumerate(turns):
            load(screened_hbm.at[:, columns(turn * 2 + x)], screened_own.at[i], 4)
        pltpu.make_async_copy(psi_v_hbm, psi.at[0], local_sem.at[1]).wait()
        ref = psi_half(psi.at[0], half)
        send(ref, psi_half(psi.at[1], half), POINTS, psi_recv.at[0], mate_x, half)
        got(lines(mate_x, half), trial_recv.at[mate_x])
        spread(mate_x, has_up, has_down)
        load_block.wait()
        cross(home_slot, last)

        pltpu.make_async_copy(stage, stage, local_sem.at[3]).wait()
        for i in range(slots):
            screened_out[i] = stage[i].astype(bf16)
        for i in range(slots):
            send(screened_out.at[i], screened_in.at[i], SHARE, screened_recv.at[i], mate_x, half)

        for e in range(events):
            for xx in range(2):
                tile = tile_of(source[e], y, xx)
                got(lines(tile, half), trial_recv.at[tile])
                spread(tile, on_up[e], on_down[e])
            if e == events - 2:
                for s in range(CUTS):
                    along(home_slot, s, has_up & at_end, has_down & at_end)
        for s in range(CUTS):
            if events > 1:
                along(home_slot, s, has_up & ~at_end, has_down & ~at_end)
            else:
                along(home_slot, s, has_up, has_down)
        for s in range(last):
            cross(home_slot, s)

        back[...] = jnp.zeros_like(back)
        valence = layers * 4 * 2 * rows
        psi_t[0] = psi[0].reshape(valence, points).T

        for e in range(-1, events):
            for xx in range(2):
                tile = tile_of(source[e] if e >= 0 else z, across, xx)
                got(lines(tile, half), trial_recv.at[tile])
                hand(tile)

        ref = psi_half(psi.at[1], half)
        got(ref, psi_recv.at[0])
        send(ref, ref, POINTS, psi_recv.at[1], me, other)
        came(mate_slot, last)
        along(mate_slot, last, has_up, has_down)
        arrive(1, 0, CUTS)
        got(whole.at[pl.ds(0, layers * 4 * rows), :], hand_recv.at[0])

    wide = 256

    def project(p):
        def chunk(j, carry):
            cols = pl.ds(pl.multiple_of(j * wide, wide), wide)
            flat[p, :, cols] = jnp.dot(
                psi_t[p], whole[:, cols], preferred_element_type=f32
            ).astype(bf16)
            return carry

        lax.fori_loop(0, conduct // wide, chunk, 0)

    with jax.named_scope("pproj"):
        project(0)
        got(psi_half(psi.at[1], other), psi_recv.at[1])
        psi_t[1] = psi[1].reshape(valence, points).T
        project(1)

    farthest = layers - 1

    def receive(i):
        kind, e = order[i]
        if kind == "z" and e > 0:
            arrive(e + 1, last if e + 1 == farthest else 0, CUTS)
        if kind == "y":
            for s in range(last):
                came(turns[i], s)

    def between(i):
        if i + 1 < slots and order[i + 1] == ("z", farthest - 1) and farthest > 1:
            arrive(farthest, 0, last)

    def step(p, share, slot, ready=None, between=None):
        block = block_of(slot)
        pair = jnp.dot(flat[p], block[...], preferred_element_type=f32)
        if ready is not None:
            ready()
        weighted = (share().astype(f32) * pair).astype(bf16)
        for h in (other, half):
            rows_of = pl.ds(pl.multiple_of(h * middle, middle), middle)
            back[p, h] += back_product(weighted, block[rows_of, :])
            if between is not None and h is other:
                between()

    pltpu.make_async_copy(screened_own, screened_own, local_sem.at[4]).wait()

    def use(k, carry):
        slot = turns[0]
        for i in range(final):
            slot = jnp.where(k == i, turns[i], slot)
            pl.when(k == i)(functools.partial(receive, i))
        step(0, lambda: screened_own[k], slot)
        for i in range(final):
            pl.when(k == i)(functools.partial(between, i))
        got(screened_in.at[k], screened_recv.at[k])
        step(1, lambda: screened_in[k], slot)
        return carry

    final = slots - 1
    with jax.named_scope("puse"):
        lax.fori_loop(0, final, use, 0)
        receive(final)
        step(0, lambda: screened_own[final], turns[final])

    def span(kind):
        return pl.ds(kind * part, part)

    def swap(p):
        for kind in range(2):
            give[kind, p] = back[p, other, :, span(kind)].astype(bf16)
            send(give.at[kind, p], take.at[kind, p], GIVE, take_recv.at[kind, p], me, other)

    def split(kind, p):
        got(take.at[kind, p], take_recv.at[kind, p])
        total = back[p, half, :, span(kind)] + take[kind, p].astype(f32)
        high = total.astype(bf16)
        flat[p, :, span(kind)] = high
        low = (total - high.astype(f32)).astype(bf16)
        flat[p, :, pl.ds(middle + kind * part, part)] = low

    block_rows = 2 * rows

    def product(p, kind, i):
        left = psi[p, i].reshape(4 * block_rows, points)
        total = None
        for level in range(2):
            cols = pl.ds(level * middle + kind * part, part)
            value = jnp.dot(left, flat[p, :, cols], preferred_element_type=f32)
            total = value if total is None else total + value
        return total.reshape(2, 2, block_rows, part)

    def prepare(i):
        for kind in range(2):
            if i < AHEAD:
                keep[kind, i] += product(1, kind, i)
            else:
                keep[kind, i] = product(0, kind, i) + product(1, kind, i)
        for kind in range(2):
            if kind == 0:
                away = keep[kind, i, :, pl.ds(aside, 1)]
            else:
                away = keep[kind, i, pl.ds(across, 1)]
            first_send[kind, i] = away.reshape(2, block_rows, part).astype(bf16)

    def leave(i):
        for kind in range(2):
            ref = first_send.at[kind, i]
            recv = first_recv.at[kind, i]
            send(ref, first_got.at[kind, i], FIRST, recv, [mate_x, mate_y][kind], half)

    def again(i, kind):
        got(first_got.at[kind, i], first_recv.at[kind, i])
        yy, xx = [(across, x), (y, aside)][kind]
        away = [across, aside][kind]
        value = keep[kind, i, yy, xx] + first_got[kind, i, away].astype(f32)
        second_send[kind, i] = value.astype(bf16)
        ref = second_send.at[kind, i]
        recv = second_recv.at[kind, i]
        send(ref, second_got.at[kind, i], SECOND, recv, [mate_y, mate_x][kind], half)
        keep[kind, i, y, x] += first_got[kind, i, [y, x][kind]].astype(f32)

    def deliver(i, kind):
        got(second_got.at[kind, i], second_recv.at[kind, i])
        value = keep[kind, i, y, x] + second_got[kind, i].astype(f32)
        keep[kind, i, y, x] = value
        third[kind, i] = value.astype(bf16)
        layer = ranks[i]
        for v in range(2):
            send(
                third.at[kind, i, pl.ds(v * rows, rows)],
                parts.at[half, kind, z],
                THIRD,
                parts_recv.at[half, kind],
                tile_of(layer, y, x),
                v,
                (z != layer) | (half != v),
            )

    with jax.named_scope("plast"):
        swap(0)
        step(
            1,
            lambda: screened_in[final],
            turns[final],
            lambda: got(screened_in.at[final], screened_recv.at[final]),
            lambda: swap(1),
        )

    with jax.named_scope("pearly"):
        for kind in range(2):
            split(kind, 0)
        for i in range(AHEAD):
            for kind in range(2):
                keep[kind, i] = product(0, kind, i)

    with jax.named_scope("preduce"):
        for kind in range(2):
            split(kind, 1)
        prepare(0)
        leave(0)
        prepare(1)
        leave(1)
        for i in range(layers):
            if i + 2 < layers:
                prepare(i + 2)
            for kind in range(2):
                again(i, kind)
            if i + 2 < layers:
                leave(i + 2)
            if i > 0:
                for kind in range(2):
                    deliver(i - 1, kind)
        for kind in range(2):
            deliver(layers - 1, kind)

    with jax.named_scope("psum"):
        for flip in range(2):
            vec = lax.rem(half + flip, 2)
            for kind in range(2):
                value = None
                if flip == 0:
                    mine = pl.ds(pl.multiple_of(half * rows, rows), rows)
                    value = keep[kind, place_of(z), y, x, mine]
                count = layers - 1 + flip
                got(parts.at[vec, kind, pl.ds(0, count)], parts_recv.at[vec, kind])
                for d in range(1 - flip, layers):
                    more = parts[vec, kind, lax.rem(z + d, layers)].astype(f32)
                    value = more if value is None else value + more
                block = pl.ds(pl.multiple_of(vec * middle + kind * part, 128), part)
                result[:, block] = value

    def rows_as(count):
        return panel.at[pl.ds(0, count * conduct // width), :]

    def pieces_as(count):
        return panel.at[pl.ds(0, count * height), :]

    with jax.named_scope("pend"):
        sent(pieces_as(CUTS + events * last), ACROSS)
        for k in range(layers):
            ends = (k == 0) + (k == layers - 1)
            onward = sum((o < k < layers - 1) or (0 < k < o) for o in table[k])
            count = (2 - ends + onward) * (CUTS + 1)
            pl.when(z == k)(functools.partial(sent, pieces_as(count), LAYERS))
            count = 1 + 2 * (2 - ends + 2) + 2 * (2 * events + onward) + 2 * layers
            pl.when(z == k)(functools.partial(sent, rows_as(count * rows), ROWS))
        sent(screened_out, SHARE)
        sent(psi.at[1], POINTS)
        sent(give, GIVE)
        sent(first_send, FIRST)
        sent(second_send, SECOND)
        sent(rows_as(2 * (2 * layers - 1) * rows * part // conduct), THIRD)


def write_out(result, out_hbm, sem):
    copy = pltpu.make_async_copy(result, out_hbm, sem)
    copy.start()
    copy.wait()


def fused(tiles, trial, psi_v, psi_c, screened):
    rows, conduct = trial.shape[1:]
    valence, points = psi_v.shape
    width = psi_c.shape[2]
    middle = conduct // 2
    part = middle // 2
    layers = tiles // 4
    slots = layers * 2
    bf16, f32 = jnp.bfloat16, jnp.float32
    far = pl.BlockSpec(memory_space=pl.ANY)
    dma = pltpu.SemaphoreType.DMA
    vmem = pltpu.VMEM
    out = pl.pallas_call(
        functools.partial(body, layers),
        out_shape=vmem((rows, conduct), f32),
        in_specs=[far] * 4,
        out_specs=pl.BlockSpec(memory_space=vmem),
        scratch_shapes=[
            vmem((valence, conduct), bf16),
            vmem((2, layers, 2, 2, 2 * rows, points), bf16),
            vmem((2, points, valence), bf16),
            vmem((slots, points, width), f32),
            vmem((slots, points, width), f32),
            vmem((slots, points, width), bf16),
            vmem((slots, points, width), bf16),
            vmem((slots * conduct, width), bf16),
            vmem((2, points, conduct), bf16),
            vmem((2, 2, points, middle), f32),
            vmem((2, 2, points, part), bf16),
            vmem((2, 2, points, part), bf16),
            vmem((2, layers, 2, 2 * rows, part), bf16),
            vmem((2, layers, 2, 2 * rows, part), bf16),
            vmem((2, layers, 2, 2, 2 * rows, part), f32),
            vmem((2, layers, 2 * rows, part), bf16),
            vmem((2, layers, 2 * rows, part), bf16),
            vmem((2, layers, 2 * rows, part), bf16),
            vmem((2, 2, layers, rows, part), bf16),
            dma((5,)),
            dma((9,)),
            dma((tiles,)),
            dma((1,)),
            dma((2,)),
            dma((slots,)),
            dma((slots, CUTS)),
            dma((2, 2)),
            dma((2, layers)),
            dma((2, layers)),
            dma((2, 2)),
        ],
        compiler_params=pltpu.CompilerParams(
            collective_id=0, has_side_effects=True, vmem_limit_bytes=58 * 1024 * 1024
        ),
    )(
        trial[0],
        psi_v.reshape(layers, 2, 2, 2 * rows, points),
        psi_c[:, 0, :],
        screened,
    )
    out = pl.pallas_call(
        write_out,
        out_shape=jax.ShapeDtypeStruct((rows, conduct), f32),
        in_specs=[pl.BlockSpec(memory_space=vmem)],
        out_specs=far,
        scratch_shapes=[dma(())],
        compiler_params=pltpu.CompilerParams(vmem_limit_bytes=1024 * 1024),
    )(out)
    return out[None]


def solution(mesh):
    tiles = mesh.shape["tile"]

    def shards(trial, psi_v, psi_c, screened):
        fits = (
            trial.shape[0] == 1
            and mesh.shape["vec"] == 2
            and tiles % 8 == 0
            and psi_v.shape[1] % 128 == 0
            and psi_c.shape[2] % 128 == 0
            and trial.shape[1] % 16 == 0
            and trial.shape[2] % 512 == 0
        )
        if fits:
            return fused(tiles, trial, psi_v, psi_c, screened)
        return plain(trial, psi_v, psi_c, screened)

    in_specs = (
        P(None, ("tile", "vec"), None),
        P(None, "tile"),
        P(None, "vec", "tile"),
        P("tile", "vec"),
    )
    out_specs = P(None, ("tile", "vec"), None)
    return jax.shard_map(shards, mesh=mesh, in_specs=in_specs, out_specs=out_specs, check_vma=False)
```

```python
import functools

import jax
import jax.numpy as jnp
from jax import lax
from jax.experimental import pallas as pl
from jax.experimental.pallas import tpu as pltpu
from jax.sharding import PartitionSpec as P

CUTS = 4
AHEAD = 2
ROWS, ACROSS, LAYERS, SHARE, POINTS, GIVE, FIRST, SECOND, THIRD = range(9)


def back_product(weighted_flat, panel):
    return lax.dot_general(
        weighted_flat, panel, (((1,), (1,)), ((), ())), preferred_element_type=jnp.float32
    )


def plain(trial, psi_v, psi_c, screened):
    count = trial.shape[0]
    points = psi_v.shape[1]
    conduct = trial.shape[2]
    whole = lax.all_gather(trial, ("tile", "vec"), axis=1, tiled=True)
    projected = jnp.einsum("vp,kvc->kpc", psi_v, whole, preferred_element_type=jnp.float32).astype(
        jnp.bfloat16
    )
    flat = projected.reshape(count * points, conduct)
    panel_local = psi_c[:, 0, :]
    panel = lax.all_gather(panel_local, "tile", axis=1, tiled=True)
    pair = jnp.dot(flat, panel, preferred_element_type=jnp.float32)
    weighted = (screened[None] * pair.reshape(count, points, -1)).astype(jnp.bfloat16)
    weighted_flat = weighted.reshape(count * points, -1)
    back = back_product(weighted_flat, panel)
    back = back.reshape(count, points, conduct)
    left = psi_v.astype(jnp.float32)
    summed = lax.psum(back, "vec")
    tiles = lax.axis_size("tile")
    halves = lax.axis_size("vec")
    owned = left.shape[0] // (tiles * halves)
    grouped = left.reshape(tiles, halves, owned, points)
    mine = lax.dynamic_index_in_dim(grouped, lax.axis_index("vec"), 1, keepdims=False).reshape(
        tiles * owned, points
    )
    pieces = []
    for one in range(count):
        term = jnp.dot(mine, summed[one], precision=lax.Precision.HIGHEST)
        pieces.append(lax.psum_scatter(term, "tile", scatter_dimension=0, tiled=True))
    return jnp.stack(pieces, axis=0)


def sources_of(layers):
    return [
        sorted((o for o in range(layers) if o != z), key=lambda o: (abs(o - z), o))
        for z in range(layers)
    ]


def outer_first(layers):
    return sorted(range(layers), key=lambda k: (-abs(2 * k - layers + 1), k))


def pick(values, at):
    chosen = jnp.int32(values[0])
    for k, value in enumerate(values[1:], 1):
        chosen = jnp.where(at == k, jnp.int32(value), chosen)
    return chosen


def body(
    layers,
    trial_hbm,
    psi_v_hbm,
    psi_c_hbm,
    screened_hbm,
    result,
    whole,
    psi,
    psi_t,
    stage,
    screened_own,
    screened_out,
    screened_in,
    panel,
    flat,
    back,
    give,
    take,
    first_send,
    first_got,
    keep,
    second_send,
    second_got,
    third,
    parts,
    local_sem,
    sends,
    trial_recv,
    hand_recv,
    psi_recv,
    screened_recv,
    block_recv,
    take_recv,
    first_recv,
    second_recv,
    parts_recv,
):
    bf16, f32 = jnp.bfloat16, jnp.float32
    me = lax.axis_index("tile")
    half = lax.axis_index("vec")
    other = 1 - half
    z, y, x = me // 4, (me // 2) % 2, me % 2
    across = lax.rem(y + 1, 2)
    aside = lax.rem(x + 1, 2)
    table = sources_of(layers)
    events = layers - 1
    source = [pick([row[e] for row in table], z) for e in range(events)]
    distance = [pick([abs(row[e] - k) for k, row in enumerate(table)], z) for e in range(events)]
    at_distance = [[distance[e] == k for k in range(layers)] for e in range(events)]

    ranks = outer_first(layers)

    def place_of(zz):
        return pick([ranks.index(k) for k in range(layers)], zz)

    def tile_of(zz, yy, xx):
        return zz * 4 + yy * 2 + xx

    mate_x, mate_y = tile_of(z, y, aside), tile_of(z, across, x)
    up, down = jnp.minimum(z + 1, layers - 1), jnp.maximum(z - 1, 0)
    has_up, has_down = z < layers - 1, z > 0
    at_end = (z == 0) | (z == layers - 1)
    on_up = [has_up & (source[e] < z) for e in range(events)]
    on_down = [has_down & (source[e] > z) for e in range(events)]

    def slot_of(zz, yy):
        return zz * 2 + yy

    slots = layers * 2
    order = [("own", 0)]
    for e in range(events - 1):
        order += [("z", e), ("y", e - 1)]
    order += [("y", events - 2), ("z", events - 1), ("y", events - 1)]

    def slot_at(kind, e):
        zz = source[e] if e >= 0 and kind != "own" else z
        return slot_of(zz, across if kind == "y" else y)

    turns = [slot_at(*event) for event in order]

    rows, conduct = trial_hbm.shape
    width = psi_c_hbm.shape[1]
    points = psi_v_hbm.shape[-1]
    middle = conduct // 2
    part = middle // 2
    height = psi_c_hbm.shape[0] // CUTS

    def lines(tile, vec):
        tile = place_of(tile // 4) * 4 + tile % 4
        start = pl.multiple_of((tile * 2 + vec) * rows, rows)
        return whole.at[pl.ds(start, rows), :]

    def columns(tile):
        return pl.ds(pl.multiple_of(tile * width, 128), width)

    def load(src, dst, sem):
        copy = pltpu.make_async_copy(src, dst, local_sem.at[sem])
        copy.start()
        return copy

    home_slot, mate_slot = slot_of(z, y), slot_of(z, across)

    def block_of(slot):
        return panel.at[pl.ds(pl.multiple_of(slot * conduct, conduct), conduct), :]

    load_rows = load(trial_hbm, lines(me, half), 0)
    for i, layer in enumerate(ranks):
        load(psi_v_hbm.at[layer], psi.at[0, i], 1)
    load_block = load(psi_c_hbm, block_of(home_slot), 2)

    def remote(src, dst, send, recv, tile, vec):
        return pltpu.make_async_remote_copy(
            src_ref=src,
            dst_ref=dst,
            send_sem=send,
            recv_sem=recv,
            device_id=(tile, vec),
            device_id_type=pl.DeviceIdType.MESH,
        )

    partners = [(mate_x, half, None), (mate_y, half, None), (me, other, None)]
    partners += [(tile_of(up, y, x), half, has_up), (tile_of(down, y, x), half, has_down)]
    with jax.named_scope("pbar"):
        barrier = pltpu.get_barrier_semaphore()

        def greet(tile, vec):
            pl.semaphore_signal(
                barrier, inc=1, device_id=(tile, vec), device_id_type=pl.DeviceIdType.MESH
            )

        for tile, vec, cond in partners:
            if cond is None:
                greet(tile, vec)
            else:
                pl.when(cond)(functools.partial(greet, tile, vec))
        for k in range(layers):
            count = 3 + (k > 0) + (k < layers - 1)
            pl.when(z == k)(functools.partial(pl.semaphore_wait, barrier, count))

    def send(src, dst, group, recv, tile, vec, cond=None):
        copy = remote(src, dst, sends.at[group], recv, tile, vec)
        if cond is None:
            copy.start()
        else:
            pl.when(cond)(copy.start)

    def sent(ref, group):
        remote(ref, ref, sends.at[group], psi_recv.at[0], me, other).wait_send()

    def got(ref, recv):
        remote(ref, ref, sends.at[0], recv, me, other).wait_recv()

    def piece(slot, s):
        start = pl.multiple_of(slot * conduct + s * height, height)
        return panel.at[pl.ds(start, height), :]

    def hand(tile):
        ref = lines(tile, half)
        send(ref, ref, ROWS, hand_recv.at[0], me, other)

    def spread(tile, to_up, to_down):
        ref = lines(tile, half)
        recv = trial_recv.at[tile]
        send(ref, ref, ROWS, recv, tile_of(up, y, x), half, to_up)
        send(ref, ref, ROWS, recv, tile_of(down, y, x), half, to_down)
        send(ref, ref, ROWS, recv, mate_y, half)
        hand(tile)

    last = CUTS - 1

    def along(slot, s, to_up, to_down):
        ref = piece(slot, s)
        recv = block_recv.at[slot, s]
        send(ref, ref, LAYERS, recv, tile_of(up, y, x), half, to_up)
        send(ref, ref, LAYERS, recv, tile_of(down, y, x), half, to_down)

    def cross(slot, s):
        ref = piece(slot, s)
        send(ref, ref, ACROSS, block_recv.at[slot, s], mate_y, half)

    def came(slot, s):
        got(piece(slot, s), block_recv.at[slot, s])

    pair_layers = layers // 2

    def psi_half(ref, which):
        return ref.at[pl.ds(which * pair_layers, pair_layers)]

    def take_piece(e, s):
        slot = slot_of(source[e], y)
        came(slot, s)
        along(slot, s, on_up[e], on_down[e])
        if s < last:
            cross(slot, s)

    def take_mate(e):
        slot = slot_of(source[e], across)
        came(slot, last)
        along(slot, last, on_up[e], on_down[e])

    def at_k(k):
        return [e for e in range(events) if any(abs(row[e] - r) == k for r, row in enumerate(table))]

    def arrive(k, first, final):
        for s in range(first, final):
            for e in at_k(k):
                pl.when(at_distance[e][k])(functools.partial(take_piece, e, s))
        if final == CUTS:
            for e in at_k(k):
                pl.when(at_distance[e][k])(functools.partial(take_mate, e))

    with jax.named_scope("ptrial"):
        ref = lines(me, half)
        load_rows.wait()
        send(ref, ref, ROWS, trial_recv.at[me], mate_x, half)
        spread(me, has_up, has_down)
        for i, turn in enumerate(turns):
            load(screened_hbm.at[:, columns(turn * 2 + aside)], stage.at[i], 3)
        for i, turn in enumerate(turns):
            load(screened_hbm.at[:, columns(turn * 2 + x)], screened_own.at[i], 4)
        pltpu.make_async_copy(psi_v_hbm, psi.at[0], local_sem.at[1]).wait()
        ref = psi_half(psi.at[0], half)
        send(ref, psi_half(psi.at[1], half), POINTS, psi_recv.at[0], mate_x, half)
        got(lines(mate_x, half), trial_recv.at[mate_x])
        spread(mate_x, has_up, has_down)
        load_block.wait()
        cross(home_slot, last)

        pltpu.make_async_copy(stage, stage, local_sem.at[3]).wait()
        for i in range(slots):
            screened_out[i] = stage[i].astype(bf16)
        for i in range(slots):
            send(screened_out.at[i], screened_in.at[i], SHARE, screened_recv.at[i], mate_x, half)

        for e in range(events):
            for xx in range(2):
                tile = tile_of(source[e], y, xx)
                got(lines(tile, half), trial_recv.at[tile])
                spread(tile, on_up[e], on_down[e])
            if e == events - 2:
                cross(home_slot, 0)
                for s in range(CUTS):
                    if s < CUTS // 2:
                        along(home_slot, s, has_up, has_down)
                    else:
                        along(home_slot, s, has_up & at_end, has_down & at_end)
        if events > 1:
            for s in range(CUTS // 2, CUTS):
                along(home_slot, s, has_up & ~at_end, has_down & ~at_end)
        else:
            for s in range(CUTS):
                along(home_slot, s, has_up, has_down)
        for s in range(1 if events > 1 else 0, last):
            cross(home_slot, s)

        back[...] = jnp.zeros_like(back)
        valence = layers * 4 * 2 * rows
        psi_t[0] = psi[0].reshape(valence, points).T

        for e in range(-1, events):
            for xx in range(2):
                tile = tile_of(source[e] if e >= 0 else z, across, xx)
                got(lines(tile, half), trial_recv.at[tile])
                hand(tile)

        ref = psi_half(psi.at[1], half)
        got(ref, psi_recv.at[0])
        send(ref, ref, POINTS, psi_recv.at[1], me, other)
        came(mate_slot, last)
        along(mate_slot, last, has_up, has_down)
        arrive(1, 0, CUTS)
        got(whole.at[pl.ds(0, layers * 4 * rows), :], hand_recv.at[0])

    wide = 256

    def project(p):
        def chunk(j, carry):
            cols = pl.ds(pl.multiple_of(j * wide, wide), wide)
            flat[p, :, cols] = jnp.dot(
                psi_t[p], whole[:, cols], preferred_element_type=f32
            ).astype(bf16)
            return carry

        lax.fori_loop(0, conduct // wide, chunk, 0)

    with jax.named_scope("pproj"):
        project(0)
        got(psi_half(psi.at[1], other), psi_recv.at[1])
        psi_t[1] = psi[1].reshape(valence, points).T
        project(1)

    farthest = layers - 1

    def receive(i):
        kind, e = order[i]
        if kind == "z" and e > 0:
            arrive(e + 1, last if e + 1 == farthest else 0, CUTS)
        if kind == "y":
            for s in range(last):
                came(turns[i], s)

    def between(i):
        if i + 1 < slots and order[i + 1] == ("z", farthest - 1) and farthest > 1:
            arrive(farthest, 0, last)

    def step(p, share, slot, ready=None, between=None):
        block = block_of(slot)
        pair = jnp.dot(flat[p], block[...], preferred_element_type=f32)
        if ready is not None:
            ready()
        weighted = (share().astype(f32) * pair).astype(bf16)
        for h in (other, half):
            rows_of = pl.ds(pl.multiple_of(h * middle, middle), middle)
            back[p, h] += back_product(weighted, block[rows_of, :])
            if between is not None and h is other:
                between()

    pltpu.make_async_copy(screened_own, screened_own, local_sem.at[4]).wait()

    def use(k, carry):
        slot = turns[0]
        for i in range(final):
            slot = jnp.where(k == i, turns[i], slot)
            pl.when(k == i)(functools.partial(receive, i))
        step(0, lambda: screened_own[k], slot)
        for i in range(final):
            pl.when(k == i)(functools.partial(between, i))
        got(screened_in.at[k], screened_recv.at[k])
        step(1, lambda: screened_in[k], slot)
        return carry

    final = slots - 1
    with jax.named_scope("puse"):
        lax.fori_loop(0, final, use, 0)
        receive(final)
        step(0, lambda: screened_own[final], turns[final])

    def span(kind):
        return pl.ds(kind * part, part)

    def swap(p):
        for kind in range(2):
            give[kind, p] = back[p, other, :, span(kind)].astype(bf16)
            send(give.at[kind, p], take.at[kind, p], GIVE, take_recv.at[kind, p], me, other)

    def split(kind, p):
        got(take.at[kind, p], take_recv.at[kind, p])
        total = back[p, half, :, span(kind)] + take[kind, p].astype(f32)
        high = total.astype(bf16)
        flat[p, :, span(kind)] = high
        low = (total - high.astype(f32)).astype(bf16)
        flat[p, :, pl.ds(middle + kind * part, part)] = low

    block_rows = 2 * rows

    def product(p, kind, i):
        left = psi[p, i].reshape(4 * block_rows, points)
        total = None
        for level in range(2):
            cols = pl.ds(level * middle + kind * part, part)
            value = jnp.dot(left, flat[p, :, cols], preferred_element_type=f32)
            total = value if total is None else total + value
        return total.reshape(2, 2, block_rows, part)

    def prepare(i):
        for kind in range(2):
            if i < AHEAD:
                keep[kind, i] += product(1, kind, i)
            else:
                keep[kind, i] = product(0, kind, i) + product(1, kind, i)
        for kind in range(2):
            if kind == 0:
                away = keep[kind, i, :, pl.ds(aside, 1)]
            else:
                away = keep[kind, i, pl.ds(across, 1)]
            first_send[kind, i] = away.reshape(2, block_rows, part).astype(bf16)

    def leave(i):
        for kind in range(2):
            ref = first_send.at[kind, i]
            recv = first_recv.at[kind, i]
            send(ref, first_got.at[kind, i], FIRST, recv, [mate_x, mate_y][kind], half)

    def again(i, kind):
        got(first_got.at[kind, i], first_recv.at[kind, i])
        yy, xx = [(across, x), (y, aside)][kind]
        away = [across, aside][kind]
        value = keep[kind, i, yy, xx] + first_got[kind, i, away].astype(f32)
        second_send[kind, i] = value.astype(bf16)
        ref = second_send.at[kind, i]
        recv = second_recv.at[kind, i]
        send(ref, second_got.at[kind, i], SECOND, recv, [mate_y, mate_x][kind], half)
        keep[kind, i, y, x] += first_got[kind, i, [y, x][kind]].astype(f32)

    def deliver(i, kind):
        got(second_got.at[kind, i], second_recv.at[kind, i])
        value = keep[kind, i, y, x] + second_got[kind, i].astype(f32)
        keep[kind, i, y, x] = value
        third[kind, i] = value.astype(bf16)
        layer = ranks[i]
        for v in range(2):
            send(
                third.at[kind, i, pl.ds(v * rows, rows)],
                parts.at[half, kind, z],
                THIRD,
                parts_recv.at[half, kind],
                tile_of(layer, y, x),
                v,
                (z != layer) | (half != v),
            )

    with jax.named_scope("plast"):
        swap(0)
        step(
            1,
            lambda: screened_in[final],
            turns[final],
            lambda: got(screened_in.at[final], screened_recv.at[final]),
            lambda: swap(1),
        )

    with jax.named_scope("pearly"):
        for kind in range(2):
            split(kind, 0)
        for i in range(AHEAD):
            for kind in range(2):
                keep[kind, i] = product(0, kind, i)

    with jax.named_scope("preduce"):
        for kind in range(2):
            split(kind, 1)
        lead = layers - 1
        for i in range(lead):
            prepare(i)
            leave(i)
        prepare(lead)
        for i in range(layers):
            for kind in range(2):
                again(i, kind)
            if i == 0:
                leave(lead)
            if i > 0:
                for kind in range(2):
                    deliver(i - 1, kind)
        for kind in range(2):
            deliver(layers - 1, kind)

    with jax.named_scope("psum"):
        for flip in range(2):
            vec = lax.rem(half + flip, 2)
            for kind in range(2):
                value = None
                if flip == 0:
                    mine = pl.ds(pl.multiple_of(half * rows, rows), rows)
                    value = keep[kind, place_of(z), y, x, mine]
                count = layers - 1 + flip
                got(parts.at[vec, kind, pl.ds(0, count)], parts_recv.at[vec, kind])
                for d in range(1 - flip, layers):
                    more = parts[vec, kind, lax.rem(z + d, layers)].astype(f32)
                    value = more if value is None else value + more
                block = pl.ds(pl.multiple_of(vec * middle + kind * part, 128), part)
                result[:, block] = value

    def rows_as(count):
        return panel.at[pl.ds(0, count * conduct // width), :]

    def pieces_as(count):
        return panel.at[pl.ds(0, count * height), :]

    with jax.named_scope("pend"):
        sent(pieces_as(CUTS + events * last), ACROSS)
        for k in range(layers):
            ends = (k == 0) + (k == layers - 1)
            onward = sum((o < k < layers - 1) or (0 < k < o) for o in table[k])
            count = (2 - ends + onward) * (CUTS + 1)
            pl.when(z == k)(functools.partial(sent, pieces_as(count), LAYERS))
            count = 1 + 2 * (2 - ends + 2) + 2 * (2 * events + onward) + 2 * layers
            pl.when(z == k)(functools.partial(sent, rows_as(count * rows), ROWS))
        sent(screened_out, SHARE)
        sent(psi.at[1], POINTS)
        sent(give, GIVE)
        sent(first_send, FIRST)
        sent(second_send, SECOND)
        sent(rows_as(2 * (2 * layers - 1) * rows * part // conduct), THIRD)


def write_out(result, out_hbm, sem):
    copy = pltpu.make_async_copy(result, out_hbm, sem)
    copy.start()
    copy.wait()


def fused(tiles, trial, psi_v, psi_c, screened):
    rows, conduct = trial.shape[1:]
    valence, points = psi_v.shape
    width = psi_c.shape[2]
    middle = conduct // 2
    part = middle // 2
    layers = tiles // 4
    slots = layers * 2
    bf16, f32 = jnp.bfloat16, jnp.float32
    far = pl.BlockSpec(memory_space=pl.ANY)
    dma = pltpu.SemaphoreType.DMA
    vmem = pltpu.VMEM
    out = pl.pallas_call(
        functools.partial(body, layers),
        out_shape=vmem((rows, conduct), f32),
        in_specs=[far] * 4,
        out_specs=pl.BlockSpec(memory_space=vmem),
        scratch_shapes=[
            vmem((valence, conduct), bf16),
            vmem((2, layers, 2, 2, 2 * rows, points), bf16),
            vmem((2, points, valence), bf16),
            vmem((slots, points, width), f32),
            vmem((slots, points, width), f32),
            vmem((slots, points, width), bf16),
            vmem((slots, points, width), bf16),
            vmem((slots * conduct, width), bf16),
            vmem((2, points, conduct), bf16),
            vmem((2, 2, points, middle), f32),
            vmem((2, 2, points, part), bf16),
            vmem((2, 2, points, part), bf16),
            vmem((2, layers, 2, 2 * rows, part), bf16),
            vmem((2, layers, 2, 2 * rows, part), bf16),
            vmem((2, layers, 2, 2, 2 * rows, part), f32),
            vmem((2, layers, 2 * rows, part), bf16),
            vmem((2, layers, 2 * rows, part), bf16),
            vmem((2, layers, 2 * rows, part), bf16),
            vmem((2, 2, layers, rows, part), bf16),
            dma((5,)),
            dma((9,)),
            dma((tiles,)),
            dma((1,)),
            dma((2,)),
            dma((slots,)),
            dma((slots, CUTS)),
            dma((2, 2)),
            dma((2, layers)),
            dma((2, layers)),
            dma((2, 2)),
        ],
        compiler_params=pltpu.CompilerParams(
            collective_id=0, has_side_effects=True, vmem_limit_bytes=58 * 1024 * 1024
        ),
    )(
        trial[0],
        psi_v.reshape(layers, 2, 2, 2 * rows, points),
        psi_c[:, 0, :],
        screened,
    )
    out = pl.pallas_call(
        write_out,
        out_shape=jax.ShapeDtypeStruct((rows, conduct), f32),
        in_specs=[pl.BlockSpec(memory_space=vmem)],
        out_specs=far,
        scratch_shapes=[dma(())],
        compiler_params=pltpu.CompilerParams(vmem_limit_bytes=1024 * 1024),
    )(out)
    return out[None]


def solution(mesh):
    tiles = mesh.shape["tile"]

    def shards(trial, psi_v, psi_c, screened):
        fits = (
            trial.shape[0] == 1
            and mesh.shape["vec"] == 2
            and tiles % 8 == 0
            and psi_v.shape[1] % 128 == 0
            and psi_c.shape[2] % 128 == 0
            and trial.shape[1] % 16 == 0
            and trial.shape[2] % 512 == 0
        )
        if fits:
            return fused(tiles, trial, psi_v, psi_c, screened)
        return plain(trial, psi_v, psi_c, screened)

    in_specs = (
        P(None, ("tile", "vec"), None),
        P(None, "tile"),
        P(None, "vec", "tile"),
        P("tile", "vec"),
    )
    out_specs = P(None, ("tile", "vec"), None)
    return jax.shard_map(shards, mesh=mesh, in_specs=in_specs, out_specs=out_specs, check_vma=False)
```

```python
import functools

import jax
import jax.numpy as jnp
from jax import lax
from jax.experimental import pallas as pl
from jax.experimental.pallas import tpu as pltpu
from jax.sharding import PartitionSpec as P

CUTS = 4
AHEAD = 2
ROWS, ACROSS, LAYERS, SHARE, POINTS, GIVE, FIRST, SECOND, THIRD = range(9)


def back_product(weighted_flat, panel):
    return lax.dot_general(
        weighted_flat, panel, (((1,), (1,)), ((), ())), preferred_element_type=jnp.float32
    )


def plain(trial, psi_v, psi_c, screened):
    count = trial.shape[0]
    points = psi_v.shape[1]
    conduct = trial.shape[2]
    whole = lax.all_gather(trial, ("tile", "vec"), axis=1, tiled=True)
    projected = jnp.einsum("vp,kvc->kpc", psi_v, whole, preferred_element_type=jnp.float32).astype(
        jnp.bfloat16
    )
    flat = projected.reshape(count * points, conduct)
    panel_local = psi_c[:, 0, :]
    panel = lax.all_gather(panel_local, "tile", axis=1, tiled=True)
    pair = jnp.dot(flat, panel, preferred_element_type=jnp.float32)
    weighted = (screened[None] * pair.reshape(count, points, -1)).astype(jnp.bfloat16)
    weighted_flat = weighted.reshape(count * points, -1)
    back = back_product(weighted_flat, panel)
    back = back.reshape(count, points, conduct)
    left = psi_v.astype(jnp.float32)
    summed = lax.psum(back, "vec")
    tiles = lax.axis_size("tile")
    halves = lax.axis_size("vec")
    owned = left.shape[0] // (tiles * halves)
    grouped = left.reshape(tiles, halves, owned, points)
    mine = lax.dynamic_index_in_dim(grouped, lax.axis_index("vec"), 1, keepdims=False).reshape(
        tiles * owned, points
    )
    pieces = []
    for one in range(count):
        term = jnp.dot(mine, summed[one], precision=lax.Precision.HIGHEST)
        pieces.append(lax.psum_scatter(term, "tile", scatter_dimension=0, tiled=True))
    return jnp.stack(pieces, axis=0)


def sources_of(layers):
    return [
        sorted((o for o in range(layers) if o != z), key=lambda o: (abs(o - z), o))
        for z in range(layers)
    ]


def outer_first(layers):
    return sorted(range(layers), key=lambda k: (-abs(2 * k - layers + 1), k))


def pick(values, at):
    chosen = jnp.int32(values[0])
    for k, value in enumerate(values[1:], 1):
        chosen = jnp.where(at == k, jnp.int32(value), chosen)
    return chosen


def body(
    layers,
    trial_hbm,
    psi_v_hbm,
    psi_c_hbm,
    screened_hbm,
    result,
    whole,
    psi,
    psi_t,
    stage,
    screened_own,
    screened_out,
    screened_in,
    panel,
    flat,
    back,
    give,
    take,
    first_send,
    first_got,
    keep,
    second_send,
    second_got,
    third,
    parts,
    local_sem,
    sends,
    trial_recv,
    hand_recv,
    psi_recv,
    screened_recv,
    block_recv,
    take_recv,
    first_recv,
    second_recv,
    parts_recv,
):
    bf16, f32 = jnp.bfloat16, jnp.float32
    me = lax.axis_index("tile")
    half = lax.axis_index("vec")
    other = 1 - half
    z, y, x = me // 4, (me // 2) % 2, me % 2
    across = lax.rem(y + 1, 2)
    aside = lax.rem(x + 1, 2)
    table = sources_of(layers)
    events = layers - 1
    source = [pick([row[e] for row in table], z) for e in range(events)]
    distance = [pick([abs(row[e] - k) for k, row in enumerate(table)], z) for e in range(events)]
    at_distance = [[distance[e] == k for k in range(layers)] for e in range(events)]

    ranks = outer_first(layers)

    def place_of(zz):
        return pick([ranks.index(k) for k in range(layers)], zz)

    def tile_of(zz, yy, xx):
        return zz * 4 + yy * 2 + xx

    mate_x, mate_y = tile_of(z, y, aside), tile_of(z, across, x)
    up, down = jnp.minimum(z + 1, layers - 1), jnp.maximum(z - 1, 0)
    has_up, has_down = z < layers - 1, z > 0
    at_end = (z == 0) | (z == layers - 1)
    on_up = [has_up & (source[e] < z) for e in range(events)]
    on_down = [has_down & (source[e] > z) for e in range(events)]

    def slot_of(zz, yy):
        return zz * 2 + yy

    slots = layers * 2
    order = [("own", 0)]
    for e in range(events - 1):
        order += [("z", e), ("y", e - 1)]
    order += [("y", events - 2), ("z", events - 1), ("y", events - 1)]

    def slot_at(kind, e):
        zz = source[e] if e >= 0 and kind != "own" else z
        return slot_of(zz, across if kind == "y" else y)

    turns = [slot_at(*event) for event in order]

    rows, conduct = trial_hbm.shape
    width = psi_c_hbm.shape[1]
    points = psi_v_hbm.shape[-1]
    middle = conduct // 2
    part = middle // 2
    height = psi_c_hbm.shape[0] // CUTS

    def lines(tile, vec):
        tile = place_of(tile // 4) * 4 + tile % 4
        start = pl.multiple_of((tile * 2 + vec) * rows, rows)
        return whole.at[pl.ds(start, rows), :]

    def columns(tile):
        return pl.ds(pl.multiple_of(tile * width, 128), width)

    def load(src, dst, sem):
        copy = pltpu.make_async_copy(src, dst, local_sem.at[sem])
        copy.start()
        return copy

    home_slot, mate_slot = slot_of(z, y), slot_of(z, across)

    def block_of(slot):
        return panel.at[pl.ds(pl.multiple_of(slot * conduct, conduct), conduct), :]

    load_rows = load(trial_hbm, lines(me, half), 0)
    for i, layer in enumerate(ranks):
        load(psi_v_hbm.at[layer], psi.at[0, i], 1)
    load_block = load(psi_c_hbm, block_of(home_slot), 2)

    def remote(src, dst, send, recv, tile, vec):
        return pltpu.make_async_remote_copy(
            src_ref=src,
            dst_ref=dst,
            send_sem=send,
            recv_sem=recv,
            device_id=(tile, vec),
            device_id_type=pl.DeviceIdType.MESH,
        )

    partners = [(mate_x, half, None), (mate_y, half, None), (me, other, None)]
    partners += [(tile_of(up, y, x), half, has_up), (tile_of(down, y, x), half, has_down)]
    with jax.named_scope("pbar"):
        barrier = pltpu.get_barrier_semaphore()

        def greet(tile, vec):
            pl.semaphore_signal(
                barrier, inc=1, device_id=(tile, vec), device_id_type=pl.DeviceIdType.MESH
            )

        for tile, vec, cond in partners:
            if cond is None:
                greet(tile, vec)
            else:
                pl.when(cond)(functools.partial(greet, tile, vec))
        for k in range(layers):
            count = 3 + (k > 0) + (k < layers - 1)
            pl.when(z == k)(functools.partial(pl.semaphore_wait, barrier, count))

    def send(src, dst, group, recv, tile, vec, cond=None):
        copy = remote(src, dst, sends.at[group], recv, tile, vec)
        if cond is None:
            copy.start()
        else:
            pl.when(cond)(copy.start)

    def sent(ref, group):
        remote(ref, ref, sends.at[group], psi_recv.at[0], me, other).wait_send()

    def got(ref, recv):
        remote(ref, ref, sends.at[0], recv, me, other).wait_recv()

    def piece(slot, s):
        start = pl.multiple_of(slot * conduct + s * height, height)
        return panel.at[pl.ds(start, height), :]

    def hand(tile):
        ref = lines(tile, half)
        send(ref, ref, ROWS, hand_recv.at[0], me, other)

    def spread(tile, to_up, to_down):
        ref = lines(tile, half)
        recv = trial_recv.at[tile]
        send(ref, ref, ROWS, recv, tile_of(up, y, x), half, to_up)
        send(ref, ref, ROWS, recv, tile_of(down, y, x), half, to_down)
        send(ref, ref, ROWS, recv, mate_y, half)
        hand(tile)

    last = CUTS - 1

    def along(slot, s, to_up, to_down):
        ref = piece(slot, s)
        recv = block_recv.at[slot, s]
        send(ref, ref, LAYERS, recv, tile_of(up, y, x), half, to_up)
        send(ref, ref, LAYERS, recv, tile_of(down, y, x), half, to_down)

    def cross(slot, s):
        ref = piece(slot, s)
        send(ref, ref, ACROSS, block_recv.at[slot, s], mate_y, half)

    def came(slot, s):
        got(piece(slot, s), block_recv.at[slot, s])

    pair_layers = layers // 2

    def psi_half(ref, which):
        return ref.at[pl.ds(which * pair_layers, pair_layers)]

    def take_piece(e, s):
        slot = slot_of(source[e], y)
        came(slot, s)
        along(slot, s, on_up[e], on_down[e])
        if s < last:
            cross(slot, s)

    def take_mate(e):
        slot = slot_of(source[e], across)
        came(slot, last)
        along(slot, last, on_up[e], on_down[e])

    def at_k(k):
        return [e for e in range(events) if any(abs(row[e] - r) == k for r, row in enumerate(table))]

    def arrive(k, first, final):
        for s in range(first, final):
            for e in at_k(k):
                pl.when(at_distance[e][k])(functools.partial(take_piece, e, s))
        if final == CUTS:
            for e in at_k(k):
                pl.when(at_distance[e][k])(functools.partial(take_mate, e))

    with jax.named_scope("ptrial"):
        ref = lines(me, half)
        load_rows.wait()
        send(ref, ref, ROWS, trial_recv.at[me], mate_x, half)
        spread(me, has_up, has_down)
        for i, turn in enumerate(turns):
            load(screened_hbm.at[:, columns(turn * 2 + aside)], stage.at[i], 3)
        for i, turn in enumerate(turns):
            load(screened_hbm.at[:, columns(turn * 2 + x)], screened_own.at[i], 4)
        pltpu.make_async_copy(psi_v_hbm, psi.at[0], local_sem.at[1]).wait()
        ref = psi_half(psi.at[0], half)
        send(ref, psi_half(psi.at[1], half), POINTS, psi_recv.at[0], mate_x, half)
        got(lines(mate_x, half), trial_recv.at[mate_x])
        spread(mate_x, has_up, has_down)
        load_block.wait()
        cross(home_slot, last)

        pltpu.make_async_copy(stage, stage, local_sem.at[3]).wait()
        for i in range(slots):
            screened_out[i] = stage[i].astype(bf16)
        for i in range(slots):
            send(screened_out.at[i], screened_in.at[i], SHARE, screened_recv.at[i], mate_x, half)

        for e in range(events):
            for xx in range(2):
                tile = tile_of(source[e], y, xx)
                got(lines(tile, half), trial_recv.at[tile])
                spread(tile, on_up[e], on_down[e])
            if e == events - 2:
                cross(home_slot, 0)
                for s in range(CUTS):
                    if s < CUTS // 2:
                        along(home_slot, s, has_up, has_down)
                    else:
                        along(home_slot, s, has_up & at_end, has_down & at_end)
        if events > 1:
            for s in range(CUTS // 2, CUTS):
                along(home_slot, s, has_up & ~at_end, has_down & ~at_end)
        else:
            for s in range(CUTS):
                along(home_slot, s, has_up, has_down)
        for s in range(1 if events > 1 else 0, last):
            cross(home_slot, s)

        back[...] = jnp.zeros_like(back)
        valence = layers * 4 * 2 * rows
        psi_t[0] = psi[0].reshape(valence, points).T

        came(mate_slot, last)
        along(mate_slot, last, has_up, has_down)
        arrive(1, 0, CUTS // 2)
        for e in range(-1, events):
            for xx in range(2):
                tile = tile_of(source[e] if e >= 0 else z, across, xx)
                got(lines(tile, half), trial_recv.at[tile])
                hand(tile)

        ref = psi_half(psi.at[1], half)
        got(ref, psi_recv.at[0])
        send(ref, ref, POINTS, psi_recv.at[1], me, other)
        arrive(1, CUTS // 2, CUTS)
        got(whole.at[pl.ds(0, layers * 4 * rows), :], hand_recv.at[0])

    wide = 256

    def project(p):
        def chunk(j, carry):
            cols = pl.ds(pl.multiple_of(j * wide, wide), wide)
            flat[p, :, cols] = jnp.dot(
                psi_t[p], whole[:, cols], preferred_element_type=f32
            ).astype(bf16)
            return carry

        lax.fori_loop(0, conduct // wide, chunk, 0)

    with jax.named_scope("pproj"):
        project(0)
        got(psi_half(psi.at[1], other), psi_recv.at[1])
        psi_t[1] = psi[1].reshape(valence, points).T
        project(1)

    turn_of = {e + 1: i for i, (kind, e) in enumerate(order) if kind == "z" and e > 0}

    def receive(i):
        kind, e = order[i]
        if kind == "z" and e > 0:
            arrive(e + 1, last, CUTS)
        if kind == "y":
            for s in range(last):
                came(turns[i], s)

    def between(i):
        for k, turn in turn_of.items():
            if i == turn - 2:
                arrive(k, 0, CUTS // 2)
            if i == turn - 1:
                arrive(k, CUTS // 2, last)

    def step(p, share, slot, ready=None, done=None):
        block = block_of(slot)
        pair = jnp.dot(flat[p], block[...], preferred_element_type=f32)
        if ready is not None:
            ready()
        weighted = (share().astype(f32) * pair).astype(bf16)
        for h in range(2):
            back[p, h] += back_product(weighted, block[pl.ds(h * middle, middle), :])
            if done is not None:
                done(h)

    pltpu.make_async_copy(screened_own, screened_own, local_sem.at[4]).wait()

    def use(k, carry):
        slot = turns[0]
        for i in range(final):
            slot = jnp.where(k == i, turns[i], slot)
            pl.when(k == i)(functools.partial(receive, i))
        step(0, lambda: screened_own[k], slot)
        for i in range(final):
            pl.when(k == i)(functools.partial(between, i))
        got(screened_in.at[k], screened_recv.at[k])
        step(1, lambda: screened_in[k], slot)
        return carry

    final = slots - 1
    with jax.named_scope("puse"):
        lax.fori_loop(0, final, use, 0)
        receive(final)
        step(0, lambda: screened_own[final], turns[final])

    def span(kind):
        return pl.ds(kind * part, part)

    def swap(p):
        for kind in range(2):
            give[kind, p] = back[p, other, :, span(kind)].astype(bf16)
            send(give.at[kind, p], take.at[kind, p], GIVE, take_recv.at[kind, p], me, other)

    def split(kind, p):
        got(take.at[kind, p], take_recv.at[kind, p])
        total = back[p, half, :, span(kind)] + take[kind, p].astype(f32)
        high = total.astype(bf16)
        flat[p, :, span(kind)] = high
        low = (total - high.astype(f32)).astype(bf16)
        flat[p, :, pl.ds(middle + kind * part, part)] = low

    block_rows = 2 * rows

    def product(p, kind, i):
        left = psi[p, i].reshape(4 * block_rows, points)
        total = None
        for level in range(2):
            cols = pl.ds(level * middle + kind * part, part)
            value = jnp.dot(left, flat[p, :, cols], preferred_element_type=f32)
            total = value if total is None else total + value
        return total.reshape(2, 2, block_rows, part)

    def prepare(i):
        for kind in range(2):
            if i < AHEAD:
                keep[kind, i] += product(1, kind, i)
            else:
                keep[kind, i] = product(0, kind, i) + product(1, kind, i)
        for kind in range(2):
            if kind == 0:
                away = keep[kind, i, :, pl.ds(aside, 1)]
            else:
                away = keep[kind, i, pl.ds(across, 1)]
            first_send[kind, i] = away.reshape(2, block_rows, part).astype(bf16)

    def leave(i):
        for kind in range(2):
            ref = first_send.at[kind, i]
            recv = first_recv.at[kind, i]
            send(ref, first_got.at[kind, i], FIRST, recv, [mate_x, mate_y][kind], half)

    def again(i, kind):
        got(first_got.at[kind, i], first_recv.at[kind, i])
        yy, xx = [(across, x), (y, aside)][kind]
        away = [across, aside][kind]
        value = keep[kind, i, yy, xx] + first_got[kind, i, away].astype(f32)
        second_send[kind, i] = value.astype(bf16)
        ref = second_send.at[kind, i]
        recv = second_recv.at[kind, i]
        send(ref, second_got.at[kind, i], SECOND, recv, [mate_y, mate_x][kind], half)
        keep[kind, i, y, x] += first_got[kind, i, [y, x][kind]].astype(f32)

    def deliver(i, kind):
        got(second_got.at[kind, i], second_recv.at[kind, i])
        value = keep[kind, i, y, x] + second_got[kind, i].astype(f32)
        keep[kind, i, y, x] = value
        third[kind, i] = value.astype(bf16)
        layer = ranks[i]
        for v in range(2):
            send(
                third.at[kind, i, pl.ds(v * rows, rows)],
                parts.at[half, kind, z],
                THIRD,
                parts_recv.at[half, kind],
                tile_of(layer, y, x),
                v,
                (z != layer) | (half != v),
            )

    def early():
        for kind in range(2):
            split(kind, 0)
        for i in range(AHEAD):
            for kind in range(2):
                keep[kind, i] = product(0, kind, i)

    with jax.named_scope("plast"):
        swap(0)
        pl.when(half == 0)(early)
        step(
            1,
            lambda: screened_in[final],
            turns[final],
            lambda: got(screened_in.at[final], screened_recv.at[final]),
            lambda h: pl.when(half != h)(functools.partial(swap, 1)),
        )

    with jax.named_scope("pearly"):
        pl.when(half == 1)(early)

    with jax.named_scope("preduce"):
        for kind in range(2):
            split(kind, 1)
        lead = layers - 1
        for i in range(lead):
            prepare(i)
            leave(i)
        prepare(lead)
        for i in range(layers):
            for kind in range(2):
                again(i, kind)
            if i == 0:
                leave(lead)
            if i > 0:
                for kind in range(2):
                    deliver(i - 1, kind)
        for kind in range(2):
            deliver(layers - 1, kind)

    with jax.named_scope("psum"):
        for flip in range(2):
            vec = lax.rem(half + flip, 2)
            for kind in range(2):
                value = None
                if flip == 0:
                    mine = pl.ds(pl.multiple_of(half * rows, rows), rows)
                    value = keep[kind, place_of(z), y, x, mine]
                count = layers - 1 + flip
                got(parts.at[vec, kind, pl.ds(0, count)], parts_recv.at[vec, kind])
                for d in range(1 - flip, layers):
                    more = parts[vec, kind, lax.rem(z + d, layers)].astype(f32)
                    value = more if value is None else value + more
                block = pl.ds(pl.multiple_of(vec * middle + kind * part, 128), part)
                result[:, block] = value

    def rows_as(count):
        return panel.at[pl.ds(0, count * conduct // width), :]

    def pieces_as(count):
        return panel.at[pl.ds(0, count * height), :]

    with jax.named_scope("pend"):
        sent(pieces_as(CUTS + events * last), ACROSS)
        for k in range(layers):
            ends = (k == 0) + (k == layers - 1)
            onward = sum((o < k < layers - 1) or (0 < k < o) for o in table[k])
            count = (2 - ends + onward) * (CUTS + 1)
            pl.when(z == k)(functools.partial(sent, pieces_as(count), LAYERS))
            count = 1 + 2 * (2 - ends + 2) + 2 * (2 * events + onward) + 2 * layers
            pl.when(z == k)(functools.partial(sent, rows_as(count * rows), ROWS))
        sent(screened_out, SHARE)
        sent(psi.at[1], POINTS)
        sent(give, GIVE)
        sent(first_send, FIRST)
        sent(second_send, SECOND)
        sent(rows_as(2 * (2 * layers - 1) * rows * part // conduct), THIRD)


def write_out(result, out_hbm, sem):
    copy = pltpu.make_async_copy(result, out_hbm, sem)
    copy.start()
    copy.wait()


def fused(tiles, trial, psi_v, psi_c, screened):
    rows, conduct = trial.shape[1:]
    valence, points = psi_v.shape
    width = psi_c.shape[2]
    middle = conduct // 2
    part = middle // 2
    layers = tiles // 4
    slots = layers * 2
    bf16, f32 = jnp.bfloat16, jnp.float32
    far = pl.BlockSpec(memory_space=pl.ANY)
    dma = pltpu.SemaphoreType.DMA
    vmem = pltpu.VMEM
    out = pl.pallas_call(
        functools.partial(body, layers),
        out_shape=vmem((rows, conduct), f32),
        in_specs=[far] * 4,
        out_specs=pl.BlockSpec(memory_space=vmem),
        scratch_shapes=[
            vmem((valence, conduct), bf16),
            vmem((2, layers, 2, 2, 2 * rows, points), bf16),
            vmem((2, points, valence), bf16),
            vmem((slots, points, width), f32),
            vmem((slots, points, width), f32),
            vmem((slots, points, width), bf16),
            vmem((slots, points, width), bf16),
            vmem((slots * conduct, width), bf16),
            vmem((2, points, conduct), bf16),
            vmem((2, 2, points, middle), f32),
            vmem((2, 2, points, part), bf16),
            vmem((2, 2, points, part), bf16),
            vmem((2, layers, 2, 2 * rows, part), bf16),
            vmem((2, layers, 2, 2 * rows, part), bf16),
            vmem((2, layers, 2, 2, 2 * rows, part), f32),
            vmem((2, layers, 2 * rows, part), bf16),
            vmem((2, layers, 2 * rows, part), bf16),
            vmem((2, layers, 2 * rows, part), bf16),
            vmem((2, 2, layers, rows, part), bf16),
            dma((5,)),
            dma((9,)),
            dma((tiles,)),
            dma((1,)),
            dma((2,)),
            dma((slots,)),
            dma((slots, CUTS)),
            dma((2, 2)),
            dma((2, layers)),
            dma((2, layers)),
            dma((2, 2)),
        ],
        compiler_params=pltpu.CompilerParams(
            collective_id=0, has_side_effects=True, vmem_limit_bytes=58 * 1024 * 1024
        ),
    )(
        trial[0],
        psi_v.reshape(layers, 2, 2, 2 * rows, points),
        psi_c[:, 0, :],
        screened,
    )
    out = pl.pallas_call(
        write_out,
        out_shape=jax.ShapeDtypeStruct((rows, conduct), f32),
        in_specs=[pl.BlockSpec(memory_space=vmem)],
        out_specs=far,
        scratch_shapes=[dma(())],
        compiler_params=pltpu.CompilerParams(vmem_limit_bytes=1024 * 1024),
    )(out)
    return out[None]


def solution(mesh):
    tiles = mesh.shape["tile"]

    def shards(trial, psi_v, psi_c, screened):
        fits = (
            trial.shape[0] == 1
            and mesh.shape["vec"] == 2
            and tiles % 8 == 0
            and psi_v.shape[1] % 128 == 0
            and psi_c.shape[2] % 128 == 0
            and trial.shape[1] % 16 == 0
            and trial.shape[2] % 512 == 0
        )
        if fits:
            return fused(tiles, trial, psi_v, psi_c, screened)
        return plain(trial, psi_v, psi_c, screened)

    in_specs = (
        P(None, ("tile", "vec"), None),
        P(None, "tile"),
        P(None, "vec", "tile"),
        P("tile", "vec"),
    )
    out_specs = P(None, ("tile", "vec"), None)
    return jax.shard_map(shards, mesh=mesh, in_specs=in_specs, out_specs=out_specs, check_vma=False)
```

```python
import functools

import jax
import jax.numpy as jnp
from jax import lax
from jax.experimental import pallas as pl
from jax.experimental.pallas import tpu as pltpu
from jax.sharding import PartitionSpec as P

CUTS = 4
AHEAD = 2
ROWS, ACROSS, LAYERS, SHARE, POINTS, GIVE, FIRST, SECOND, THIRD = range(9)


def back_product(weighted_flat, panel):
    return lax.dot_general(
        weighted_flat, panel, (((1,), (1,)), ((), ())), preferred_element_type=jnp.float32
    )


def plain(trial, psi_v, psi_c, screened):
    count = trial.shape[0]
    points = psi_v.shape[1]
    conduct = trial.shape[2]
    whole = lax.all_gather(trial, ("tile", "vec"), axis=1, tiled=True)
    projected = jnp.einsum("vp,kvc->kpc", psi_v, whole, preferred_element_type=jnp.float32).astype(
        jnp.bfloat16
    )
    flat = projected.reshape(count * points, conduct)
    panel_local = psi_c[:, 0, :]
    panel = lax.all_gather(panel_local, "tile", axis=1, tiled=True)
    pair = jnp.dot(flat, panel, preferred_element_type=jnp.float32)
    weighted = (screened[None] * pair.reshape(count, points, -1)).astype(jnp.bfloat16)
    weighted_flat = weighted.reshape(count * points, -1)
    back = back_product(weighted_flat, panel)
    back = back.reshape(count, points, conduct)
    left = psi_v.astype(jnp.float32)
    summed = lax.psum(back, "vec")
    tiles = lax.axis_size("tile")
    halves = lax.axis_size("vec")
    owned = left.shape[0] // (tiles * halves)
    grouped = left.reshape(tiles, halves, owned, points)
    mine = lax.dynamic_index_in_dim(grouped, lax.axis_index("vec"), 1, keepdims=False).reshape(
        tiles * owned, points
    )
    pieces = []
    for one in range(count):
        term = jnp.dot(mine, summed[one], precision=lax.Precision.HIGHEST)
        pieces.append(lax.psum_scatter(term, "tile", scatter_dimension=0, tiled=True))
    return jnp.stack(pieces, axis=0)


def sources_of(layers):
    return [
        sorted((o for o in range(layers) if o != z), key=lambda o: (abs(o - z), o))
        for z in range(layers)
    ]


def outer_first(layers):
    return sorted(range(layers), key=lambda k: (-abs(2 * k - layers + 1), k))


def pick(values, at):
    chosen = jnp.int32(values[0])
    for k, value in enumerate(values[1:], 1):
        chosen = jnp.where(at == k, jnp.int32(value), chosen)
    return chosen


def body(
    layers,
    trial_hbm,
    psi_v_hbm,
    psi_c_hbm,
    screened_hbm,
    result,
    whole,
    psi,
    psi_t,
    stage,
    screened_own,
    screened_out,
    screened_in,
    panel,
    flat,
    pair,
    back,
    give,
    take,
    first_send,
    first_got,
    keep,
    final_sum,
    second_send,
    second_got,
    third,
    parts,
    local_sem,
    sends,
    trial_recv,
    hand_recv,
    psi_recv,
    screened_recv,
    block_recv,
    take_recv,
    first_recv,
    second_recv,
    parts_recv,
):
    bf16, f32 = jnp.bfloat16, jnp.float32
    me = lax.axis_index("tile")
    half = lax.axis_index("vec")
    other = 1 - half
    z, y, x = me // 4, (me // 2) % 2, me % 2
    across = lax.rem(y + 1, 2)
    aside = lax.rem(x + 1, 2)
    table = sources_of(layers)
    events = layers - 1
    source = [pick([row[e] for row in table], z) for e in range(events)]
    distance = [pick([abs(row[e] - k) for k, row in enumerate(table)], z) for e in range(events)]
    at_distance = [[distance[e] == k for k in range(layers)] for e in range(events)]

    ranks = outer_first(layers)

    def place_of(zz):
        return pick([ranks.index(k) for k in range(layers)], zz)

    def tile_of(zz, yy, xx):
        return zz * 4 + yy * 2 + xx

    mate_x, mate_y = tile_of(z, y, aside), tile_of(z, across, x)
    up, down = jnp.minimum(z + 1, layers - 1), jnp.maximum(z - 1, 0)
    has_up, has_down = z < layers - 1, z > 0
    at_end = (z == 0) | (z == layers - 1)
    on_up = [has_up & (source[e] < z) for e in range(events)]
    on_down = [has_down & (source[e] > z) for e in range(events)]

    def slot_of(zz, yy):
        return zz * 2 + yy

    slots = layers * 2
    final = slots - 1
    order = [("own", 0)]
    for e in range(events - 1):
        order += [("z", e), ("y", e - 1)]
    order += [("y", events - 2), ("z", events - 1), ("y", events - 1)]

    def slot_at(kind, e):
        zz = source[e] if e >= 0 and kind != "own" else z
        return slot_of(zz, across if kind == "y" else y)

    turns = [slot_at(*event) for event in order]

    rows, conduct = trial_hbm.shape
    width = psi_c_hbm.shape[1]
    points = psi_v_hbm.shape[-1]
    middle = conduct // 2
    part = middle // 2
    height = psi_c_hbm.shape[0] // CUTS

    def lines(tile, vec):
        place = place_of(tile // 4)
        place = ((place // 2) * 2 + vec) * 2 + place % 2
        start = pl.multiple_of((place * 4 + tile % 4) * rows, rows)
        return whole.at[pl.ds(start, rows), :]

    def columns(tile):
        return pl.ds(pl.multiple_of(tile * width, 128), width)

    def load(src, dst, sem):
        copy = pltpu.make_async_copy(src, dst, local_sem.at[sem])
        copy.start()
        return copy

    home_slot, mate_slot = slot_of(z, y), slot_of(z, across)

    def block_of(slot):
        return panel.at[pl.ds(pl.multiple_of(slot * conduct, conduct), conduct), :]

    load_rows = load(trial_hbm, lines(me, half), 0)
    for i, layer in enumerate(ranks):
        for v in range(2):
            load(psi_v_hbm.at[layer, :, :, v], psi.at[0, i // 2 * 2 + v, i % 2], 1)
    load_block = load(psi_c_hbm, block_of(home_slot), 2)

    def low_or_high(r):
        return pl.ds(r * (points // 2), points // 2)

    def remote(src, dst, send, recv, tile, vec):
        return pltpu.make_async_remote_copy(
            src_ref=src,
            dst_ref=dst,
            send_sem=send,
            recv_sem=recv,
            device_id=(tile, vec),
            device_id_type=pl.DeviceIdType.MESH,
        )

    partners = [(mate_x, half, None), (mate_y, half, None), (me, other, None)]
    partners += [(tile_of(up, y, x), half, has_up), (tile_of(down, y, x), half, has_down)]
    with jax.named_scope("pbar"):
        barrier = pltpu.get_barrier_semaphore()

        def greet(tile, vec):
            pl.semaphore_signal(
                barrier, inc=1, device_id=(tile, vec), device_id_type=pl.DeviceIdType.MESH
            )

        for tile, vec, cond in partners:
            if cond is None:
                greet(tile, vec)
            else:
                pl.when(cond)(functools.partial(greet, tile, vec))
        for k in range(layers):
            count = 3 + (k > 0) + (k < layers - 1)
            pl.when(z == k)(functools.partial(pl.semaphore_wait, barrier, count))

    def send(src, dst, group, recv, tile, vec, cond=None):
        copy = remote(src, dst, sends.at[group], recv, tile, vec)
        if cond is None:
            copy.start()
        else:
            pl.when(cond)(copy.start)

    def sent(ref, group):
        remote(ref, ref, sends.at[group], psi_recv.at[0], me, other).wait_send()

    def got(ref, recv):
        remote(ref, ref, sends.at[0], recv, me, other).wait_recv()

    def piece(slot, s):
        start = pl.multiple_of(slot * conduct + s * height, height)
        return panel.at[pl.ds(start, height), :]

    def hand(tile):
        ref = lines(tile, half)
        send(ref, ref, ROWS, hand_recv.at[0], me, other)

    def spread(tile, to_up, to_down):
        ref = lines(tile, half)
        recv = trial_recv.at[tile]
        send(ref, ref, ROWS, recv, tile_of(up, y, x), half, to_up)
        send(ref, ref, ROWS, recv, tile_of(down, y, x), half, to_down)
        send(ref, ref, ROWS, recv, mate_y, half)
        hand(tile)

    last = CUTS - 1

    def along(slot, s, to_up, to_down):
        ref = piece(slot, s)
        recv = block_recv.at[slot, s]
        send(ref, ref, LAYERS, recv, tile_of(up, y, x), half, to_up)
        send(ref, ref, LAYERS, recv, tile_of(down, y, x), half, to_down)

    def cross(slot, s):
        ref = piece(slot, s)
        send(ref, ref, ACROSS, block_recv.at[slot, s], mate_y, half)

    def came(slot, s):
        got(piece(slot, s), block_recv.at[slot, s])

    pair_layers = layers // 2

    def psi_half(ref, which):
        return ref.at[pl.ds(which * pair_layers, pair_layers)]

    def take_piece(e, s):
        slot = slot_of(source[e], y)
        came(slot, s)
        along(slot, s, on_up[e], on_down[e])
        if s < last:
            cross(slot, s)

    def take_mate(e):
        slot = slot_of(source[e], across)
        came(slot, last)
        along(slot, last, on_up[e], on_down[e])

    def at_k(k):
        return [e for e in range(events) if any(abs(row[e] - r) == k for r, row in enumerate(table))]

    def arrive(k, first, final):
        for s in range(first, final):
            for e in at_k(k):
                pl.when(at_distance[e][k])(functools.partial(take_piece, e, s))
        if final == CUTS:
            for e in at_k(k):
                pl.when(at_distance[e][k])(functools.partial(take_mate, e))

    with jax.named_scope("ptrial"):
        ref = lines(me, half)
        load_rows.wait()
        send(ref, ref, ROWS, trial_recv.at[me], mate_x, half)
        spread(me, has_up, has_down)
        for i, turn in enumerate(turns):
            load(screened_hbm.at[:, columns(turn * 2 + aside)], stage.at[i], 3)
        for i, turn in enumerate(turns):
            load(screened_hbm.at[:, columns(turn * 2 + x)], screened_own.at[i], 4)
        pltpu.make_async_copy(psi.at[0], psi.at[0], local_sem.at[1]).wait()
        ref = psi_half(psi.at[0], half)
        send(ref, psi_half(psi.at[1], half), POINTS, psi_recv.at[0], mate_x, half)
        got(lines(mate_x, half), trial_recv.at[mate_x])
        spread(mate_x, has_up, has_down)
        load_block.wait()
        cross(home_slot, last)
        along(home_slot, 0, has_up, has_down)

        pltpu.make_async_copy(stage, stage, local_sem.at[3]).wait()
        for i in range(slots):
            screened_out[i] = stage[i].astype(bf16)
        for i in range(final):
            send(screened_out.at[i], screened_in.at[i], SHARE, screened_recv.at[i], mate_x, half)
        for r in range(2):
            src, dst = screened_out.at[final, low_or_high(r)], screened_in.at[final, low_or_high(r)]
            send(src, dst, SHARE, screened_recv.at[final + r], mate_x, half)

        for e in range(events):
            for xx in range(2):
                tile = tile_of(source[e], y, xx)
                got(lines(tile, half), trial_recv.at[tile])
                spread(tile, on_up[e], on_down[e])
            if e == events - 2:
                cross(home_slot, 0)
                for s in range(1, CUTS):
                    if s < CUTS // 2:
                        along(home_slot, s, has_up, has_down)
                    else:
                        along(home_slot, s, has_up & at_end, has_down & at_end)
        if events > 1:
            for s in range(CUTS // 2, CUTS):
                along(home_slot, s, has_up & ~at_end, has_down & ~at_end)
        else:
            for s in range(1, CUTS):
                along(home_slot, s, has_up, has_down)
        for s in range(1 if events > 1 else 0, last):
            cross(home_slot, s)

        back[...] = jnp.zeros_like(back)
        valence = layers * 4 * 2 * rows
        psi_t[0] = psi[0].reshape(valence, points).T

        came(mate_slot, last)
        along(mate_slot, last, has_up, has_down)
        arrive(1, 0, CUTS // 2)
        for e in range(-1, events):
            for xx in range(2):
                tile = tile_of(source[e] if e >= 0 else z, across, xx)
                got(lines(tile, half), trial_recv.at[tile])
                hand(tile)

        ref = psi_half(psi.at[1], half)
        got(ref, psi_recv.at[0])
        send(ref, ref, POINTS, psi_recv.at[1], me, other)
        arrive(1, CUTS // 2, CUTS)
        got(whole.at[pl.ds(0, layers * 4 * rows), :], hand_recv.at[0])

    wide = 256

    def project(p):
        def chunk(j, carry):
            cols = pl.ds(pl.multiple_of(j * wide, wide), wide)
            flat[p, :, cols] = jnp.dot(
                psi_t[p], whole[:, cols], preferred_element_type=f32
            ).astype(bf16)
            return carry

        lax.fori_loop(0, conduct // wide, chunk, 0)

    with jax.named_scope("pproj"):
        project(0)
        got(psi_half(psi.at[1], other), psi_recv.at[1])
        psi_t[1] = psi[1].reshape(valence, points).T
        project(1)

    turn_of = {e + 1: i for i, (kind, e) in enumerate(order) if kind == "z" and e > 0}

    def receive(i):
        kind, e = order[i]
        if kind == "z" and e > 0:
            arrive(e + 1, last, CUTS)
        if kind == "y":
            for s in range(last):
                came(turns[i], s)

    def between(i):
        for k, turn in turn_of.items():
            if i == turn - 2:
                arrive(k, 0, CUTS // 2)
            if i == turn - 1:
                arrive(k, CUTS // 2, last)

    def step(p, share, slot):
        block = block_of(slot)
        product = jnp.dot(flat[p], block[...], preferred_element_type=f32)
        weighted = (share.astype(f32) * product).astype(bf16)
        for h in range(2):
            back[p, h] += back_product(weighted, block[pl.ds(h * middle, middle), :])

    def last_step():
        block = block_of(turns[final])
        pair[...] = jnp.dot(flat[1], block[...], preferred_element_type=f32)
        for r in range(2):
            ref = screened_in.at[final, low_or_high(r)]
            got(ref, screened_recv.at[final + r])
            weighted = (ref[...].astype(f32) * pair[low_or_high(r)]).astype(bf16)
            for h in range(2):
                back[1, h, low_or_high(r)] += back_product(
                    weighted, block[pl.ds(h * middle, middle), :]
                )
                if r == 1:
                    pl.when(half != h)(functools.partial(swap, 1))

    pltpu.make_async_copy(screened_own, screened_own, local_sem.at[4]).wait()

    def use(k, carry):
        slot = turns[0]
        for i in range(final):
            slot = jnp.where(k == i, turns[i], slot)
            pl.when(k == i)(functools.partial(receive, i))
        step(0, screened_own[k], slot)
        for i in range(final):
            pl.when(k == i)(functools.partial(between, i))
        got(screened_in.at[k], screened_recv.at[k])
        step(1, screened_in[k], slot)
        return carry

    with jax.named_scope("puse"):
        lax.fori_loop(0, final, use, 0)
        receive(final)
        step(0, screened_own[final], turns[final])

    def span(kind):
        return pl.ds(kind * part, part)

    def swap(p):
        for kind in range(2):
            give[kind, p] = back[p, other, :, span(kind)].astype(bf16)
            send(give.at[kind, p], take.at[kind, p], GIVE, take_recv.at[kind, p], me, other)

    def split(kind, p):
        got(take.at[kind, p], take_recv.at[kind, p])
        total = back[p, half, :, span(kind)] + take[kind, p].astype(f32)
        high = total.astype(bf16)
        flat[p, :, span(kind)] = high
        low = (total - high.astype(f32)).astype(bf16)
        flat[p, :, pl.ds(middle + kind * part, part)] = low

    def product(p, kind, i):
        left = psi[p, i].reshape(8 * rows, points)
        total = None
        for level in range(2):
            cols = pl.ds(level * middle + kind * part, part)
            value = jnp.dot(left, flat[p, :, cols], preferred_element_type=f32)
            total = value if total is None else total + value
        return total.reshape(2, 2, 2, rows, part)

    def prepare(i, kind):
        if i < AHEAD:
            keep[kind, i] += product(1, kind, i)
        else:
            keep[kind, i] = product(0, kind, i) + product(1, kind, i)
        if kind == 0:
            away = keep[kind, i, :, :, pl.ds(aside, 1)]
        else:
            away = keep[kind, i, :, pl.ds(across, 1)]
        first_send[kind, i] = away.reshape(2, 2, rows, part).astype(bf16)

    def leave(i, kind):
        ref = first_send.at[kind, i]
        recv = first_recv.at[kind, i]
        send(ref, first_got.at[kind, i], FIRST, recv, [mate_x, mate_y][kind], half)

    def again(i, kind):
        got(first_got.at[kind, i], first_recv.at[kind, i])
        yy, xx = [(across, x), (y, aside)][kind]
        away, home = [(across, y), (aside, x)][kind]
        value = keep[kind, i, :, yy, xx] + first_got[kind, i, :, away].astype(f32)
        second_send[kind, i] = value.astype(bf16)
        ref = second_send.at[kind, i]
        recv = second_recv.at[kind, i]
        send(ref, second_got.at[kind, i], SECOND, recv, [mate_y, mate_x][kind], half)
        final_sum[kind, i] = keep[kind, i, :, y, x] + first_got[kind, i, :, home].astype(f32)

    def deliver(i, kind):
        got(second_got.at[kind, i], second_recv.at[kind, i])
        value = final_sum[kind, i] + second_got[kind, i].astype(f32)
        final_sum[kind, i] = value
        third[kind, i] = value.astype(bf16)
        for side in range(2):
            layer, v = ranks[i // 2 * 2 + side], i % 2
            send(
                third.at[kind, i, side],
                parts.at[half, kind, z],
                THIRD,
                parts_recv.at[half, kind],
                tile_of(layer, y, x),
                v,
                (z != layer) | (half != v),
            )

    def early():
        for kind in range(2):
            split(kind, 0)
        for i in range(AHEAD):
            for kind in range(2):
                keep[kind, i] = product(0, kind, i)

    with jax.named_scope("plast"):
        swap(0)
        pl.when(half == 0)(early)
        last_step()

    with jax.named_scope("pearly"):
        pl.when(half == 1)(early)

    with jax.named_scope("preduce"):
        for kind in range(2):
            split(kind, 1)
            prepare(0, kind)
            leave(0, kind)
        lead = layers - 1
        for i in range(1, layers):
            for kind in range(2):
                prepare(i, kind)
            if i < lead:
                for kind in range(2):
                    leave(i, kind)
        for i in range(layers):
            for kind in range(2):
                again(i, kind)
            if i == 0:
                for kind in range(2):
                    leave(lead, kind)
            if i > 0:
                for kind in range(2):
                    deliver(i - 1, kind)
        for kind in range(2):
            deliver(layers - 1, kind)

    with jax.named_scope("psum"):
        for flip in range(2):
            vec = lax.rem(half + flip, 2)
            for kind in range(2):
                value = None
                if flip == 0:
                    place = place_of(z)
                    value = final_sum[kind, (place // 2) * 2 + half, place % 2]
                count = layers - 1 + flip
                got(parts.at[vec, kind, pl.ds(0, count)], parts_recv.at[vec, kind])
                for d in range(1 - flip, layers):
                    more = parts[vec, kind, lax.rem(z + d, layers)].astype(f32)
                    value = more if value is None else value + more
                block = pl.ds(pl.multiple_of(vec * middle + kind * part, 128), part)
                result[:, block] = value

    def rows_as(count):
        return panel.at[pl.ds(0, count * conduct // width), :]

    def pieces_as(count):
        return panel.at[pl.ds(0, count * height), :]

    with jax.named_scope("pend"):
        sent(pieces_as(CUTS + events * last), ACROSS)
        for k in range(layers):
            ends = (k == 0) + (k == layers - 1)
            onward = sum((o < k < layers - 1) or (0 < k < o) for o in table[k])
            count = (2 - ends + onward) * (CUTS + 1)
            pl.when(z == k)(functools.partial(sent, pieces_as(count), LAYERS))
            count = 1 + 2 * (2 - ends + 2) + 2 * (2 * events + onward) + 2 * layers
            pl.when(z == k)(functools.partial(sent, rows_as(count * rows), ROWS))
        sent(screened_out, SHARE)
        sent(psi.at[1], POINTS)
        sent(give, GIVE)
        sent(first_send, FIRST)
        sent(second_send, SECOND)
        sent(rows_as(2 * (2 * layers - 1) * rows * part // conduct), THIRD)


def write_out(result, out_hbm, sem):
    copy = pltpu.make_async_copy(result, out_hbm, sem)
    copy.start()
    copy.wait()


def fused(tiles, trial, psi_v, psi_c, screened):
    rows, conduct = trial.shape[1:]
    valence, points = psi_v.shape
    width = psi_c.shape[2]
    middle = conduct // 2
    part = middle // 2
    layers = tiles // 4
    slots = layers * 2
    bf16, f32 = jnp.bfloat16, jnp.float32
    far = pl.BlockSpec(memory_space=pl.ANY)
    dma = pltpu.SemaphoreType.DMA
    vmem = pltpu.VMEM
    out = pl.pallas_call(
        functools.partial(body, layers),
        out_shape=vmem((rows, conduct), f32),
        in_specs=[far] * 4,
        out_specs=pl.BlockSpec(memory_space=vmem),
        scratch_shapes=[
            vmem((valence, conduct), bf16),
            vmem((2, layers, 2, 2, 2, rows, points), bf16),
            vmem((2, points, valence), bf16),
            vmem((slots, points, width), f32),
            vmem((slots, points, width), f32),
            vmem((slots, points, width), bf16),
            vmem((slots, points, width), bf16),
            vmem((slots * conduct, width), bf16),
            vmem((2, points, conduct), bf16),
            vmem((points, width), f32),
            vmem((2, 2, points, middle), f32),
            vmem((2, 2, points, part), bf16),
            vmem((2, 2, points, part), bf16),
            vmem((2, layers, 2, 2, rows, part), bf16),
            vmem((2, layers, 2, 2, rows, part), bf16),
            vmem((2, layers, 2, 2, 2, rows, part), f32),
            vmem((2, layers, 2, rows, part), f32),
            vmem((2, layers, 2, rows, part), bf16),
            vmem((2, layers, 2, rows, part), bf16),
            vmem((2, layers, 2, rows, part), bf16),
            vmem((2, 2, layers, rows, part), bf16),
            dma((5,)),
            dma((9,)),
            dma((tiles,)),
            dma((1,)),
            dma((2,)),
            dma((slots + 1,)),
            dma((slots, CUTS)),
            dma((2, 2)),
            dma((2, layers)),
            dma((2, layers)),
            dma((2, 2)),
        ],
        compiler_params=pltpu.CompilerParams(
            collective_id=0, has_side_effects=True, vmem_limit_bytes=58 * 1024 * 1024
        ),
    )(
        trial[0],
        psi_v.reshape(layers, 2, 2, 2, rows, points),
        psi_c[:, 0, :],
        screened,
    )
    out = pl.pallas_call(
        write_out,
        out_shape=jax.ShapeDtypeStruct((rows, conduct), f32),
        in_specs=[pl.BlockSpec(memory_space=vmem)],
        out_specs=far,
        scratch_shapes=[dma(())],
        compiler_params=pltpu.CompilerParams(vmem_limit_bytes=1024 * 1024),
    )(out)
    return out[None]


def solution(mesh):
    tiles = mesh.shape["tile"]

    def shards(trial, psi_v, psi_c, screened):
        fits = (
            trial.shape[0] == 1
            and mesh.shape["vec"] == 2
            and tiles % 8 == 0
            and psi_v.shape[1] % 128 == 0
            and psi_c.shape[2] % 128 == 0
            and trial.shape[1] % 16 == 0
            and trial.shape[2] % 512 == 0
        )
        if fits:
            return fused(tiles, trial, psi_v, psi_c, screened)
        return plain(trial, psi_v, psi_c, screened)

    in_specs = (
        P(None, ("tile", "vec"), None),
        P(None, "tile"),
        P(None, "vec", "tile"),
        P("tile", "vec"),
    )
    out_specs = P(None, ("tile", "vec"), None)
    return jax.shard_map(shards, mesh=mesh, in_specs=in_specs, out_specs=out_specs, check_vma=False)
```

```python
import functools

import jax
import jax.numpy as jnp
from jax import lax
from jax.experimental import pallas as pl
from jax.experimental.pallas import tpu as pltpu
from jax.sharding import PartitionSpec as P

CUTS = 4
AHEAD = 2
ROWS, ACROSS, LAYERS, SHARE, POINTS, GIVE, FIRST, SECOND, THIRD = range(9)


def back_product(weighted_flat, panel):
    return lax.dot_general(
        weighted_flat, panel, (((1,), (1,)), ((), ())), preferred_element_type=jnp.float32
    )


def plain(trial, psi_v, psi_c, screened):
    count = trial.shape[0]
    points = psi_v.shape[1]
    conduct = trial.shape[2]
    whole = lax.all_gather(trial, ("tile", "vec"), axis=1, tiled=True)
    projected = jnp.einsum("vp,kvc->kpc", psi_v, whole, preferred_element_type=jnp.float32).astype(
        jnp.bfloat16
    )
    flat = projected.reshape(count * points, conduct)
    panel_local = psi_c[:, 0, :]
    panel = lax.all_gather(panel_local, "tile", axis=1, tiled=True)
    pair = jnp.dot(flat, panel, preferred_element_type=jnp.float32)
    weighted = (screened[None] * pair.reshape(count, points, -1)).astype(jnp.bfloat16)
    weighted_flat = weighted.reshape(count * points, -1)
    back = back_product(weighted_flat, panel)
    back = back.reshape(count, points, conduct)
    left = psi_v.astype(jnp.float32)
    summed = lax.psum(back, "vec")
    tiles = lax.axis_size("tile")
    halves = lax.axis_size("vec")
    owned = left.shape[0] // (tiles * halves)
    grouped = left.reshape(tiles, halves, owned, points)
    mine = lax.dynamic_index_in_dim(grouped, lax.axis_index("vec"), 1, keepdims=False).reshape(
        tiles * owned, points
    )
    pieces = []
    for one in range(count):
        term = jnp.dot(mine, summed[one], precision=lax.Precision.HIGHEST)
        pieces.append(lax.psum_scatter(term, "tile", scatter_dimension=0, tiled=True))
    return jnp.stack(pieces, axis=0)


def sources_of(layers):
    return [
        sorted((o for o in range(layers) if o != z), key=lambda o: (abs(o - z), o))
        for z in range(layers)
    ]


def outer_first(layers):
    return sorted(range(layers), key=lambda k: (-abs(2 * k - layers + 1), k))


def pick(values, at):
    chosen = jnp.int32(values[0])
    for k, value in enumerate(values[1:], 1):
        chosen = jnp.where(at == k, jnp.int32(value), chosen)
    return chosen


def body(
    layers,
    trial_hbm,
    psi_v_hbm,
    psi_c_hbm,
    screened_hbm,
    result,
    whole,
    psi,
    psi_t,
    stage,
    screened_own,
    screened_out,
    screened_in,
    panel,
    flat,
    pair,
    back,
    give,
    take,
    first_send,
    first_got,
    keep,
    final_sum,
    second_send,
    second_got,
    third,
    parts,
    local_sem,
    sends,
    trial_recv,
    hand_recv,
    psi_recv,
    screened_recv,
    block_recv,
    take_recv,
    first_recv,
    second_recv,
    parts_recv,
):
    bf16, f32 = jnp.bfloat16, jnp.float32
    me = lax.axis_index("tile")
    half = lax.axis_index("vec")
    other = 1 - half
    z, y, x = me // 4, (me // 2) % 2, me % 2
    across = lax.rem(y + 1, 2)
    aside = lax.rem(x + 1, 2)
    table = sources_of(layers)
    events = layers - 1
    source = [pick([row[e] for row in table], z) for e in range(events)]
    distance = [pick([abs(row[e] - k) for k, row in enumerate(table)], z) for e in range(events)]
    at_distance = [[distance[e] == k for k in range(layers)] for e in range(events)]

    ranks = outer_first(layers)

    def place_of(zz):
        return pick([ranks.index(k) for k in range(layers)], zz)

    def tile_of(zz, yy, xx):
        return zz * 4 + yy * 2 + xx

    mate_x, mate_y = tile_of(z, y, aside), tile_of(z, across, x)
    up, down = jnp.minimum(z + 1, layers - 1), jnp.maximum(z - 1, 0)
    has_up, has_down = z < layers - 1, z > 0
    at_end = (z == 0) | (z == layers - 1)
    on_up = [has_up & (source[e] < z) for e in range(events)]
    on_down = [has_down & (source[e] > z) for e in range(events)]

    def slot_of(zz, yy):
        return zz * 2 + yy

    slots = layers * 2
    final = slots - 1
    order = [("own", 0)]
    for e in range(events - 1):
        order += [("z", e), ("y", e - 1)]
    order += [("y", events - 2), ("z", events - 1), ("y", events - 1)]

    def slot_at(kind, e):
        zz = source[e] if e >= 0 and kind != "own" else z
        return slot_of(zz, across if kind == "y" else y)

    turns = [slot_at(*event) for event in order]

    rows, conduct = trial_hbm.shape
    width = psi_c_hbm.shape[1]
    points = psi_v_hbm.shape[-1]
    middle = conduct // 2
    part = middle // 2
    height = psi_c_hbm.shape[0] // CUTS

    def lines(tile, vec):
        place = place_of(tile // 4)
        place = ((place // 2) * 2 + vec) * 2 + place % 2
        start = pl.multiple_of((place * 4 + tile % 4) * rows, rows)
        return whole.at[pl.ds(start, rows), :]

    def columns(tile):
        return pl.ds(pl.multiple_of(tile * width, 128), width)

    def load(src, dst, sem):
        copy = pltpu.make_async_copy(src, dst, local_sem.at[sem])
        copy.start()
        return copy

    home_slot, mate_slot = slot_of(z, y), slot_of(z, across)

    def block_of(slot):
        return panel.at[pl.ds(pl.multiple_of(slot * conduct, conduct), conduct), :]

    load_rows = load(trial_hbm, lines(me, half), 0)
    for i, layer in enumerate(ranks):
        for v in range(2):
            load(psi_v_hbm.at[layer, :, :, v], psi.at[0, i // 2 * 2 + v, i % 2], 1)
    load_block = load(psi_c_hbm, block_of(home_slot), 2)

    def low_or_high(r):
        return pl.ds(r * (points // 2), points // 2)

    def remote(src, dst, send, recv, tile, vec):
        return pltpu.make_async_remote_copy(
            src_ref=src,
            dst_ref=dst,
            send_sem=send,
            recv_sem=recv,
            device_id=(tile, vec),
            device_id_type=pl.DeviceIdType.MESH,
        )

    partners = [(mate_x, half, None), (mate_y, half, None), (me, other, None)]
    partners += [(tile_of(up, y, x), half, has_up), (tile_of(down, y, x), half, has_down)]
    with jax.named_scope("pbar"):
        barrier = pltpu.get_barrier_semaphore()

        def greet(tile, vec):
            pl.semaphore_signal(
                barrier, inc=1, device_id=(tile, vec), device_id_type=pl.DeviceIdType.MESH
            )

        for tile, vec, cond in partners:
            if cond is None:
                greet(tile, vec)
            else:
                pl.when(cond)(functools.partial(greet, tile, vec))
        for k in range(layers):
            count = 3 + (k > 0) + (k < layers - 1)
            pl.when(z == k)(functools.partial(pl.semaphore_wait, barrier, count))

    def send(src, dst, group, recv, tile, vec, cond=None):
        copy = remote(src, dst, sends.at[group], recv, tile, vec)
        if cond is None:
            copy.start()
        else:
            pl.when(cond)(copy.start)

    def sent(ref, group):
        remote(ref, ref, sends.at[group], psi_recv.at[0], me, other).wait_send()

    def got(ref, recv):
        remote(ref, ref, sends.at[0], recv, me, other).wait_recv()

    def piece(slot, s):
        start = pl.multiple_of(slot * conduct + s * height, height)
        return panel.at[pl.ds(start, height), :]

    def hand(tile):
        ref = lines(tile, half)
        send(ref, ref, ROWS, hand_recv.at[0], me, other)

    def spread(tile, to_up, to_down):
        ref = lines(tile, half)
        recv = trial_recv.at[tile]
        send(ref, ref, ROWS, recv, tile_of(up, y, x), half, to_up)
        send(ref, ref, ROWS, recv, tile_of(down, y, x), half, to_down)
        send(ref, ref, ROWS, recv, mate_y, half)
        hand(tile)

    last = CUTS - 1

    def along(slot, s, to_up, to_down):
        ref = piece(slot, s)
        recv = block_recv.at[slot, s]
        send(ref, ref, LAYERS, recv, tile_of(up, y, x), half, to_up)
        send(ref, ref, LAYERS, recv, tile_of(down, y, x), half, to_down)

    def cross(slot, s):
        ref = piece(slot, s)
        send(ref, ref, ACROSS, block_recv.at[slot, s], mate_y, half)

    def came(slot, s):
        got(piece(slot, s), block_recv.at[slot, s])

    pair_layers = layers // 2

    def psi_half(ref, which):
        return ref.at[pl.ds(which * pair_layers, pair_layers)]

    def take_piece(e, s):
        slot = slot_of(source[e], y)
        came(slot, s)
        along(slot, s, on_up[e], on_down[e])
        if s < last:
            cross(slot, s)

    def take_mate(e):
        slot = slot_of(source[e], across)
        came(slot, last)
        along(slot, last, on_up[e], on_down[e])

    def at_k(k):
        return [e for e in range(events) if any(abs(row[e] - r) == k for r, row in enumerate(table))]

    def arrive(k, first, final):
        for s in range(first, final):
            for e in at_k(k):
                pl.when(at_distance[e][k])(functools.partial(take_piece, e, s))
        if final == CUTS:
            for e in at_k(k):
                pl.when(at_distance[e][k])(functools.partial(take_mate, e))

    with jax.named_scope("ptrial"):
        ref = lines(me, half)
        load_rows.wait()
        send(ref, ref, ROWS, trial_recv.at[me], mate_x, half)
        spread(me, has_up, has_down)
        for i, turn in enumerate(turns):
            load(screened_hbm.at[:, columns(turn * 2 + aside)], stage.at[i], 3)
        for i, turn in enumerate(turns):
            load(screened_hbm.at[:, columns(turn * 2 + x)], screened_own.at[i], 4)
        pltpu.make_async_copy(psi.at[0], psi.at[0], local_sem.at[1]).wait()
        ref = psi_half(psi.at[0], half)
        send(ref, psi_half(psi.at[1], half), POINTS, psi_recv.at[0], mate_x, half)
        got(lines(mate_x, half), trial_recv.at[mate_x])
        spread(mate_x, has_up, has_down)
        load_block.wait()
        cross(home_slot, last)
        along(home_slot, 0, has_up, has_down)

        pltpu.make_async_copy(stage, stage, local_sem.at[3]).wait()
        for i in range(slots):
            screened_out[i] = stage[i].astype(bf16)
        for i in range(final):
            send(screened_out.at[i], screened_in.at[i], SHARE, screened_recv.at[i], mate_x, half)
        for r in range(2):
            src, dst = screened_out.at[final, low_or_high(r)], screened_in.at[final, low_or_high(r)]
            send(src, dst, SHARE, screened_recv.at[final + r], mate_x, half)

        for e in range(events):
            for xx in range(2):
                tile = tile_of(source[e], y, xx)
                got(lines(tile, half), trial_recv.at[tile])
                spread(tile, on_up[e], on_down[e])
            if e == events - 2:
                cross(home_slot, 0)
                for s in range(1, CUTS):
                    if s < CUTS // 2:
                        along(home_slot, s, has_up, has_down)
                    else:
                        along(home_slot, s, has_up & at_end, has_down & at_end)
        if events > 1:
            for s in range(CUTS // 2, CUTS):
                along(home_slot, s, has_up & ~at_end, has_down & ~at_end)
        else:
            for s in range(1, CUTS):
                along(home_slot, s, has_up, has_down)
        for s in range(1 if events > 1 else 0, last):
            cross(home_slot, s)

        back[...] = jnp.zeros_like(back)
        valence = layers * 4 * 2 * rows
        psi_t[0] = psi[0].reshape(valence, points).T

        came(mate_slot, last)
        along(mate_slot, last, has_up, has_down)
        arrive(1, 0, CUTS // 2)
        for e in range(-1, events):
            for xx in range(2):
                tile = tile_of(source[e] if e >= 0 else z, across, xx)
                got(lines(tile, half), trial_recv.at[tile])
                hand(tile)

        ref = psi_half(psi.at[1], half)
        got(ref, psi_recv.at[0])
        send(ref, ref, POINTS, psi_recv.at[1], me, other)
        arrive(1, CUTS // 2, CUTS)
        got(whole.at[pl.ds(0, layers * 4 * rows), :], hand_recv.at[0])

    wide = 256

    def project(p):
        def chunk(j, carry):
            cols = pl.ds(pl.multiple_of(j * wide, wide), wide)
            flat[p, :, cols] = jnp.dot(
                psi_t[p], whole[:, cols], preferred_element_type=f32
            ).astype(bf16)
            return carry

        lax.fori_loop(0, conduct // wide, chunk, 0)

    with jax.named_scope("pproj"):
        project(0)
        got(psi_half(psi.at[1], other), psi_recv.at[1])
        psi_t[1] = psi[1].reshape(valence, points).T
        project(1)

    turn_of = {e + 1: i for i, (kind, e) in enumerate(order) if kind == "z" and e > 0}

    def receive(i):
        kind, e = order[i]
        if kind == "z" and e > 0:
            arrive(e + 1, last, CUTS)
        if kind == "y":
            for s in range(last):
                came(turns[i], s)

    def between(i):
        for k, turn in turn_of.items():
            if i == turn - 2:
                arrive(k, 0, CUTS // 2)
            if i == turn - 1:
                arrive(k, CUTS // 2, last)

    def step(p, share, slot):
        block = block_of(slot)
        product = jnp.dot(flat[p], block[...], preferred_element_type=f32)
        weighted = (share.astype(f32) * product).astype(bf16)
        for h in range(2):
            back[p, h] += back_product(weighted, block[pl.ds(h * middle, middle), :])

    def last_step():
        block = block_of(turns[final])
        pair[...] = jnp.dot(flat[1], block[...], preferred_element_type=f32)
        for r in range(2):
            ref = screened_in.at[final, low_or_high(r)]
            got(ref, screened_recv.at[final + r])
            weighted = (ref[...].astype(f32) * pair[low_or_high(r)]).astype(bf16)
            for h in range(2):
                back[1, h, low_or_high(r)] += back_product(
                    weighted, block[pl.ds(h * middle, middle), :]
                )
                if r == 1:
                    pl.when(half != h)(functools.partial(swap, 1))

    pltpu.make_async_copy(screened_own, screened_own, local_sem.at[4]).wait()

    def use(k, carry):
        slot = turns[0]
        for i in range(final):
            slot = jnp.where(k == i, turns[i], slot)
            pl.when(k == i)(functools.partial(receive, i))
        step(0, screened_own[k], slot)
        for i in range(final):
            pl.when(k == i)(functools.partial(between, i))
        got(screened_in.at[k], screened_recv.at[k])
        step(1, screened_in[k], slot)
        return carry

    with jax.named_scope("puse"):
        lax.fori_loop(0, final, use, 0)
        receive(final)
        step(0, screened_own[final], turns[final])

    def span(kind):
        return pl.ds(kind * part, part)

    def swap(p):
        for kind in range(2):
            give[kind, p] = back[p, other, :, span(kind)].astype(bf16)
        for kind in range(2):
            send(give.at[kind, p], take.at[kind, p], GIVE, take_recv.at[kind, p], me, other)

    def split(kind, p):
        got(take.at[kind, p], take_recv.at[kind, p])
        total = back[p, half, :, span(kind)] + take[kind, p].astype(f32)
        high = total.astype(bf16)
        flat[p, :, span(kind)] = high
        low = (total - high.astype(f32)).astype(bf16)
        flat[p, :, pl.ds(middle + kind * part, part)] = low

    def product(p, kind, i):
        left = psi[p, i].reshape(8 * rows, points)
        total = None
        for level in range(2):
            cols = pl.ds(level * middle + kind * part, part)
            value = jnp.dot(left, flat[p, :, cols], preferred_element_type=f32)
            total = value if total is None else total + value
        return total.reshape(2, 2, 2, rows, part)

    def prepare(i, kind):
        if i < AHEAD:
            keep[kind, i] += product(1, kind, i)
        else:
            keep[kind, i] = product(0, kind, i) + product(1, kind, i)
        if kind == 0:
            away = keep[kind, i, :, :, pl.ds(aside, 1)]
        else:
            away = keep[kind, i, :, pl.ds(across, 1)]
        first_send[kind, i] = away.reshape(2, 2, rows, part).astype(bf16)

    def leave(i, kind):
        ref = first_send.at[kind, i]
        recv = first_recv.at[kind, i]
        send(ref, first_got.at[kind, i], FIRST, recv, [mate_x, mate_y][kind], half)

    def again(i, kind):
        got(first_got.at[kind, i], first_recv.at[kind, i])
        yy, xx = [(across, x), (y, aside)][kind]
        away, home = [(across, y), (aside, x)][kind]
        value = keep[kind, i, :, yy, xx] + first_got[kind, i, :, away].astype(f32)
        second_send[kind, i] = value.astype(bf16)
        final_sum[kind, i] = keep[kind, i, :, y, x] + first_got[kind, i, :, home].astype(f32)
        ref = second_send.at[kind, i]
        recv = second_recv.at[kind, i]
        send(ref, second_got.at[kind, i], SECOND, recv, [mate_y, mate_x][kind], half)

    def deliver(i, kind):
        got(second_got.at[kind, i], second_recv.at[kind, i])
        value = final_sum[kind, i] + second_got[kind, i].astype(f32)
        third[kind, i] = value.astype(bf16)
        final_sum[kind, i] = value
        for side in range(2):
            layer, v = ranks[i // 2 * 2 + side], i % 2
            send(
                third.at[kind, i, side],
                parts.at[half, kind, z],
                THIRD,
                parts_recv.at[half, kind],
                tile_of(layer, y, x),
                v,
                (z != layer) | (half != v),
            )

    def early():
        for kind in range(2):
            split(kind, 0)
        for i in range(AHEAD):
            for kind in range(2):
                keep[kind, i] = product(0, kind, i)

    with jax.named_scope("plast"):
        swap(0)
        pl.when(half == 0)(early)
        last_step()

    with jax.named_scope("pearly"):
        pl.when(half == 1)(early)

    with jax.named_scope("preduce"):
        for kind in range(2):
            split(kind, 1)
            prepare(0, kind)
            leave(0, kind)
        lead = layers - 1
        for i in range(1, layers):
            for kind in range(2):
                prepare(i, kind)
            if i < lead:
                for kind in range(2):
                    leave(i, kind)
        for i in range(layers):
            for kind in range(2):
                again(i, kind)
            if i == 0:
                for kind in range(2):
                    leave(lead, kind)
            if i > 0:
                for kind in range(2):
                    deliver(i - 1, kind)
        for kind in range(2):
            deliver(layers - 1, kind)

    with jax.named_scope("psum"):
        for flip in range(2):
            vec = lax.rem(half + flip, 2)
            for kind in range(2):
                value = None
                if flip == 0:
                    place = place_of(z)
                    value = final_sum[kind, (place // 2) * 2 + half, place % 2]
                count = layers - 1 + flip
                got(parts.at[vec, kind, pl.ds(0, count)], parts_recv.at[vec, kind])
                for d in range(1 - flip, layers):
                    more = parts[vec, kind, lax.rem(z + d, layers)].astype(f32)
                    value = more if value is None else value + more
                block = pl.ds(pl.multiple_of(vec * middle + kind * part, 128), part)
                result[:, block] = value

    def rows_as(count):
        return panel.at[pl.ds(0, count * conduct // width), :]

    def pieces_as(count):
        return panel.at[pl.ds(0, count * height), :]

    with jax.named_scope("pend"):
        sent(pieces_as(CUTS + events * last), ACROSS)
        for k in range(layers):
            ends = (k == 0) + (k == layers - 1)
            onward = sum((o < k < layers - 1) or (0 < k < o) for o in table[k])
            count = (2 - ends + onward) * (CUTS + 1)
            pl.when(z == k)(functools.partial(sent, pieces_as(count), LAYERS))
            count = 1 + 2 * (2 - ends + 2) + 2 * (2 * events + onward) + 2 * layers
            pl.when(z == k)(functools.partial(sent, rows_as(count * rows), ROWS))
        sent(screened_out, SHARE)
        sent(psi.at[1], POINTS)
        sent(give, GIVE)
        sent(first_send, FIRST)
        sent(second_send, SECOND)
        sent(rows_as(2 * (2 * layers - 1) * rows * part // conduct), THIRD)


def write_out(result, out_hbm, sem):
    copy = pltpu.make_async_copy(result, out_hbm, sem)
    copy.start()
    copy.wait()


def fused(tiles, trial, psi_v, psi_c, screened):
    rows, conduct = trial.shape[1:]
    valence, points = psi_v.shape
    width = psi_c.shape[2]
    middle = conduct // 2
    part = middle // 2
    layers = tiles // 4
    slots = layers * 2
    bf16, f32 = jnp.bfloat16, jnp.float32
    far = pl.BlockSpec(memory_space=pl.ANY)
    dma = pltpu.SemaphoreType.DMA
    vmem = pltpu.VMEM
    out = pl.pallas_call(
        functools.partial(body, layers),
        out_shape=vmem((rows, conduct), f32),
        in_specs=[far] * 4,
        out_specs=pl.BlockSpec(memory_space=vmem),
        scratch_shapes=[
            vmem((valence, conduct), bf16),
            vmem((2, layers, 2, 2, 2, rows, points), bf16),
            vmem((2, points, valence), bf16),
            vmem((slots, points, width), f32),
            vmem((slots, points, width), f32),
            vmem((slots, points, width), bf16),
            vmem((slots, points, width), bf16),
            vmem((slots * conduct, width), bf16),
            vmem((2, points, conduct), bf16),
            vmem((points, width), f32),
            vmem((2, 2, points, middle), f32),
            vmem((2, 2, points, part), bf16),
            vmem((2, 2, points, part), bf16),
            vmem((2, layers, 2, 2, rows, part), bf16),
            vmem((2, layers, 2, 2, rows, part), bf16),
            vmem((2, layers, 2, 2, 2, rows, part), f32),
            vmem((2, layers, 2, rows, part), f32),
            vmem((2, layers, 2, rows, part), bf16),
            vmem((2, layers, 2, rows, part), bf16),
            vmem((2, layers, 2, rows, part), bf16),
            vmem((2, 2, layers, rows, part), bf16),
            dma((5,)),
            dma((9,)),
            dma((tiles,)),
            dma((1,)),
            dma((2,)),
            dma((slots + 1,)),
            dma((slots, CUTS)),
            dma((2, 2)),
            dma((2, layers)),
            dma((2, layers)),
            dma((2, 2)),
        ],
        compiler_params=pltpu.CompilerParams(
            collective_id=0, has_side_effects=True, vmem_limit_bytes=58 * 1024 * 1024
        ),
    )(
        trial[0],
        psi_v.reshape(layers, 2, 2, 2, rows, points),
        psi_c[:, 0, :],
        screened,
    )
    out = pl.pallas_call(
        write_out,
        out_shape=jax.ShapeDtypeStruct((rows, conduct), f32),
        in_specs=[pl.BlockSpec(memory_space=vmem)],
        out_specs=far,
        scratch_shapes=[dma(())],
        compiler_params=pltpu.CompilerParams(vmem_limit_bytes=1024 * 1024),
    )(out)
    return out[None]


def solution(mesh):
    tiles = mesh.shape["tile"]

    def shards(trial, psi_v, psi_c, screened):
        fits = (
            trial.shape[0] == 1
            and mesh.shape["vec"] == 2
            and tiles % 8 == 0
            and psi_v.shape[1] % 128 == 0
            and psi_c.shape[2] % 128 == 0
            and trial.shape[1] % 16 == 0
            and trial.shape[2] % 512 == 0
        )
        if fits:
            return fused(tiles, trial, psi_v, psi_c, screened)
        return plain(trial, psi_v, psi_c, screened)

    in_specs = (
        P(None, ("tile", "vec"), None),
        P(None, "tile"),
        P(None, "vec", "tile"),
        P("tile", "vec"),
    )
    out_specs = P(None, ("tile", "vec"), None)
    return jax.shard_map(shards, mesh=mesh, in_specs=in_specs, out_specs=out_specs, check_vma=False)
```

```python
import functools

import jax
import jax.numpy as jnp
from jax import lax
from jax.experimental import pallas as pl
from jax.experimental.pallas import tpu as pltpu
from jax.sharding import PartitionSpec as P

CUTS = 4
AHEAD = 2
ROWS, ACROSS, LAYERS, SHARE, POINTS, GIVE, FIRST, SECOND, THIRD = range(9)


def back_product(weighted_flat, panel):
    return lax.dot_general(
        weighted_flat, panel, (((1,), (1,)), ((), ())), preferred_element_type=jnp.float32
    )


def plain(trial, psi_v, psi_c, screened):
    count = trial.shape[0]
    points = psi_v.shape[1]
    conduct = trial.shape[2]
    whole = lax.all_gather(trial, ("tile", "vec"), axis=1, tiled=True)
    projected = jnp.einsum("vp,kvc->kpc", psi_v, whole, preferred_element_type=jnp.float32).astype(
        jnp.bfloat16
    )
    flat = projected.reshape(count * points, conduct)
    panel_local = psi_c[:, 0, :]
    panel = lax.all_gather(panel_local, "tile", axis=1, tiled=True)
    pair = jnp.dot(flat, panel, preferred_element_type=jnp.float32)
    weighted = (screened[None] * pair.reshape(count, points, -1)).astype(jnp.bfloat16)
    weighted_flat = weighted.reshape(count * points, -1)
    back = back_product(weighted_flat, panel)
    back = back.reshape(count, points, conduct)
    left = psi_v.astype(jnp.float32)
    summed = lax.psum(back, "vec")
    tiles = lax.axis_size("tile")
    halves = lax.axis_size("vec")
    owned = left.shape[0] // (tiles * halves)
    grouped = left.reshape(tiles, halves, owned, points)
    mine = lax.dynamic_index_in_dim(grouped, lax.axis_index("vec"), 1, keepdims=False).reshape(
        tiles * owned, points
    )
    pieces = []
    for one in range(count):
        term = jnp.dot(mine, summed[one], precision=lax.Precision.HIGHEST)
        pieces.append(lax.psum_scatter(term, "tile", scatter_dimension=0, tiled=True))
    return jnp.stack(pieces, axis=0)


def sources_of(layers):
    return [
        sorted((o for o in range(layers) if o != z), key=lambda o: (abs(o - z), o))
        for z in range(layers)
    ]


def outer_first(layers):
    return sorted(range(layers), key=lambda k: (-abs(2 * k - layers + 1), k))


def pick(values, at):
    chosen = jnp.int32(values[0])
    for k, value in enumerate(values[1:], 1):
        chosen = jnp.where(at == k, jnp.int32(value), chosen)
    return chosen


def body(
    layers,
    trial_hbm,
    psi_v_hbm,
    psi_c_hbm,
    screened_hbm,
    result,
    whole,
    psi,
    psi_t,
    stage,
    screened_own,
    screened_out,
    screened_in,
    panel,
    flat,
    pair,
    back,
    give,
    take,
    first_send,
    first_got,
    keep,
    final_sum,
    second_send,
    second_got,
    third,
    parts,
    local_sem,
    sends,
    trial_recv,
    across_recv,
    hand_recv,
    psi_recv,
    screened_recv,
    block_recv,
    mate_recv,
    take_recv,
    first_recv,
    second_recv,
    parts_recv,
):
    bf16, f32 = jnp.bfloat16, jnp.float32
    me = lax.axis_index("tile")
    half = lax.axis_index("vec")
    other = 1 - half
    z, y, x = me // 4, (me // 2) % 2, me % 2
    across = lax.rem(y + 1, 2)
    aside = lax.rem(x + 1, 2)
    table = sources_of(layers)
    events = layers - 1
    source = [pick([row[e] for row in table], z) for e in range(events)]
    distance = [pick([abs(row[e] - k) for k, row in enumerate(table)], z) for e in range(events)]
    at_distance = [[distance[e] == k for k in range(layers)] for e in range(events)]

    ranks = outer_first(layers)

    def place_of(zz):
        return pick([ranks.index(k) for k in range(layers)], zz)

    def tile_of(zz, yy, xx):
        return zz * 4 + yy * 2 + xx

    mate_x, mate_y = tile_of(z, y, aside), tile_of(z, across, x)
    up, down = jnp.minimum(z + 1, layers - 1), jnp.maximum(z - 1, 0)
    has_up, has_down = z < layers - 1, z > 0
    at_end = (z == 0) | (z == layers - 1)
    on_up = [has_up & (source[e] < z) for e in range(events)]
    on_down = [has_down & (source[e] > z) for e in range(events)]

    def slot_of(zz, yy):
        return zz * 2 + yy

    slots = layers * 2
    final = slots - 1
    order = [("own", 0)]
    for e in range(events - 1):
        order += [("z", e), ("y", e - 1)]
    order += [("y", events - 2), ("z", events - 1), ("y", events - 1)]

    def slot_at(kind, e):
        zz = source[e] if e >= 0 and kind != "own" else z
        return slot_of(zz, across if kind == "y" else y)

    turns = [slot_at(*event) for event in order]

    rows, conduct = trial_hbm.shape
    width = psi_c_hbm.shape[1]
    points = psi_v_hbm.shape[-1]
    middle = conduct // 2
    part = middle // 2
    height = psi_c_hbm.shape[0] // CUTS

    def lines(tile, vec):
        place = place_of(tile // 4)
        place = ((place // 2) * 2 + vec) * 2 + place % 2
        start = pl.multiple_of((place * 4 + tile % 4) * rows, rows)
        return whole.at[pl.ds(start, rows), :]

    def columns(tile):
        return pl.ds(pl.multiple_of(tile * width, 128), width)

    def load(src, dst, sem):
        copy = pltpu.make_async_copy(src, dst, local_sem.at[sem])
        copy.start()
        return copy

    home_slot, mate_slot = slot_of(z, y), slot_of(z, across)

    def block_of(slot):
        return panel.at[pl.ds(pl.multiple_of(slot * conduct, conduct), conduct), :]

    load_rows = load(trial_hbm, lines(me, half), 0)
    for i, layer in enumerate(ranks):
        for v in range(2):
            load(psi_v_hbm.at[layer, :, :, v], psi.at[0, i // 2 * 2 + v, i % 2], 1)
    load_block = load(psi_c_hbm, block_of(home_slot), 2)

    def low_or_high(r):
        return pl.ds(r * (points // 2), points // 2)

    def remote(src, dst, send, recv, tile, vec):
        return pltpu.make_async_remote_copy(
            src_ref=src,
            dst_ref=dst,
            send_sem=send,
            recv_sem=recv,
            device_id=(tile, vec),
            device_id_type=pl.DeviceIdType.MESH,
        )

    partners = [(mate_x, half, None), (mate_y, half, None), (me, other, None)]
    partners += [(tile_of(up, y, x), half, has_up), (tile_of(down, y, x), half, has_down)]
    with jax.named_scope("pbar"):
        barrier = pltpu.get_barrier_semaphore()

        def greet(tile, vec):
            pl.semaphore_signal(
                barrier, inc=1, device_id=(tile, vec), device_id_type=pl.DeviceIdType.MESH
            )

        for tile, vec, cond in partners:
            if cond is None:
                greet(tile, vec)
            else:
                pl.when(cond)(functools.partial(greet, tile, vec))
        for k in range(layers):
            count = 3 + (k > 0) + (k < layers - 1)
            pl.when(z == k)(functools.partial(pl.semaphore_wait, barrier, count))

    def send(src, dst, group, recv, tile, vec, cond=None):
        copy = remote(src, dst, sends.at[group], recv, tile, vec)
        if cond is None:
            copy.start()
        else:
            pl.when(cond)(copy.start)

    def sent(ref, group):
        remote(ref, ref, sends.at[group], psi_recv.at[0], me, other).wait_send()

    def got(ref, recv):
        remote(ref, ref, sends.at[0], recv, me, other).wait_recv()

    def piece(slot, s):
        start = pl.multiple_of(slot * conduct + s * height, height)
        return panel.at[pl.ds(start, height), :]

    def hand(tile):
        ref = lines(tile, half)
        send(ref, ref, ROWS, hand_recv.at[0], me, other)

    def rows_sem(tile):
        return trial_recv.at[(tile // 4) * 2 + tile % 2]

    def spread(tile, to_up, to_down):
        ref = lines(tile, half)
        recv = rows_sem(tile)
        send(ref, ref, ROWS, recv, tile_of(up, y, x), half, to_up)
        send(ref, ref, ROWS, recv, tile_of(down, y, x), half, to_down)
        send(ref, ref, ROWS, across_recv.at[0], mate_y, half)
        hand(tile)

    last = CUTS - 1

    def along(slot, s, to_up, to_down, mate=False):
        ref = piece(slot, s)
        recv = mate_recv.at[slot // 2, 1] if mate else block_recv.at[slot // 2, s]
        send(ref, ref, LAYERS, recv, tile_of(up, y, x), half, to_up)
        send(ref, ref, LAYERS, recv, tile_of(down, y, x), half, to_down)

    def cross(slot, s):
        ref = piece(slot, s)
        send(ref, ref, ACROSS, mate_recv.at[slot // 2, s // last], mate_y, half)

    def came(slot, s):
        got(piece(slot, s), block_recv.at[slot // 2, s])

    def mate_came(slot):
        got(piece(slot, last), mate_recv.at[slot // 2, 1])

    pair_layers = layers // 2

    def psi_half(ref, which):
        return ref.at[pl.ds(which * pair_layers, pair_layers)]

    def take_piece(e, s):
        slot = slot_of(source[e], y)
        came(slot, s)
        along(slot, s, on_up[e], on_down[e])
        if s < last:
            cross(slot, s)

    def take_mate(e):
        slot = slot_of(source[e], across)
        mate_came(slot)
        along(slot, last, on_up[e], on_down[e], True)

    def at_k(k):
        return [e for e in range(events) if any(abs(row[e] - r) == k for r, row in enumerate(table))]

    def arrive(k, first, final):
        for s in range(first, final):
            for e in at_k(k):
                pl.when(at_distance[e][k])(functools.partial(take_piece, e, s))
        if final == CUTS:
            for e in at_k(k):
                pl.when(at_distance[e][k])(functools.partial(take_mate, e))

    with jax.named_scope("ptrial"):
        ref = lines(me, half)
        load_rows.wait()
        send(ref, ref, ROWS, rows_sem(me), mate_x, half)
        spread(me, has_up, has_down)
        for i, turn in enumerate(turns):
            load(screened_hbm.at[:, columns(turn * 2 + aside)], stage.at[i], 3)
        for i, turn in enumerate(turns):
            load(screened_hbm.at[:, columns(turn * 2 + x)], screened_own.at[i], 4)
        pltpu.make_async_copy(psi.at[0], psi.at[0], local_sem.at[1]).wait()
        ref = psi_half(psi.at[0], half)
        send(ref, psi_half(psi.at[1], half), POINTS, psi_recv.at[0], mate_x, half)
        got(lines(mate_x, half), rows_sem(mate_x))
        spread(mate_x, has_up, has_down)
        load_block.wait()
        cross(home_slot, last)
        along(home_slot, 0, has_up, has_down)

        pltpu.make_async_copy(stage, stage, local_sem.at[3]).wait()
        for i in range(slots):
            screened_out[i] = stage[i].astype(bf16)
        for i in range(final):
            send(screened_out.at[i], screened_in.at[i], SHARE, screened_recv.at[i], mate_x, half)
        for r in range(2):
            src, dst = screened_out.at[final, low_or_high(r)], screened_in.at[final, low_or_high(r)]
            send(src, dst, SHARE, screened_recv.at[final + r], mate_x, half)

        for e in range(events):
            for xx in range(2):
                tile = tile_of(source[e], y, xx)
                got(lines(tile, half), rows_sem(tile))
                spread(tile, on_up[e], on_down[e])
            if e == events - 2:
                cross(home_slot, 0)
                for s in range(1, CUTS):
                    if s < CUTS // 2:
                        along(home_slot, s, has_up, has_down)
                    else:
                        along(home_slot, s, has_up & at_end, has_down & at_end)
        if events > 1:
            for s in range(CUTS // 2, CUTS):
                along(home_slot, s, has_up & ~at_end, has_down & ~at_end)
        else:
            for s in range(1, CUTS):
                along(home_slot, s, has_up, has_down)
        for s in range(1 if events > 1 else 0, last):
            cross(home_slot, s)

        back[...] = jnp.zeros_like(back)
        valence = layers * 4 * 2 * rows
        psi_t[0] = psi[0].reshape(valence, points).T

        mate_came(mate_slot)
        along(mate_slot, last, has_up, has_down, True)
        arrive(1, 0, CUTS // 2)
        got(whole.at[pl.ds(0, layers * 2 * rows), :], across_recv.at[0])
        for e in range(-1, events):
            for xx in range(2):
                hand(tile_of(source[e] if e >= 0 else z, across, xx))

        ref = psi_half(psi.at[1], half)
        got(ref, psi_recv.at[0])
        send(ref, ref, POINTS, psi_recv.at[1], me, other)
        arrive(1, CUTS // 2, CUTS)
        got(whole.at[pl.ds(0, layers * 4 * rows), :], hand_recv.at[0])

    wide = 256

    def project(p):
        def chunk(j, carry):
            cols = pl.ds(pl.multiple_of(j * wide, wide), wide)
            flat[p, :, cols] = jnp.dot(
                psi_t[p], whole[:, cols], preferred_element_type=f32
            ).astype(bf16)
            return carry

        lax.fori_loop(0, conduct // wide, chunk, 0)

    with jax.named_scope("pproj"):
        project(0)
        got(psi_half(psi.at[1], other), psi_recv.at[1])
        psi_t[1] = psi[1].reshape(valence, points).T
        project(1)

    turn_of = {e + 1: i for i, (kind, e) in enumerate(order) if kind == "z" and e > 0}

    def receive(i):
        kind, e = order[i]
        if kind == "z" and e > 0:
            arrive(e + 1, last, CUTS)
        if kind == "y":
            start = pl.multiple_of(turns[i] * conduct, conduct)
            got(panel.at[pl.ds(start, last * height), :], mate_recv.at[turns[i] // 2, 0])

    def between(i):
        for k, turn in turn_of.items():
            if i == turn - 2:
                arrive(k, 0, CUTS // 2)
            if i == turn - 1:
                arrive(k, CUTS // 2, last)

    def step(p, share, slot):
        block = block_of(slot)
        product = jnp.dot(flat[p], block[...], preferred_element_type=f32)
        weighted = (share.astype(f32) * product).astype(bf16)
        for h in range(2):
            back[p, h] += back_product(weighted, block[pl.ds(h * middle, middle), :])

    def last_step():
        block = block_of(turns[final])
        pair[...] = jnp.dot(flat[1], block[...], preferred_element_type=f32)
        for r in range(2):
            ref = screened_in.at[final, low_or_high(r)]
            got(ref, screened_recv.at[final + r])
            weighted = (ref[...].astype(f32) * pair[low_or_high(r)]).astype(bf16)
            for h in range(2):
                back[1, h, low_or_high(r)] += back_product(
                    weighted, block[pl.ds(h * middle, middle), :]
                )
                if r == 1:
                    pl.when(half != h)(functools.partial(swap, 1))

    pltpu.make_async_copy(screened_own, screened_own, local_sem.at[4]).wait()

    def use(k, carry):
        slot = turns[0]
        for i in range(final):
            slot = jnp.where(k == i, turns[i], slot)
            pl.when(k == i)(functools.partial(receive, i))
        step(0, screened_own[k], slot)
        for i in range(final):
            pl.when(k == i)(functools.partial(between, i))
        got(screened_in.at[k], screened_recv.at[k])
        step(1, screened_in[k], slot)
        return carry

    with jax.named_scope("puse"):
        lax.fori_loop(0, final, use, 0)
        receive(final)
        step(0, screened_own[final], turns[final])

    def span(kind):
        return pl.ds(kind * part, part)

    def swap(p):
        for kind in range(2):
            give[kind, p] = back[p, other, :, span(kind)].astype(bf16)
            send(give.at[kind, p], take.at[kind, p], GIVE, take_recv.at[kind, p], me, other)

    def split(kind, p):
        got(take.at[kind, p], take_recv.at[kind, p])
        total = back[p, half, :, span(kind)] + take[kind, p].astype(f32)
        high = total.astype(bf16)
        flat[p, :, span(kind)] = high
        low = (total - high.astype(f32)).astype(bf16)
        flat[p, :, pl.ds(middle + kind * part, part)] = low

    def product(p, kind, i):
        left = psi[p, i].reshape(8 * rows, points)
        total = None
        for level in range(2):
            cols = pl.ds(level * middle + kind * part, part)
            value = jnp.dot(left, flat[p, :, cols], preferred_element_type=f32)
            total = value if total is None else total + value
        return total.reshape(2, 2, 2, rows, part)

    def prepare(i, kind):
        if i < AHEAD:
            keep[kind, i] += product(1, kind, i)
        else:
            keep[kind, i] = product(0, kind, i) + product(1, kind, i)
        if kind == 0:
            away = keep[kind, i, :, :, pl.ds(aside, 1)]
        else:
            away = keep[kind, i, :, pl.ds(across, 1)]
        first_send[kind, i] = away.reshape(2, 2, rows, part).astype(bf16)

    def leave(i, kind):
        ref = first_send.at[kind, i]
        recv = first_recv.at[kind, i]
        send(ref, first_got.at[kind, i], FIRST, recv, [mate_x, mate_y][kind], half)

    def again(i, kind):
        got(first_got.at[kind, i], first_recv.at[kind, i])
        yy, xx = [(across, x), (y, aside)][kind]
        away, home = [(across, y), (aside, x)][kind]
        value = keep[kind, i, :, yy, xx] + first_got[kind, i, :, away].astype(f32)
        second_send[kind, i] = value.astype(bf16)
        ref = second_send.at[kind, i]
        recv = second_recv.at[kind, i]
        send(ref, second_got.at[kind, i], SECOND, recv, [mate_y, mate_x][kind], half)
        final_sum[kind, i] = keep[kind, i, :, y, x] + first_got[kind, i, :, home].astype(f32)

    def deliver(i, kind):
        got(second_got.at[kind, i], second_recv.at[kind, i])
        value = final_sum[kind, i] + second_got[kind, i].astype(f32)
        final_sum[kind, i] = value
        third[kind, i] = value.astype(bf16)
        for side in range(2):
            layer, v = ranks[i // 2 * 2 + side], i % 2
            send(
                third.at[kind, i, side],
                parts.at[half, kind, z],
                THIRD,
                parts_recv.at[half, kind],
                tile_of(layer, y, x),
                v,
                (z != layer) | (half != v),
            )

    def early():
        for kind in range(2):
            split(kind, 0)
        for i in range(AHEAD):
            for kind in range(2):
                keep[kind, i] = product(0, kind, i)

    with jax.named_scope("plast"):
        swap(0)
        pl.when(half == 0)(early)
        last_step()

    with jax.named_scope("pearly"):
        pl.when(half == 1)(early)

    with jax.named_scope("preduce"):
        for kind in range(2):
            split(kind, 1)
            prepare(0, kind)
            leave(0, kind)
        lead = layers - 1
        for i in range(1, layers):
            for kind in range(2):
                prepare(i, kind)
            if i < lead:
                for kind in range(2):
                    leave(i, kind)
        for i in range(layers):
            for kind in range(2):
                again(i, kind)
            if i == 0:
                for kind in range(2):
                    leave(lead, kind)
            if i > 0:
                for kind in range(2):
                    deliver(i - 1, kind)
        for kind in range(2):
            deliver(layers - 1, kind)

    with jax.named_scope("psum"):
        for flip in range(2):
            vec = lax.rem(half + flip, 2)
            for kind in range(2):
                value = None
                if flip == 0:
                    place = place_of(z)
                    value = final_sum[kind, (place // 2) * 2 + half, place % 2]
                count = layers - 1 + flip
                got(parts.at[vec, kind, pl.ds(0, count)], parts_recv.at[vec, kind])
                for d in range(1 - flip, layers):
                    more = parts[vec, kind, lax.rem(z + d, layers)].astype(f32)
                    value = more if value is None else value + more
                block = pl.ds(pl.multiple_of(vec * middle + kind * part, 128), part)
                result[:, block] = value

    def rows_as(count):
        return panel.at[pl.ds(0, count * conduct // width), :]

    def pieces_as(count):
        return panel.at[pl.ds(0, count * height), :]

    with jax.named_scope("pend"):
        sent(pieces_as(CUTS + events * last), ACROSS)
        for k in range(layers):
            ends = (k == 0) + (k == layers - 1)
            onward = sum((o < k < layers - 1) or (0 < k < o) for o in table[k])
            count = (2 - ends + onward) * (CUTS + 1)
            pl.when(z == k)(functools.partial(sent, pieces_as(count), LAYERS))
            count = 1 + 2 * (2 - ends + 2) + 2 * (2 * events + onward) + 2 * layers
            pl.when(z == k)(functools.partial(sent, rows_as(count * rows), ROWS))
        sent(screened_out, SHARE)
        sent(psi.at[1], POINTS)
        sent(give, GIVE)
        sent(first_send, FIRST)
        sent(second_send, SECOND)
        sent(rows_as(2 * (2 * layers - 1) * rows * part // conduct), THIRD)


def write_out(result, out_hbm, sem):
    part = result.shape[1] // 4
    for i in range(4):
        lot = pl.ds(i * part, part)
        pltpu.make_async_copy(result.at[:, lot], out_hbm.at[:, lot], sem).start()
    pltpu.make_async_copy(result, out_hbm, sem).wait()


def fused(tiles, trial, psi_v, psi_c, screened):
    rows, conduct = trial.shape[1:]
    valence, points = psi_v.shape
    width = psi_c.shape[2]
    middle = conduct // 2
    part = middle // 2
    layers = tiles // 4
    slots = layers * 2
    bf16, f32 = jnp.bfloat16, jnp.float32
    far = pl.BlockSpec(memory_space=pl.ANY)
    dma = pltpu.SemaphoreType.DMA
    vmem = pltpu.VMEM
    out = pl.pallas_call(
        functools.partial(body, layers),
        out_shape=vmem((rows, conduct), f32),
        in_specs=[far] * 4,
        out_specs=pl.BlockSpec(memory_space=vmem),
        scratch_shapes=[
            vmem((valence, conduct), bf16),
            vmem((2, layers, 2, 2, 2, rows, points), bf16),
            vmem((2, points, valence), bf16),
            vmem((slots, points, width), f32),
            vmem((slots, points, width), f32),
            vmem((slots, points, width), bf16),
            vmem((slots, points, width), bf16),
            vmem((slots * conduct, width), bf16),
            vmem((2, points, conduct), bf16),
            vmem((points, width), f32),
            vmem((2, 2, points, middle), f32),
            vmem((2, 2, points, part), bf16),
            vmem((2, 2, points, part), bf16),
            vmem((2, layers, 2, 2, rows, part), bf16),
            vmem((2, layers, 2, 2, rows, part), bf16),
            vmem((2, layers, 2, 2, 2, rows, part), f32),
            vmem((2, layers, 2, rows, part), f32),
            vmem((2, layers, 2, rows, part), bf16),
            vmem((2, layers, 2, rows, part), bf16),
            vmem((2, layers, 2, rows, part), bf16),
            vmem((2, 2, layers, rows, part), bf16),
            dma((5,)),
            dma((9,)),
            dma((slots,)),
            dma((1,)),
            dma((1,)),
            dma((2,)),
            dma((slots + 1,)),
            dma((layers, CUTS)),
            dma((layers, 2)),
            dma((2, 2)),
            dma((2, layers)),
            dma((2, layers)),
            dma((2, 2)),
        ],
        compiler_params=pltpu.CompilerParams(
            collective_id=0, has_side_effects=True, vmem_limit_bytes=58 * 1024 * 1024
        ),
    )(
        trial[0],
        psi_v.reshape(layers, 2, 2, 2, rows, points),
        psi_c[:, 0, :],
        screened,
    )
    out = pl.pallas_call(
        write_out,
        out_shape=jax.ShapeDtypeStruct((rows, conduct), f32),
        in_specs=[pl.BlockSpec(memory_space=vmem)],
        out_specs=far,
        scratch_shapes=[dma(())],
        compiler_params=pltpu.CompilerParams(vmem_limit_bytes=1024 * 1024),
    )(out)
    return out[None]


def solution(mesh):
    tiles = mesh.shape["tile"]

    def shards(trial, psi_v, psi_c, screened):
        fits = (
            trial.shape[0] == 1
            and mesh.shape["vec"] == 2
            and tiles % 8 == 0
            and psi_v.shape[1] % 128 == 0
            and psi_c.shape[2] % 128 == 0
            and trial.shape[1] % 16 == 0
            and trial.shape[2] % 512 == 0
        )
        if fits:
            return fused(tiles, trial, psi_v, psi_c, screened)
        return plain(trial, psi_v, psi_c, screened)

    in_specs = (
        P(None, ("tile", "vec"), None),
        P(None, "tile"),
        P(None, "vec", "tile"),
        P("tile", "vec"),
    )
    out_specs = P(None, ("tile", "vec"), None)
    return jax.shard_map(shards, mesh=mesh, in_specs=in_specs, out_specs=out_specs, check_vma=False)
```
